32 devices in a mesh: ctx: 4 (over x, core), wsh: 8 (over z, y).
Axes of the slice: x: 2, y: 2, z: 4, core: 2. Of those that a mesh axis runs over, the one named last changes fastest.
Arguments:
- inputs: bfloat16 [8, 1024, 1024], P('wsh', 'ctx'), may hold values from -6 to 6
- enc_states: bfloat16 [8, 512, 1024], P('wsh', 'ctx'), may hold values from -6 to 6
- cotangent: bfloat16 [8, 1024, 1024], P('wsh', 'ctx'), may hold values from -6 to 6
- slot_order: int32 [8, 1024], P('wsh'), may hold values from 0 to 1023, each once within a row
- seq_lengths: int32 [8, 8], P('wsh'), may hold values from 1 to 512, 1024 in all within a row
- enc_lengths: int32 [8, 8], P('wsh'), may hold values from 1 to 256, 512 in all within a row
- self_query: bfloat16 [1024, 1024], P('wsh'), may hold values from -0.1875 to 0.1875
- self_key: bfloat16 [1024, 1024], P('wsh'), may hold values from -0.1875 to 0.1875
- self_value: bfloat16 [1024, 1024], P('wsh'), may hold values from -0.1875 to 0.1875
- self_out: bfloat16 [1024, 1024], P('wsh'), may hold values from -1 to 1
- cross_query: bfloat16 [1024, 1024], P('wsh'), may hold values from -0.1875 to 0.1875
- cross_key: bfloat16 [1024, 1024], P('wsh'), may hold values from -0.1875 to 0.1875
- cross_value: bfloat16 [1024, 1024], P('wsh'), may hold values from -0.1875 to 0.1875
- cross_out: bfloat16 [1024, 1024], P('wsh'), may hold values from -1 to 1
- feed_in: bfloat16 [1024, 4096], P('wsh'), may hold values from -0.1875 to 0.1875
- feed_out: bfloat16 [4096, 1024], P('wsh'), may hold values from -0.09375 to 0.09375
- norm_gains: bfloat16 [1024, 4], P('wsh'), may hold values from 0.5 to 1.5
- norm_shifts: bfloat16 [1024, 4], P('wsh'), may hold values from -1 to 1
Outputs:
- output: float32 [8, 1024, 1024], P('wsh', 'ctx')
- input_grad: float32 [8, 1024, 1024], P('wsh', 'ctx')
- enc_grad: float32 [8, 512, 1024], P('wsh', 'ctx')
- self_query_grad: float32 [1024, 1024], P('wsh')
- self_key_grad: float32 [1024, 1024], P('wsh')
- self_value_grad: float32 [1024, 1024], P('wsh')
- self_out_grad: float32 [1024, 1024], P('wsh')
- cross_query_grad: float32 [1024, 1024], P('wsh')
- cross_key_grad: float32 [1024, 1024], P('wsh')
- cross_value_grad: float32 [1024, 1024], P('wsh')
- cross_out_grad: float32 [1024, 1024], P('wsh')
- feed_in_grad: float32 [1024, 4096], P('wsh')
- feed_out_grad: float32 [4096, 1024], P('wsh')
- gain_grad: float32 [1024, 4], P('wsh')
- shift_grad: float32 [1024, 4], P('wsh')
The draws below stay inside these ranges and needn't reach their ends.
Inputs may be any that keep to these rules, and one draw needn't show every extreme that they name: Each row of slot_order is a permutation of 0 to 1023. `seq_lengths`: each row sums to 1024. `enc_lengths`: each row sums to 512.
All inputs are finite; a program needn't handle non-finite values.
Results may differ from the reference program's by a relative error of at most 0.023.
Values may be sent and summed in bfloat16 or wider, within the bound.
No kernel may reach another device: no remote copies, remote signals or barrier semaphores. Data moves between devices by JAX's collectives and lax.ppermute only.
A program may use at most 256 MiB of HBM per device.

```python
import math
import jax
import jax.numpy as jnp
import numpy as np
from jax import lax

D = 1024
FF = 4096
HEAD_DIM = 64
NSEQ = 8
GROUPS = 8
GROUP_TOK = 1024
ENC_GROUP = 512
MAXLEN = 512
ENC_MAX = 256


def levels(rng, shape, shards, least, high):
    gain, own = 1.0, jax.random.fold_in(rng, 6)
    for dim, parts in shards:
        steps = jnp.exp(jax.random.uniform(jax.random.fold_in(own, dim), (parts,), jnp.float32, least / len(shards), high / len(shards)))
        gain = gain * jnp.repeat(steps, shape[dim] // parts).reshape([-1 if axis == dim else 1 for axis in range(len(shape))])
    return gain


def length_profile(amount, total, limit, lean):
    loads = [(1 << 20) // math.isqrt(rank ** lean) + 1 for rank in range(2, amount + 1)]
    surplus, holding = total - limit - (amount - 1), [1] * (amount - 1)
    while surplus > 0:
        free = [i for i in range(amount - 1) if holding[i] < limit]
        mass, budget = sum([loads[i] for i in free]), surplus
        for i in free:
            more = min(limit - holding[i], max(1, budget * loads[i] // mass), surplus)
            holding[i] = holding[i] + more
            surplus = surplus - more
    return np.array([limit] + holding)


def ragged(rng, amount, total, bound, skew):
    if amount == 2:
        one = jax.random.randint(rng, (), max(1, total - bound), min(bound, total - 1) + 1)
        return jnp.stack([one, total - one])
    lengths = jnp.asarray(length_profile(amount, total, bound, skew), jnp.int32)
    pairs = (amount - 1) // 2
    giver, sink = lengths[1:1 + 2 * pairs:2], lengths[2:2 + 2 * pairs:2]
    room = jnp.minimum(giver - 1, bound - sink)
    passed = jax.random.randint(jax.random.fold_in(rng, 1), (pairs,), 0, 1 << 20) % (room + 1)
    lengths = lengths.at[1:1 + 2 * pairs:2].set(giver - passed).at[2:2 + 2 * pairs:2].set(sink + passed)
    return lengths[jax.random.permutation(jax.random.fold_in(rng, 2), amount)]


def noise(own_key, shape, width, bound, cuts=(), kind=jnp.bfloat16):
    gain = levels(own_key, shape, cuts, -0.22, 0.18) if cuts else 1.0
    entries = jax.random.normal(own_key, shape, jnp.float32) * width * gain
    return jnp.minimum(jnp.maximum(entries, -bound), bound).astype(kind)


def setup_inputs(seed: int = 0) -> dict:
    seeds = jax.random.split(jax.random.key(seed), 19)
    return {
        "inputs": noise(seeds[0], (GROUPS, GROUP_TOK, D), 1.0, 6.0, ((0, 8), (1, 4))),
        "enc_states": noise(seeds[1], (GROUPS, ENC_GROUP, D), 1.0, 6.0, ((0, 8), (1, 4))),
        "cotangent": noise(seeds[2], (GROUPS, GROUP_TOK, D), 1.0, 6.0, ((0, 8), (1, 4))),
        "slot_order": jax.vmap(lambda own: jax.random.permutation(own, GROUP_TOK))(jax.random.split(seeds[3], GROUPS)).reshape((GROUPS, GROUP_TOK)).astype(jnp.int32),
        "seq_lengths": jax.vmap(lambda own: ragged(own, NSEQ, GROUP_TOK, MAXLEN, 2))(jax.random.split(seeds[4], GROUPS)).reshape((GROUPS, NSEQ)).astype(jnp.int32),
        "enc_lengths": jax.vmap(lambda own: ragged(own, NSEQ, ENC_GROUP, ENC_MAX, 2))(jax.random.split(seeds[5], GROUPS)).reshape((GROUPS, NSEQ)).astype(jnp.int32),
        "self_query": noise(seeds[6], (D, D), D ** -0.5, 0.1875, ((0, 8),)),
        "self_key": noise(seeds[7], (D, D), D ** -0.5, 0.1875, ((0, 8),)),
        "self_value": noise(seeds[8], (D, D), D ** -0.5, 0.1875, ((0, 8),)),
        "self_out": noise(seeds[9], (D, D), (max(D * 16 // MAXLEN, 1)) ** -0.5, 1.0, ((0, 8),)),
        "cross_query": noise(seeds[10], (D, D), D ** -0.5, 0.1875, ((0, 8),)),
        "cross_key": noise(seeds[11], (D, D), D ** -0.5, 0.1875, ((0, 8),)),
        "cross_value": noise(seeds[12], (D, D), D ** -0.5, 0.1875, ((0, 8),)),
        "cross_out": noise(seeds[13], (D, D), (max(D * 8 // ENC_MAX, 1)) ** -0.5, 1.0, ((0, 8),)),
        "feed_in": noise(seeds[14], (D, FF), D ** -0.5, 0.1875, ((0, 8),)),
        "feed_out": noise(seeds[15], (FF, D), FF ** -0.5, 0.09375, ((0, 8),)),
        "norm_gains": jnp.clip(1.0 + 0.1 * jax.random.normal(seeds[16], (D, 4), jnp.float32), 0.5, 1.5).astype(jnp.bfloat16),
        "norm_shifts": noise(seeds[17], (D, 4), 0.2, 1.0, ((0, 8),)),
    }


@jax.custom_vjp
def low(v):
    return lax.optimization_barrier(v.astype(jnp.bfloat16)).astype(jnp.float32)

@jax.custom_vjp
def low_back(v):
    return v

def low_keep(v):
    return (low(v), None)

def low_pass(kept, grad):
    return (grad,)

def back_keep(v):
    return (v, None)

def back_low(kept, grad):
    return (low(grad),)
low.defvjp(low_keep, low_pass)
low_back.defvjp(back_keep, back_low)

def product(left, right):
    return jnp.dot(left, right, precision=lax.Precision.HIGHEST, preferred_element_type=jnp.float32)

def layer_norm(values, scale_row, shift_row):
    center = values - lax.optimization_barrier(jnp.mean(values, axis=-1, keepdims=True))
    spread = lax.optimization_barrier(jnp.mean(center * center, axis=-1, keepdims=True))
    return center * lax.rsqrt(spread + 1e-05) * scale_row + shift_row

def count_below(places, ends):
    hits = (places[:, None] >= ends[None, :]).astype(jnp.int32)
    return lax.optimization_barrier(jnp.sum(hits, axis=1, dtype=jnp.int32)).astype(jnp.int32)

def attention(queries, keys, values, query_seg, query_place, key_seg, key_place, causal):
    total_rows = queries.shape[0]
    block_rows = min(512, total_rows)
    head_count = queries.shape[1] // HEAD_DIM
    key_heads = keys.reshape(keys.shape[0], head_count, HEAD_DIM)
    value_heads = values.reshape(values.shape[0], head_count, HEAD_DIM)
    block_seg = query_seg.astype(jnp.int32).reshape(-1, block_rows)
    block_place = query_place.astype(jnp.int32).reshape(-1, block_rows)
    key_seg = key_seg.astype(jnp.int32)
    key_place = key_place.astype(jnp.int32)

    def one_block(query_block, seg_block, place_block):
        scores = jnp.einsum('qhd,khd->hqk', query_block.reshape(block_rows, head_count, HEAD_DIM), key_heads, precision=lax.Precision.HIGHEST)
        scores = scores * jnp.asarray(0.125, scores.dtype)
        allowed = seg_block[:, None] == key_seg[None, :]
        if causal:
            allowed = allowed & (key_place[None, :] <= place_block[:, None])
        masked = jnp.where(allowed[None], scores, jnp.asarray(-1e+30, scores.dtype))
        masked = low_back(masked)
        probabilities = jax.nn.softmax(masked, axis=-1)
        mixed_heads = jnp.einsum('hqk,khd->qhd', low(probabilities), value_heads, precision=lax.Precision.HIGHEST)
        return mixed_heads.reshape(block_rows, -1)
    checked = jax.checkpoint(one_block)
    block_outs = lax.map(lambda pieces: checked(pieces[0], pieces[1], pieces[2]), (queries.reshape(total_rows // block_rows, block_rows, -1), block_seg, block_place))
    return block_outs.reshape(total_rows, -1)

def decoder_layer(tokens, encoder, self_query, self_key, self_value, self_out, cross_query, cross_key, cross_value, cross_out, feed_in, feed_out, gains, shifts, segment, slot_place, enc_segment):
    normed_one = low(layer_norm(tokens, gains[:, 0], shifts[:, 0]))
    queries = low_back(low(product(normed_one, self_query)))
    keys = low_back(low(product(normed_one, self_key)))
    values = low_back(low(product(normed_one, self_value)))
    attended = low_back(low(attention(queries, keys, values, segment, slot_place, segment, slot_place, True)))
    after_self = tokens + low_back(product(attended, self_out))
    normed_two = low(layer_norm(after_self, gains[:, 1], shifts[:, 1]))
    queries_two = low_back(low(product(normed_two, cross_query)))
    keys_two = low_back(low(product(encoder, cross_key)))
    values_two = low_back(low(product(encoder, cross_value)))
    attended_two = low_back(low(attention(queries_two, keys_two, values_two, segment, slot_place, enc_segment, enc_segment, False)))
    after_cross = after_self + low_back(product(attended_two, cross_out))
    normed_three = low(layer_norm(after_cross, gains[:, 2], shifts[:, 2]))
    hidden = low(jax.nn.gelu(low_back(product(normed_three, feed_in)), approximate=True))
    after_ffn = after_cross + low_back(product(hidden, feed_out))
    return layer_norm(after_ffn, gains[:, 3], shifts[:, 3])

def reference(inputs, enc_states, cotangent, slot_order, seq_lengths, enc_lengths, self_query, self_key, self_value, self_out, cross_query, cross_key, cross_value, cross_out, feed_in, feed_out, norm_gains, norm_shifts):
    params = (self_query, self_key, self_value, self_out, cross_query, cross_key, cross_value, cross_out, feed_in, feed_out, norm_gains, norm_shifts)
    floats = tuple((param.astype(jnp.float32) for param in params))

    def one_group(totals, pieces):
        tokens, encoder, grad_out, slot_place, lengths_row, enc_row = pieces
        slot_place = slot_place.astype(jnp.int32)
        seq_ends = jnp.cumsum(lengths_row.astype(jnp.int32), dtype=jnp.int32).astype(jnp.int32)
        segment = count_below(slot_place, seq_ends)
        enc_place = jnp.arange(ENC_GROUP, dtype=jnp.int32)
        enc_ends = jnp.cumsum(enc_row.astype(jnp.int32), dtype=jnp.int32).astype(jnp.int32)
        enc_segment = count_below(enc_place, enc_ends)

        def forward(token_values, enc_values, *weights):
            return decoder_layer(token_values, enc_values, *weights, segment, slot_place, enc_segment)
        result, pullback = jax.vjp(forward, tokens.astype(jnp.float32), encoder.astype(jnp.float32), *floats)
        gradients = pullback(grad_out.astype(jnp.float32))
        totals = tuple((first + second for first, second in zip(totals, gradients[2:])))
        return (totals, (result, gradients[0], gradients[1]))
    zero_grads = tuple((jnp.zeros(param.shape, jnp.float32) for param in floats))
    totals, (outputs, input_grads, enc_grads) = lax.scan(one_group, zero_grads, (inputs, enc_states, cotangent, slot_order, seq_lengths, enc_lengths))
    return (outputs, input_grads, enc_grads, totals[0], totals[1], totals[2], totals[3], totals[4], totals[5], totals[6], totals[7], totals[8], totals[9], totals[10], totals[11])
```

```python
import functools

import jax
import jax.numpy as jnp
from jax import lax
from jax.experimental import pallas as pl
from jax.experimental.pallas import tpu as pltpu
from jax.sharding import PartitionSpec as P

HEAD = 64
BF = jnp.bfloat16
F32 = jnp.float32


def dot(left, right):
    return jnp.dot(left, right, preferred_element_type=F32)


def dot_left(left, right):
    return lax.dot_general(left, right, (((0,), (0,)), ((), ())), preferred_element_type=F32)


def dot_right(left, right):
    return lax.dot_general(left, right, (((1,), (1,)), ((), ())), preferred_element_type=F32)


def swap(value, axis, bit):
    size = lax.axis_size(axis)
    return lax.ppermute(value, axis, [(i, i ^ bit) for i in range(size)])


def gather_ctx(own):
    size = lax.axis_size("ctx")
    blocks = {0: own}
    bit = size // 2
    while bit:
        for index in sorted(blocks):
            blocks[index | bit] = swap(blocks[index], "ctx", bit)
        bit //= 2
    return [blocks[index] for index in range(size)]


def scatter_ctx(blocks):
    blocks = dict(enumerate(blocks))
    size, bit = len(blocks), 1
    while bit < size:
        for index in sorted(blocks, reverse=True):
            if index & bit:
                arrived = swap(blocks.pop(index).astype(BF), "ctx", bit)
                blocks[index ^ bit] = blocks[index ^ bit] + arrived.astype(F32)
        bit *= 2
    return blocks[0]


def halves(blocks):
    middle = len(blocks) // 2
    return (jnp.concatenate(blocks[:middle], 0), jnp.concatenate(blocks[middle:], 0))


def scatter_halves(low, high, rows):
    count = low.shape[0] // rows
    cut = [low[i * rows : (i + 1) * rows] for i in range(count)]
    return scatter_ctx(cut + [high[i * rows : (i + 1) * rows] for i in range(count)])


def norm_parts(values):
    center = values - jnp.mean(values, axis=-1, keepdims=True)
    rate = lax.rsqrt(jnp.mean(center * center, axis=-1, keepdims=True) + 1e-05)
    return center * rate, rate


def norm_back(hat, rate, gain, grad):
    scaled = grad * gain
    inner = jnp.mean(scaled * hat, axis=-1, keepdims=True)
    result = rate * (scaled - jnp.mean(scaled, axis=-1, keepdims=True) - hat * inner)
    return result, jnp.sum(grad * hat, axis=0), jnp.sum(grad, axis=0)


def gelu_back(values, grad):
    unused, pullback = jax.vjp(lambda u: jax.nn.gelu(u, approximate=True), values)
    return pullback(grad)[0]


def split_heads(block, heads, head):
    wide = block.astype(F32)
    lane = lax.broadcasted_iota(jnp.int32, wide.shape, 1) // head
    parts = [jnp.where(lane == h, wide, 0.0).astype(BF) for h in range(heads)]
    return jnp.concatenate(parts, 0)


def spread(row, heads):
    return jnp.concatenate([row] * heads, 1)


def allowed_keys(first, chunk, low, high):
    index = first + lax.broadcasted_iota(jnp.int32, (chunk, low.shape[1]), 0)
    return (index >= low) & (index < high)


def forward_kernel(meta, q_ref, k_ref, v_ref, rows_ref, o_ref, lse_ref, top, total, mixed, *, heads, head, chunk, count, offset):
    block = pl.program_id(0) + offset
    queries = q_ref.shape[0]
    split = split_heads(q_ref[...].astype(F32) * 0.125, heads, head)
    low = spread(rows_ref[0, 0:1, :], heads)
    high = spread(rows_ref[0, 1:2, :], heads)
    top[...] = jnp.full_like(top, -1e30)
    total[...] = jnp.zeros_like(total)
    mixed[...] = jnp.zeros_like(mixed)

    def step(index, carry):
        start = pl.multiple_of((index ^ meta[0]) * chunk, chunk)
        keys = k_ref[pl.ds(start, chunk), :]
        values = jnp.transpose(v_ref[pl.ds(start, chunk), :])
        scores = dot_right(keys, split)
        scores = jnp.where(allowed_keys(index * chunk, chunk, low, high), scores, -1e30)
        before = top[...]
        now = jnp.maximum(before, jnp.max(scores, axis=0, keepdims=True))
        decay = jnp.exp(before - now)
        weight = jnp.exp(scores - now)
        top[...] = now
        total[...] = total[...] * decay + jnp.sum(weight, axis=0, keepdims=True)
        weight = weight.astype(BF)
        for h in range(heads):
            rows, cols = slice(h * head, (h + 1) * head), slice(h * queries, (h + 1) * queries)
            mixed[rows, :] = mixed[rows, :] * decay[:, cols] + dot(values[rows, :], weight[:, cols])
        return carry

    lax.fori_loop(meta[1 + block], meta[1 + count + block], step, 0)
    amount = total[...]
    for h in range(heads):
        rows, cols = slice(h * head, (h + 1) * head), slice(h * queries, (h + 1) * queries)
        mixed[rows, :] = mixed[rows, :] / amount[:, cols]
    o_ref[...] = jnp.transpose(mixed[...]).astype(BF)
    lse_ref[0] = top[...] + jnp.log(amount)


def backward_kernel(meta, q_ref, g_ref, o_ref, lse_ref, rows_ref, k_ref, v_ref, dq_ref, dk_ref, dv_ref, dq_sum, *, heads, head, chunk, count, offset):
    block = pl.program_id(0) + offset
    queries = q_ref.shape[0]

    @pl.when(pl.program_id(0) == 0)
    def _():
        dk_ref[...] = jnp.zeros_like(dk_ref)
        dv_ref[...] = jnp.zeros_like(dv_ref)

    split = split_heads(q_ref[...].astype(F32) * 0.125, heads, head)
    grads = split_heads(g_ref[...], heads, head)
    low = spread(rows_ref[0, 0:1, :], heads)
    high = spread(rows_ref[0, 1:2, :], heads)
    lse = lse_ref[0]
    product = jnp.transpose(g_ref[...].astype(F32) * o_ref[...].astype(F32))
    inner = jnp.concatenate(
        [jnp.sum(product[h * head : (h + 1) * head], axis=0, keepdims=True) for h in range(heads)], 1
    )
    dq_sum[...] = jnp.zeros_like(dq_sum)

    def step(index, carry):
        start = pl.multiple_of((index ^ meta[0]) * chunk, chunk)
        keys = k_ref[pl.ds(start, chunk), :]
        scores = dot_right(keys, split)
        scores = jnp.where(allowed_keys(index * chunk, chunk, low, high), scores, -1e30)
        weight = jnp.exp(scores - lse)
        slope = dot_right(v_ref[pl.ds(start, chunk), :], grads)
        slope = (weight * (slope - inner)).astype(BF)
        dv_ref[pl.ds(start, chunk), :] += dot(weight.astype(BF), grads)
        dk_ref[pl.ds(start, chunk), :] += dot(slope, split)
        turned = jnp.transpose(keys)
        for h in range(heads):
            rows, cols = slice(h * head, (h + 1) * head), slice(h * queries, (h + 1) * queries)
            dq_sum[rows, :] += dot(turned[rows, :], slope[:, cols])
        return carry

    lax.fori_loop(meta[1 + block], meta[1 + count + block], step, 0)
    dq_ref[...] = (jnp.transpose(dq_sum[...]) * 0.125).astype(BF)


class Attention:
    def __init__(self, low, high, tile, chunk, flip):
        self.tile, self.chunk = tile, chunk
        self.count = low.shape[0] // tile
        low, high = low.reshape(self.count, tile), high.reshape(self.count, tile)
        self.rows = jnp.stack([low, high], 1)
        first, last = jnp.min(low, 1) // chunk, (jnp.max(high, 1) - 1) // chunk + 1
        self.meta = jnp.concatenate([flip.reshape(1), first, last]).astype(jnp.int32)

    def specs(self, width, heads, offset, queries_at):
        tile = self.tile
        tall = pl.BlockSpec((tile, width), lambda i, m: (i + queries_at, 0))
        rows = pl.BlockSpec((1, 2, tile), lambda i, m: (i + offset, 0, 0))
        return tall, rows

    def forward(self, queries, keys, values, offset, steps, queries_at):
        width, heads = queries.shape[1], queries.shape[1] // HEAD
        tall, rows = self.specs(width, heads, offset, queries_at)
        whole = pl.BlockSpec(keys.shape, lambda i, m: (0, 0))
        lanes = heads * self.tile
        body = functools.partial(
            forward_kernel, heads=heads, head=HEAD, chunk=self.chunk, count=self.count, offset=offset
        )
        pairs = steps * self.tile * keys.shape[0] * heads
        return pl.pallas_call(
            body,
            grid_spec=pltpu.PrefetchScalarGridSpec(
                num_scalar_prefetch=1,
                grid=(steps,),
                in_specs=[tall, whole, whole, rows],
                out_specs=[
                    pl.BlockSpec((self.tile, width), lambda i, m: (i, 0)),
                    pl.BlockSpec((1, 1, lanes), lambda i, m: (i, 0, 0)),
                ],
                scratch_shapes=[
                    pltpu.VMEM((1, lanes), F32),
                    pltpu.VMEM((1, lanes), F32),
                    pltpu.VMEM((width, self.tile), F32),
                ],
            ),
            out_shape=[
                jax.ShapeDtypeStruct((steps * self.tile, width), BF),
                jax.ShapeDtypeStruct((steps, 1, lanes), F32),
            ],
            cost_estimate=pl.CostEstimate(flops=pairs * 256, transcendentals=pairs // 2, bytes_accessed=2 << 20),
            compiler_params=pltpu.CompilerParams(vmem_limit_bytes=24 << 20),
        )(self.meta, queries, keys, values, self.rows)

    def backward(self, queries, grads, mixed, lse, keys, values, offset, steps, queries_at):
        width, heads = queries.shape[1], queries.shape[1] // HEAD
        tall, rows = self.specs(width, heads, offset, queries_at)
        near = pl.BlockSpec((self.tile, width), lambda i, m: (i, 0))
        whole = pl.BlockSpec(keys.shape, lambda i, m: (0, 0))
        lanes = heads * self.tile
        body = functools.partial(
            backward_kernel, heads=heads, head=HEAD, chunk=self.chunk, count=self.count, offset=offset
        )
        pairs = steps * self.tile * keys.shape[0] * heads
        return pl.pallas_call(
            body,
            grid_spec=pltpu.PrefetchScalarGridSpec(
                num_scalar_prefetch=1,
                grid=(steps,),
                in_specs=[tall, near, near, pl.BlockSpec((1, 1, lanes), lambda i, m: (i, 0, 0)), rows, whole, whole],
                out_specs=[near, whole, whole],
                scratch_shapes=[pltpu.VMEM((width, self.tile), F32)],
            ),
            out_shape=[
                jax.ShapeDtypeStruct((steps * self.tile, width), BF),
                jax.ShapeDtypeStruct(keys.shape, F32),
                jax.ShapeDtypeStruct(keys.shape, F32),
            ],
            cost_estimate=pl.CostEstimate(flops=pairs * 640, transcendentals=pairs // 2, bytes_accessed=4 << 20),
            compiler_params=pltpu.CompilerParams(vmem_limit_bytes=32 << 20),
        )(self.meta, queries, grads, mixed, lse, self.rows, keys, values)


def gather_wsh(part):
    return lax.all_gather(part, "wsh", axis=0, tiled=True)


def scatter_wsh(whole):
    return lax.psum_scatter(whole.astype(BF), "wsh", scatter_dimension=0, tiled=True)


def piece_moves(groups, size):
    return [((g % size) * groups + g // size, g) for g in range(groups * size)]


def body(
    inputs,
    enc_states,
    cotangent,
    slot_order,
    seq_lengths,
    enc_lengths,
    self_query,
    self_key,
    self_value,
    self_out,
    cross_query,
    cross_key,
    cross_value,
    cross_out,
    feed_in,
    feed_out,
    norm_gains,
    norm_shifts,
):
    size, groups = lax.axis_size("ctx"), lax.axis_size("wsh")
    mine, row = lax.axis_index("ctx"), lax.axis_index("wsh")
    slots = inputs.shape[1]
    total = slots * size
    enc_slots = enc_states.shape[1]
    width = inputs.shape[2]
    rows = self_query.shape[0]
    cols = width // size
    piece = rows // size
    ff_cols = feed_in.shape[1] // size
    ff_rows = feed_out.shape[0] // size

    def columns(matrix):
        return lax.dynamic_slice_in_dim(matrix, mine * cols, cols, 1)

    norms = jnp.concatenate([norm_gains, norm_shifts, jnp.zeros((rows, 120), BF)], 1)
    self_full = gather_wsh(jnp.concatenate([columns(self_query), columns(self_key), columns(self_value), norms], 1))
    q_full, k_full, v_full = (self_full[:, i * cols : (i + 1) * cols] for i in range(3))
    norm_rows = jnp.transpose(self_full[:, 3 * cols : 3 * cols + 8].astype(F32))
    gains, shifts = norm_rows[:4, None, :], norm_rows[4:, None, :]

    def out_piece(matrix):
        return lax.dynamic_slice_in_dim(matrix, mine * piece, piece, 0)

    pieces = jnp.concatenate([out_piece(self_out), out_piece(cross_out)], 0)
    pieces = lax.ppermute(pieces, ("ctx", "wsh"), piece_moves(groups, size))
    pieces = gather_wsh(pieces).reshape(groups, 2, piece, width)
    out_full, cross_o_full = pieces[:, 0].reshape(cols, width), pieces[:, 1].reshape(cols, width)
    cross_full = gather_wsh(jnp.concatenate([columns(cross_query), columns(cross_key), columns(cross_value)], 1))
    cq_full, ck_full, cv_full = (cross_full[:, i * cols : (i + 1) * cols] for i in range(3))
    first_part = lax.dynamic_slice_in_dim(feed_in.reshape(rows, groups, size, ff_rows), mine, 1, 2)
    second_part = lax.dynamic_slice_in_dim(feed_out, mine * ff_rows, ff_rows, 0)
    feed = jnp.concatenate([first_part.reshape(rows, ff_cols), second_part.reshape(rows, ff_cols)], 0)
    feed = gather_wsh(feed).reshape(groups, 2, rows, ff_cols)
    first_full = feed[:, 0].reshape(groups * rows, ff_cols)
    second_full = feed[:, 1].reshape(groups * ff_rows, width)

    relative = jnp.arange(size, dtype=jnp.int32) ^ mine
    order = jnp.take(slot_order[0].reshape(size, slots), relative, axis=0).reshape(total)
    place = (relative[:, None] * slots + jnp.arange(slots, dtype=jnp.int32)).reshape(total)
    lower = jnp.arange(seq_lengths.shape[1])
    lower = lower[None, :] <= lower[:, None]
    ends = jnp.sum(jnp.where(lower, seq_lengths[0][None, :], 0), 1)
    enc_ends = jnp.sum(jnp.where(lower, enc_lengths[0][None, :], 0), 1)
    passed = ends[None, :] <= place[:, None]
    starts = jnp.max(jnp.where(passed, ends[None, :], 0), 1)
    enc_from = jnp.max(jnp.where(passed, enc_ends[None, :], 0), 1)
    enc_to = jnp.min(jnp.where(passed, enc_slots * size, enc_ends[None, :]), 1)
    self_att = Attention(starts, place + 1, 256, 256, mine * (slots // 256))
    cross_att = Attention(enc_from, enc_to, 256, 128, mine * (enc_slots // 128))
    tiles = total // 256
    half = tiles // 2

    to_place = (order[None, :] == place[:, None]).astype(BF)
    to_slot = (order[:slots, None] == place[None, :]).astype(BF)
    tokens_all = jnp.concatenate(gather_ctx(inputs[0]), 0)
    tokens_all = dot(to_place, tokens_all)
    tokens = tokens_all[:slots]
    encoder = jnp.concatenate(gather_ctx(enc_states[0]), 0)
    outside = jnp.concatenate(gather_ctx(cotangent[0]), 0)
    outside = dot(to_place[:slots], outside)

    hat_all, unused = norm_parts(tokens_all)
    normed_one = (hat_all * gains[0] + shifts[0]).astype(BF)
    queries = dot(normed_one, q_full).astype(BF)
    keys = dot(normed_one, k_full).astype(BF)
    values = dot(normed_one, v_full).astype(BF)
    mixed_high, lse_high = self_att.forward(queries, keys, values, half, half, half)
    mixed_low, lse_low = self_att.forward(queries, keys, values, 0, half, 0)
    after_self = tokens + scatter_halves(dot(mixed_low, out_full), dot(mixed_high, out_full), slots)

    hat_two, rate_two = norm_parts(after_self)
    normed_two = halves(gather_ctx((hat_two * gains[1] + shifts[1]).astype(BF)))
    enc_keys = dot(encoder, ck_full).astype(BF)
    enc_values = dot(encoder, cv_full).astype(BF)
    queries_two = [dot(part, cq_full).astype(BF) for part in normed_two]
    mixed_two = [
        cross_att.forward(queries_two[side], enc_keys, enc_values, side * half, half, 0) for side in range(2)
    ]
    after_cross = after_self + scatter_halves(*(dot(part[0], cross_o_full) for part in mixed_two), slots)

    hat_three, rate_three = norm_parts(after_cross)
    normed_three = halves(gather_ctx((hat_three * gains[2] + shifts[2]).astype(BF)))
    pre_act = [dot(part, first_full) for part in normed_three]
    hidden = [jax.nn.gelu(part, approximate=True).astype(BF) for part in pre_act]
    after_ffn = after_cross + scatter_halves(*(dot(part, second_full) for part in hidden), slots)
    hat_four, rate_four = norm_parts(after_ffn)
    result = hat_four * gains[3] + shifts[3]
    result = jnp.concatenate(gather_ctx(result.astype(BF)), 0)
    result = dot(to_slot, result)

    grad_ffn, gain_three, shift_three = norm_back(hat_four, rate_four, gains[3], outside)
    grad_in = halves(gather_ctx(grad_ffn.astype(BF)))
    grad_pre = [
        gelu_back(part, dot_right(grad, second_full)).astype(BF)
        for part, grad in zip(pre_act, grad_in)
    ]
    arrived = scatter_halves(*(dot_right(grad, first_full) for grad in grad_pre), slots)
    norm_part, gain_two, shift_two = norm_back(hat_three, rate_three, gains[2], arrived)
    grad_cross = grad_ffn + norm_part
    grad_first = sum(dot_left(n, g) for n, g in zip(normed_three, grad_pre))
    grad_second = sum(dot_left(n, g) for n, g in zip(hidden, grad_in))
    feed_grads = jnp.concatenate(
        [
            grad_first.astype(BF).reshape(groups, rows, ff_cols),
            grad_second.astype(BF).reshape(groups, rows, ff_cols),
        ],
        1,
    )
    feed_grads = scatter_wsh(feed_grads.reshape(groups * 2 * rows, ff_cols))
    feed_grads = lax.all_gather(feed_grads, "ctx", axis=0).reshape(size, 2, rows, ff_cols)
    feed_in_grad = jnp.transpose(feed_grads[:, 0].reshape(size, rows, groups, ff_rows), (1, 2, 0, 3))
    feed_in_grad = feed_in_grad.reshape(rows, groups * size * ff_rows).astype(F32)
    feed_out_grad = feed_grads[:, 1].reshape(size * ff_rows, width).astype(F32)

    def share(query_grad, key_grad, value_grad, out_grad):
        packed = [
            query_grad.astype(BF),
            key_grad.astype(BF),
            value_grad.astype(BF),
            out_grad.astype(BF).reshape(groups * rows, cols),
        ]
        packed = scatter_wsh(jnp.concatenate(packed, 1))
        moved = packed[:, 3 * cols :].reshape(piece, width)
        moved = lax.ppermute(moved, ("ctx", "wsh"), [(b, a) for a, b in piece_moves(groups, size)])
        packed = jnp.concatenate([packed[:, : 3 * cols], moved.reshape(rows, cols)], 1)
        packed = lax.all_gather(packed, "ctx", axis=0)
        three = [
            jnp.transpose(packed[:, :, i * cols : (i + 1) * cols], (1, 0, 2)).reshape(rows, width).astype(F32)
            for i in range(3)
        ]
        return three + [packed[:, :, 3 * cols :].reshape(size, piece, width).reshape(rows, width).astype(F32)]

    grad_in = halves(gather_ctx(grad_cross.astype(BF)))
    grad_mixed = [dot_right(grad, cross_o_full).astype(BF) for grad in grad_in]
    back = [
        cross_att.backward(
            queries_two[side], grad_mixed[side], *mixed_two[side], enc_keys, enc_values, side * half, half, 0
        )
        for side in range(2)
    ]
    arrived = scatter_halves(*(dot_right(part[0], cq_full) for part in back), slots)
    norm_part, gain_one, shift_one = norm_back(hat_two, rate_two, gains[1], arrived)
    grad_self = grad_cross + norm_part
    grad_ek = (back[0][1] + back[1][1]).astype(BF)
    grad_ev = (back[0][2] + back[1][2]).astype(BF)
    enc_part = dot_right(grad_ek, ck_full) + dot_right(grad_ev, cv_full)
    enc_grad = scatter_ctx([enc_part[i * enc_slots : (i + 1) * enc_slots] for i in range(size)])
    cross_q_grad, cross_k_grad, cross_v_grad, cross_o_grad = share(
        sum(dot_left(n, part[0]) for n, part in zip(normed_two, back)),
        dot_left(encoder, grad_ek),
        dot_left(encoder, grad_ev),
        sum(dot_left(part[0], g) for part, g in zip(mixed_two, grad_in)),
    )

    grad_in = halves(gather_ctx(grad_self.astype(BF)))
    grad_mixed = [dot_right(grad, out_full).astype(BF) for grad in grad_in]
    back_low = self_att.backward(queries, grad_mixed[0], mixed_low, lse_low, keys, values, 0, half, 0)
    back_high = self_att.backward(queries, grad_mixed[1], mixed_high, lse_high, keys, values, half, half, half)
    grad_q = jnp.concatenate([back_low[0], back_high[0]], 0)
    grad_k = (back_low[1] + back_high[1]).astype(BF)
    grad_v = (back_low[2] + back_high[2]).astype(BF)
    arrived = dot_right(grad_q, q_full) + dot_right(grad_k, k_full) + dot_right(grad_v, v_full)
    arrived = scatter_ctx([arrived[i * slots : (i + 1) * slots] for i in range(size)])
    hat_one, rate_one = norm_parts(tokens)
    norm_part, gain_zero, shift_zero = norm_back(hat_one, rate_one, gains[0], arrived)
    input_grad = grad_self + norm_part
    input_grad = jnp.concatenate(gather_ctx(input_grad.astype(BF)), 0)
    input_grad = dot(to_slot, input_grad)
    query_grad, key_grad, value_grad, out_grad = share(
        dot_left(normed_one, grad_q),
        dot_left(normed_one, grad_k),
        dot_left(normed_one, grad_v),
        dot_left(mixed_low, grad_in[0]) + dot_left(mixed_high, grad_in[1]),
    )

    terms = jnp.stack(
        [gain_zero, gain_one, gain_two, gain_three, shift_zero, shift_one, shift_two, shift_three], 0
    )
    for axis, amount in (("ctx", size), ("wsh", groups)):
        bit = 1
        while bit < amount:
            terms = terms + swap(terms, axis, bit)
            bit *= 2
    terms = jnp.transpose(lax.dynamic_slice_in_dim(terms, row * rows, rows, 1))
    return (
        result[None],
        input_grad[None],
        enc_grad[None],
        query_grad,
        key_grad,
        value_grad,
        out_grad,
        cross_q_grad,
        cross_k_grad,
        cross_v_grad,
        cross_o_grad,
        feed_in_grad,
        feed_out_grad,
        terms[:, :4],
        terms[:, 4:],
    )


def solution(mesh):
    token, weight = P("wsh", "ctx", None), P("wsh", None)
    in_specs = (token,) * 3 + (weight,) * 15
    out_specs = (token,) * 3 + (weight,) * 12
    return jax.shard_map(body, mesh=mesh, in_specs=in_specs, out_specs=out_specs, check_vma=False)
```

```python
import functools

import jax
import jax.numpy as jnp
from jax import lax
from jax.experimental import pallas as pl
from jax.experimental.pallas import tpu as pltpu
from jax.sharding import PartitionSpec as P

HEAD = 64
BF = jnp.bfloat16
F32 = jnp.float32


def dot(left, right):
    return jnp.dot(left, right, preferred_element_type=F32)


def dot_left(left, right):
    return lax.dot_general(left, right, (((0,), (0,)), ((), ())), preferred_element_type=F32)


def dot_right(left, right):
    return lax.dot_general(left, right, (((1,), (1,)), ((), ())), preferred_element_type=F32)


def swap(value, axis, bit):
    size = lax.axis_size(axis)
    return lax.ppermute(value, axis, [(i, i ^ bit) for i in range(size)])


def gather_ctx(own):
    size = lax.axis_size("ctx")
    blocks = {0: own}
    bit = size // 2
    while bit:
        for index in sorted(blocks):
            blocks[index | bit] = swap(blocks[index], "ctx", bit)
        bit //= 2
    return [blocks[index] for index in range(size)]


def scatter_ctx(blocks):
    blocks = dict(enumerate(blocks))
    size, bit = len(blocks), 1
    while bit < size:
        for index in sorted(blocks, reverse=True):
            if index & bit:
                arrived = swap(blocks.pop(index).astype(BF), "ctx", bit)
                blocks[index ^ bit] = blocks[index ^ bit] + arrived.astype(F32)
        bit *= 2
    return blocks[0]


def halves(blocks):
    middle = len(blocks) // 2
    return (jnp.concatenate(blocks[:middle], 0), jnp.concatenate(blocks[middle:], 0))


def scatter_halves(low, high, rows):
    count = low.shape[0] // rows
    cut = [low[i * rows : (i + 1) * rows] for i in range(count)]
    return scatter_ctx(cut + [high[i * rows : (i + 1) * rows] for i in range(count)])


def norm_parts(values):
    center = values - jnp.mean(values, axis=-1, keepdims=True)
    rate = lax.rsqrt(jnp.mean(center * center, axis=-1, keepdims=True) + 1e-05)
    return center * rate, rate


def norm_back(hat, rate, gain, grad):
    scaled = grad * gain
    inner = jnp.mean(scaled * hat, axis=-1, keepdims=True)
    result = rate * (scaled - jnp.mean(scaled, axis=-1, keepdims=True) - hat * inner)
    return result, jnp.sum(grad * hat, axis=0), jnp.sum(grad, axis=0)


def gelu_back(values, grad):
    unused, pullback = jax.vjp(lambda u: jax.nn.gelu(u, approximate=True), values)
    return pullback(grad)[0]


def split_heads(block, heads, head):
    wide = block.astype(F32)
    lane = lax.broadcasted_iota(jnp.int32, wide.shape, 1) // head
    parts = [jnp.where(lane == h, wide, 0.0).astype(BF) for h in range(heads)]
    return jnp.concatenate(parts, 0)


def spread(row, heads):
    return jnp.concatenate([row] * heads, 1)


def allowed_keys(first, chunk, low, high):
    index = first + lax.broadcasted_iota(jnp.int32, (chunk, low.shape[1]), 0)
    return (index >= low) & (index < high)


def forward_kernel(meta, q_ref, k_ref, v_ref, rows_ref, o_ref, lse_ref, top, total, mixed, *, heads, head, chunk, count, offset):
    block = pl.program_id(0) + offset
    queries = q_ref.shape[0]
    split = split_heads(q_ref[...].astype(F32) * 0.125, heads, head)
    low = spread(rows_ref[0, 0:1, :], heads)
    high = spread(rows_ref[0, 1:2, :], heads)
    top[...] = jnp.full_like(top, -1e30)
    total[...] = jnp.zeros_like(total)
    mixed[...] = jnp.zeros_like(mixed)

    def step(index, carry):
        start = pl.multiple_of((index ^ meta[0]) * chunk, chunk)
        keys = k_ref[pl.ds(start, chunk), :]
        values = jnp.transpose(v_ref[pl.ds(start, chunk), :])
        scores = dot_right(keys, split)
        scores = jnp.where(allowed_keys(index * chunk, chunk, low, high), scores, -1e30)
        before = top[...]
        now = jnp.maximum(before, jnp.max(scores, axis=0, keepdims=True))
        decay = jnp.exp(before - now)
        weight = jnp.exp(scores - now)
        top[...] = now
        total[...] = total[...] * decay + jnp.sum(weight, axis=0, keepdims=True)
        weight = weight.astype(BF)
        for h in range(heads):
            rows, cols = slice(h * head, (h + 1) * head), slice(h * queries, (h + 1) * queries)
            mixed[rows, :] = mixed[rows, :] * decay[:, cols] + dot(values[rows, :], weight[:, cols])
        return carry

    lax.fori_loop(meta[1 + block], meta[1 + count + block], step, 0)
    amount = total[...]
    for h in range(heads):
        rows, cols = slice(h * head, (h + 1) * head), slice(h * queries, (h + 1) * queries)
        mixed[rows, :] = mixed[rows, :] / amount[:, cols]
    o_ref[...] = jnp.transpose(mixed[...]).astype(BF)
    lse_ref[0] = top[...] + jnp.log(amount)


def backward_kernel(meta, q_ref, g_ref, o_ref, lse_ref, rows_ref, k_ref, v_ref, dq_ref, dk_ref, dv_ref, dq_sum, *, heads, head, chunk, count, offset):
    block = pl.program_id(0) + offset
    queries = q_ref.shape[0]

    @pl.when(pl.program_id(0) == 0)
    def _():
        dk_ref[...] = jnp.zeros_like(dk_ref)
        dv_ref[...] = jnp.zeros_like(dv_ref)

    split = split_heads(q_ref[...].astype(F32) * 0.125, heads, head)
    grads = split_heads(g_ref[...], heads, head)
    low = spread(rows_ref[0, 0:1, :], heads)
    high = spread(rows_ref[0, 1:2, :], heads)
    lse = lse_ref[0]
    product = jnp.transpose(g_ref[...].astype(F32) * o_ref[...].astype(F32))
    inner = jnp.concatenate(
        [jnp.sum(product[h * head : (h + 1) * head], axis=0, keepdims=True) for h in range(heads)], 1
    )
    dq_sum[...] = jnp.zeros_like(dq_sum)

    def step(index, carry):
        start = pl.multiple_of((index ^ meta[0]) * chunk, chunk)
        keys = k_ref[pl.ds(start, chunk), :]
        scores = dot_right(keys, split)
        scores = jnp.where(allowed_keys(index * chunk, chunk, low, high), scores, -1e30)
        weight = jnp.exp(scores - lse)
        slope = dot_right(v_ref[pl.ds(start, chunk), :], grads)
        slope = (weight * (slope - inner)).astype(BF)
        dv_ref[pl.ds(start, chunk), :] += dot(weight.astype(BF), grads)
        dk_ref[pl.ds(start, chunk), :] += dot(slope, split)
        turned = jnp.transpose(keys)
        for h in range(heads):
            rows, cols = slice(h * head, (h + 1) * head), slice(h * queries, (h + 1) * queries)
            dq_sum[rows, :] += dot(turned[rows, :], slope[:, cols])
        return carry

    lax.fori_loop(meta[1 + block], meta[1 + count + block], step, 0)
    dq_ref[...] = (jnp.transpose(dq_sum[...]) * 0.125).astype(BF)


class Attention:
    def __init__(self, low, high, tile, chunk, flip):
        self.tile, self.chunk = tile, chunk
        self.count = low.shape[0] // tile
        low, high = low.reshape(self.count, tile), high.reshape(self.count, tile)
        self.rows = jnp.stack([low, high], 1)
        first, last = jnp.min(low, 1) // chunk, (jnp.max(high, 1) - 1) // chunk + 1
        self.meta = jnp.concatenate([flip.reshape(1), first, last]).astype(jnp.int32)

    def specs(self, width, heads, offset, queries_at):
        tile = self.tile
        tall = pl.BlockSpec((tile, width), lambda i, m: (i + queries_at, 0))
        rows = pl.BlockSpec((1, 2, tile), lambda i, m: (i + offset, 0, 0))
        return tall, rows

    def forward(self, queries, keys, values, offset, steps, queries_at):
        width, heads = queries.shape[1], queries.shape[1] // HEAD
        tall, rows = self.specs(width, heads, offset, queries_at)
        whole = pl.BlockSpec(keys.shape, lambda i, m: (0, 0))
        lanes = heads * self.tile
        body = functools.partial(
            forward_kernel, heads=heads, head=HEAD, chunk=self.chunk, count=self.count, offset=offset
        )
        pairs = steps * self.tile * keys.shape[0] * heads
        return pl.pallas_call(
            body,
            grid_spec=pltpu.PrefetchScalarGridSpec(
                num_scalar_prefetch=1,
                grid=(steps,),
                in_specs=[tall, whole, whole, rows],
                out_specs=[
                    pl.BlockSpec((self.tile, width), lambda i, m: (i, 0)),
                    pl.BlockSpec((1, 1, lanes), lambda i, m: (i, 0, 0)),
                ],
                scratch_shapes=[
                    pltpu.VMEM((1, lanes), F32),
                    pltpu.VMEM((1, lanes), F32),
                    pltpu.VMEM((width, self.tile), F32),
                ],
            ),
            out_shape=[
                jax.ShapeDtypeStruct((steps * self.tile, width), BF),
                jax.ShapeDtypeStruct((steps, 1, lanes), F32),
            ],
            cost_estimate=pl.CostEstimate(flops=pairs * 256, transcendentals=pairs // 2, bytes_accessed=2 << 20),
            compiler_params=pltpu.CompilerParams(vmem_limit_bytes=24 << 20),
        )(self.meta, queries, keys, values, self.rows)

    def backward(self, queries, grads, mixed, lse, keys, values, offset, steps, queries_at):
        width, heads = queries.shape[1], queries.shape[1] // HEAD
        tall, rows = self.specs(width, heads, offset, queries_at)
        near = pl.BlockSpec((self.tile, width), lambda i, m: (i, 0))
        whole = pl.BlockSpec(keys.shape, lambda i, m: (0, 0))
        lanes = heads * self.tile
        body = functools.partial(
            backward_kernel, heads=heads, head=HEAD, chunk=self.chunk, count=self.count, offset=offset
        )
        pairs = steps * self.tile * keys.shape[0] * heads
        return pl.pallas_call(
            body,
            grid_spec=pltpu.PrefetchScalarGridSpec(
                num_scalar_prefetch=1,
                grid=(steps,),
                in_specs=[tall, near, near, pl.BlockSpec((1, 1, lanes), lambda i, m: (i, 0, 0)), rows, whole, whole],
                out_specs=[near, whole, whole],
                scratch_shapes=[pltpu.VMEM((width, self.tile), F32)],
            ),
            out_shape=[
                jax.ShapeDtypeStruct((steps * self.tile, width), BF),
                jax.ShapeDtypeStruct(keys.shape, F32),
                jax.ShapeDtypeStruct(keys.shape, F32),
            ],
            cost_estimate=pl.CostEstimate(flops=pairs * 640, transcendentals=pairs // 2, bytes_accessed=4 << 20),
            compiler_params=pltpu.CompilerParams(vmem_limit_bytes=32 << 20),
        )(self.meta, queries, grads, mixed, lse, self.rows, keys, values)


def gather_wsh(part):
    return lax.all_gather(part, "wsh", axis=0, tiled=True)


def scatter_wsh(whole):
    return lax.psum_scatter(whole.astype(BF), "wsh", scatter_dimension=0, tiled=True)


def piece_moves(groups, size):
    return [((g % size) * groups + g // size, g) for g in range(groups * size)]


def plain_body(
    inputs,
    enc_states,
    cotangent,
    slot_order,
    seq_lengths,
    enc_lengths,
    self_query,
    self_key,
    self_value,
    self_out,
    cross_query,
    cross_key,
    cross_value,
    cross_out,
    feed_in,
    feed_out,
    norm_gains,
    norm_shifts,
):
    size, groups = lax.axis_size("ctx"), lax.axis_size("wsh")
    mine, row = lax.axis_index("ctx"), lax.axis_index("wsh")
    slots = inputs.shape[1]
    total = slots * size
    enc_slots = enc_states.shape[1]
    width = inputs.shape[2]
    rows = self_query.shape[0]
    cols = width // size
    piece = rows // size
    ff_cols = feed_in.shape[1] // size
    ff_rows = feed_out.shape[0] // size

    def columns(matrix):
        return lax.dynamic_slice_in_dim(matrix, mine * cols, cols, 1)

    norms = jnp.concatenate([norm_gains, norm_shifts, jnp.zeros((rows, 120), BF)], 1)
    self_full = gather_wsh(jnp.concatenate([columns(self_query), columns(self_key), columns(self_value), norms], 1))
    q_full, k_full, v_full = (self_full[:, i * cols : (i + 1) * cols] for i in range(3))
    norm_rows = jnp.transpose(self_full[:, 3 * cols : 3 * cols + 8].astype(F32))
    gains, shifts = norm_rows[:4, None, :], norm_rows[4:, None, :]

    def out_piece(matrix):
        return lax.dynamic_slice_in_dim(matrix, mine * piece, piece, 0)

    pieces = jnp.concatenate([out_piece(self_out), out_piece(cross_out)], 0)
    pieces = lax.ppermute(pieces, ("ctx", "wsh"), piece_moves(groups, size))
    pieces = gather_wsh(pieces).reshape(groups, 2, piece, width)
    out_full, cross_o_full = pieces[:, 0].reshape(cols, width), pieces[:, 1].reshape(cols, width)
    cross_full = gather_wsh(jnp.concatenate([columns(cross_query), columns(cross_key), columns(cross_value)], 1))
    cq_full, ck_full, cv_full = (cross_full[:, i * cols : (i + 1) * cols] for i in range(3))
    first_part = lax.dynamic_slice_in_dim(feed_in.reshape(rows, groups, size, ff_rows), mine, 1, 2)
    second_part = lax.dynamic_slice_in_dim(feed_out, mine * ff_rows, ff_rows, 0)
    feed = jnp.concatenate([first_part.reshape(rows, ff_cols), second_part.reshape(rows, ff_cols)], 0)
    feed = gather_wsh(feed).reshape(groups, 2, rows, ff_cols)
    first_full = feed[:, 0].reshape(groups * rows, ff_cols)
    second_full = feed[:, 1].reshape(groups * ff_rows, width)

    relative = jnp.arange(size, dtype=jnp.int32) ^ mine
    order = jnp.take(slot_order[0].reshape(size, slots), relative, axis=0).reshape(total)
    place = (relative[:, None] * slots + jnp.arange(slots, dtype=jnp.int32)).reshape(total)
    lower = jnp.arange(seq_lengths.shape[1])
    lower = lower[None, :] <= lower[:, None]
    ends = jnp.sum(jnp.where(lower, seq_lengths[0][None, :], 0), 1)
    enc_ends = jnp.sum(jnp.where(lower, enc_lengths[0][None, :], 0), 1)
    passed = ends[None, :] <= place[:, None]
    starts = jnp.max(jnp.where(passed, ends[None, :], 0), 1)
    enc_from = jnp.max(jnp.where(passed, enc_ends[None, :], 0), 1)
    enc_to = jnp.min(jnp.where(passed, enc_slots * size, enc_ends[None, :]), 1)
    self_att = Attention(starts, place + 1, 256, 256, mine * (slots // 256))
    cross_att = Attention(enc_from, enc_to, 256, 128, mine * (enc_slots // 128))
    tiles = total // 256
    half = tiles // 2

    to_place = (order[None, :] == place[:, None]).astype(BF)
    to_slot = (order[:slots, None] == place[None, :]).astype(BF)
    tokens_all = jnp.concatenate(gather_ctx(inputs[0]), 0)
    tokens_all = dot(to_place, tokens_all)
    tokens = tokens_all[:slots]
    encoder = jnp.concatenate(gather_ctx(enc_states[0]), 0)
    outside = jnp.concatenate(gather_ctx(cotangent[0]), 0)
    outside = dot(to_place[:slots], outside)

    hat_all, unused = norm_parts(tokens_all)
    normed_one = (hat_all * gains[0] + shifts[0]).astype(BF)
    queries = dot(normed_one, q_full).astype(BF)
    keys = dot(normed_one, k_full).astype(BF)
    values = dot(normed_one, v_full).astype(BF)
    mixed_high, lse_high = self_att.forward(queries, keys, values, half, half, half)
    mixed_low, lse_low = self_att.forward(queries, keys, values, 0, half, 0)
    after_self = tokens + scatter_halves(dot(mixed_low, out_full), dot(mixed_high, out_full), slots)

    hat_two, rate_two = norm_parts(after_self)
    normed_two = halves(gather_ctx((hat_two * gains[1] + shifts[1]).astype(BF)))
    enc_keys = dot(encoder, ck_full).astype(BF)
    enc_values = dot(encoder, cv_full).astype(BF)
    queries_two = [dot(part, cq_full).astype(BF) for part in normed_two]
    mixed_two = [
        cross_att.forward(queries_two[side], enc_keys, enc_values, side * half, half, 0) for side in range(2)
    ]
    after_cross = after_self + scatter_halves(*(dot(part[0], cross_o_full) for part in mixed_two), slots)

    hat_three, rate_three = norm_parts(after_cross)
    normed_three = halves(gather_ctx((hat_three * gains[2] + shifts[2]).astype(BF)))
    pre_act = [dot(part, first_full) for part in normed_three]
    hidden = [jax.nn.gelu(part, approximate=True).astype(BF) for part in pre_act]
    after_ffn = after_cross + scatter_halves(*(dot(part, second_full) for part in hidden), slots)
    hat_four, rate_four = norm_parts(after_ffn)
    result = hat_four * gains[3] + shifts[3]
    result = jnp.concatenate(gather_ctx(result.astype(BF)), 0)
    result = dot(to_slot, result)

    grad_ffn, gain_three, shift_three = norm_back(hat_four, rate_four, gains[3], outside)
    grad_in = halves(gather_ctx(grad_ffn.astype(BF)))
    grad_pre = [
        gelu_back(part, dot_right(grad, second_full)).astype(BF)
        for part, grad in zip(pre_act, grad_in)
    ]
    arrived = scatter_halves(*(dot_right(grad, first_full) for grad in grad_pre), slots)
    norm_part, gain_two, shift_two = norm_back(hat_three, rate_three, gains[2], arrived)
    grad_cross = grad_ffn + norm_part
    grad_first = sum(dot_left(n, g) for n, g in zip(normed_three, grad_pre))
    grad_second = sum(dot_left(n, g) for n, g in zip(hidden, grad_in))
    feed_grads = jnp.concatenate(
        [
            grad_first.astype(BF).reshape(groups, rows, ff_cols),
            grad_second.astype(BF).reshape(groups, rows, ff_cols),
        ],
        1,
    )
    feed_grads = scatter_wsh(feed_grads.reshape(groups * 2 * rows, ff_cols))
    feed_grads = lax.all_gather(feed_grads, "ctx", axis=0).reshape(size, 2, rows, ff_cols)
    feed_in_grad = jnp.transpose(feed_grads[:, 0].reshape(size, rows, groups, ff_rows), (1, 2, 0, 3))
    feed_in_grad = feed_in_grad.reshape(rows, groups * size * ff_rows).astype(F32)
    feed_out_grad = feed_grads[:, 1].reshape(size * ff_rows, width).astype(F32)

    def share(query_grad, key_grad, value_grad, out_grad):
        packed = [
            query_grad.astype(BF),
            key_grad.astype(BF),
            value_grad.astype(BF),
            out_grad.astype(BF).reshape(groups * rows, cols),
        ]
        packed = scatter_wsh(jnp.concatenate(packed, 1))
        moved = packed[:, 3 * cols :].reshape(piece, width)
        moved = lax.ppermute(moved, ("ctx", "wsh"), [(b, a) for a, b in piece_moves(groups, size)])
        packed = jnp.concatenate([packed[:, : 3 * cols], moved.reshape(rows, cols)], 1)
        packed = lax.all_gather(packed, "ctx", axis=0)
        three = [
            jnp.transpose(packed[:, :, i * cols : (i + 1) * cols], (1, 0, 2)).reshape(rows, width).astype(F32)
            for i in range(3)
        ]
        return three + [packed[:, :, 3 * cols :].reshape(size, piece, width).reshape(rows, width).astype(F32)]

    grad_in = halves(gather_ctx(grad_cross.astype(BF)))
    grad_mixed = [dot_right(grad, cross_o_full).astype(BF) for grad in grad_in]
    back = [
        cross_att.backward(
            queries_two[side], grad_mixed[side], *mixed_two[side], enc_keys, enc_values, side * half, half, 0
        )
        for side in range(2)
    ]
    arrived = scatter_halves(*(dot_right(part[0], cq_full) for part in back), slots)
    norm_part, gain_one, shift_one = norm_back(hat_two, rate_two, gains[1], arrived)
    grad_self = grad_cross + norm_part
    grad_ek = (back[0][1] + back[1][1]).astype(BF)
    grad_ev = (back[0][2] + back[1][2]).astype(BF)
    enc_part = dot_right(grad_ek, ck_full) + dot_right(grad_ev, cv_full)
    enc_grad = scatter_ctx([enc_part[i * enc_slots : (i + 1) * enc_slots] for i in range(size)])
    cross_q_grad, cross_k_grad, cross_v_grad, cross_o_grad = share(
        sum(dot_left(n, part[0]) for n, part in zip(normed_two, back)),
        dot_left(encoder, grad_ek),
        dot_left(encoder, grad_ev),
        sum(dot_left(part[0], g) for part, g in zip(mixed_two, grad_in)),
    )

    grad_in = halves(gather_ctx(grad_self.astype(BF)))
    grad_mixed = [dot_right(grad, out_full).astype(BF) for grad in grad_in]
    back_low = self_att.backward(queries, grad_mixed[0], mixed_low, lse_low, keys, values, 0, half, 0)
    back_high = self_att.backward(queries, grad_mixed[1], mixed_high, lse_high, keys, values, half, half, half)
    grad_q = jnp.concatenate([back_low[0], back_high[0]], 0)
    grad_k = (back_low[1] + back_high[1]).astype(BF)
    grad_v = (back_low[2] + back_high[2]).astype(BF)
    arrived = dot_right(grad_q, q_full) + dot_right(grad_k, k_full) + dot_right(grad_v, v_full)
    arrived = scatter_ctx([arrived[i * slots : (i + 1) * slots] for i in range(size)])
    hat_one, rate_one = norm_parts(tokens)
    norm_part, gain_zero, shift_zero = norm_back(hat_one, rate_one, gains[0], arrived)
    input_grad = grad_self + norm_part
    input_grad = jnp.concatenate(gather_ctx(input_grad.astype(BF)), 0)
    input_grad = dot(to_slot, input_grad)
    query_grad, key_grad, value_grad, out_grad = share(
        dot_left(normed_one, grad_q),
        dot_left(normed_one, grad_k),
        dot_left(normed_one, grad_v),
        dot_left(mixed_low, grad_in[0]) + dot_left(mixed_high, grad_in[1]),
    )

    terms = jnp.stack(
        [gain_zero, gain_one, gain_two, gain_three, shift_zero, shift_one, shift_two, shift_three], 0
    )
    for axis, amount in (("ctx", size), ("wsh", groups)):
        bit = 1
        while bit < amount:
            terms = terms + swap(terms, axis, bit)
            bit *= 2
    terms = jnp.transpose(lax.dynamic_slice_in_dim(terms, row * rows, rows, 1))
    return (
        result[None],
        input_grad[None],
        enc_grad[None],
        query_grad,
        key_grad,
        value_grad,
        out_grad,
        cross_q_grad,
        cross_k_grad,
        cross_v_grad,
        cross_o_grad,
        feed_in_grad,
        feed_out_grad,
        terms[:, :4],
        terms[:, 4:],
    )


SMALL = pl.CostEstimate(flops=1 << 20, transcendentals=0, bytes_accessed=1 << 16)


def call(kernel, outs, scalars, *operands, scratch=(), aliases=None, vmem=12, space=pltpu.VMEM, out_space=pltpu.VMEM):
    specs = [pl.BlockSpec(memory_space=pltpu.SMEM)] * len(scalars)
    specs += [pl.BlockSpec(memory_space=space)] * len(operands)
    return pl.pallas_call(
        kernel,
        in_specs=specs,
        out_specs=[pl.BlockSpec(memory_space=out_space)] * len(outs),
        out_shape=[jax.ShapeDtypeStruct(shape, kind) for shape, kind in outs],
        scratch_shapes=list(scratch),
        input_output_aliases=aliases or {},
        cost_estimate=SMALL,
        compiler_params=pltpu.CompilerParams(vmem_limit_bytes=vmem << 20),
    )(*scalars, *operands)


def call_packing(kernel, outs, *operands):
    scratch = [pltpu.VMEM(operand.shape, operand.dtype) for operand in operands]
    count = len(operands)

    def fetching(*refs):
        sources, outs, held, done = refs[:count], refs[count : -count - 1], refs[-count - 1 : -1], refs[-1]
        copies = [pltpu.make_async_copy(sources[i], held[i], done.at[i]) for i in range(count)]
        for copy in copies:
            copy.start()
        for copy in copies:
            copy.wait()
        kernel(*held, *outs)

    operands = [pltpu.with_memory_space_constraint(operand, pltpu.HBM) for operand in operands]
    scratch.append(pltpu.SemaphoreType.DMA((count,)))
    return call(fetching, outs, (), *operands, scratch=scratch, space=pltpu.HBM)


def call_streaming(kernel, out, steps, *operands, vmem=20):
    shape, kind = out
    part = shape[0] // steps

    def streaming(*refs):
        *sources, out_ref, held, done = refs

        def copy(index):
            at = pl.ds(index * part, part)
            return pltpu.make_async_copy(held.at[at], out_ref.at[at], done.at[index])

        kernel(*sources, held, lambda index: copy(index).start())
        for index in range(steps):
            copy(index).wait()

    scratch = [pltpu.VMEM(shape, kind), pltpu.SemaphoreType.DMA((steps,))]
    return call(streaming, [out], (), *operands, scratch=scratch, vmem=vmem, out_space=pltpu.HBM)[0]


def one_hot(hit):
    return jnp.where(hit, 1.0, 0.0).astype(BF)


def ctx_part(size):
    return pl.ds(pl.multiple_of(lax.axis_index("ctx") * size, size), size)


def my_heads(matrix, size):
    cols = matrix.shape[1] // size
    heads = cols // HEAD
    span = HEAD * size
    source = lax.broadcasted_iota(jnp.int32, (span, cols), 0) - lax.axis_index("ctx") * HEAD
    target = lax.broadcasted_iota(jnp.int32, (span, cols), 1)
    total = None
    for head in range(heads):
        part = dot(matrix[:, head * span : (head + 1) * span], one_hot((source >= 0) & (source < HEAD) & (source == target - head * HEAD)))
        total = part if total is None else total + part
    return total.astype(BF)


def give_pieces_kernel(one, two, out_ref):
    piece = out_ref.shape[0] // 2
    start = pl.multiple_of((lax.axis_index("ctx") % 2) * 2 * piece + piece, piece)
    out_ref[:piece, :] = one[pl.ds(start, piece), :]
    out_ref[piece:, :] = two[pl.ds(start, piece), :]


def my_piece(matrix, given, which):
    piece = given.shape[0] // 2
    mine = lax.axis_index("ctx")
    start = pl.multiple_of((mine % 2) * 2 * piece, piece)
    own = matrix[pl.ds(start, piece), :].astype(F32)
    other = given[which * piece : (which + 1) * piece, :].astype(F32)
    same = lax.axis_index("wsh") % 2 == mine // 2
    return jnp.where(same, own, other).astype(BF)


def pack_kernel(wq, wk, wv, wo, given, *refs, size, which):
    *norm_refs, out_ref = refs
    rows, cols = wq.shape[0], out_ref.shape[1]
    for part, full in enumerate((wq, wk, wv)):
        out_ref[part * rows : (part + 1) * rows, :] = my_heads(full, size)
    taken = my_piece(wo, given, which)
    piece = taken.shape[0]
    for chunk in range(taken.shape[1] // cols):
        at = 3 * rows + chunk * piece
        out_ref[at : at + piece, :] = taken[:, chunk * cols : (chunk + 1) * cols]
    if norm_refs:
        gains, shifts = norm_refs
        norms = jnp.concatenate([gains[...], shifts[...]], 0).astype(F32)
        norms = jnp.concatenate([norms, jnp.zeros((8, rows), F32)], 0)
        norms = jnp.concatenate([norms, jnp.zeros((16, cols - rows), F32)], 1)
        out_ref[out_ref.shape[0] - 16 :, :] = norms.astype(BF)


def pack_feed_kernel(first, second, out_ref, groups, size):
    rows, width = first.shape[0], first.shape[1] // groups
    cols = width // size
    mine = lax.axis_index("ctx")
    for group in range(groups):
        at = pl.ds(pl.multiple_of(group * width + mine * cols, cols), cols)
        out_ref[:rows, group * cols : (group + 1) * cols] = first[:, at]
    out_ref[rows:, :] = second[ctx_part(cols), :]


def sort_kernel(order_ref, *refs, size):
    sources, (hat_ref, own_ref) = refs[:size], refs[size:]
    slots = sources[0].shape[0]
    mine = lax.axis_index("ctx")

    def block(index, carry):
        base = (mine ^ index) * slots
        total = jnp.zeros(own_ref.shape, F32)
        for source in range(size):
            order = order_ref[:, source * slots : (source + 1) * slots]
            place = base + lax.broadcasted_iota(jnp.int32, (slots, slots), 0)
            total += dot(one_hot(order == place), sources[source][...])

        @pl.when(index == 0)
        def _():
            own_ref[...] = total

        hat, unused = norm_parts(total)
        hat_ref[pl.ds(pl.multiple_of(index * slots, slots), slots), :] = hat
        return carry

    lax.fori_loop(0, size, block, 0)


def pick_kernel(order_ref, *refs, size):
    sources, out_ref = refs[:size], refs[size]
    slots = sources[0].shape[0]
    base = lax.axis_index("ctx") * slots
    total = jnp.zeros(out_ref.shape, F32)
    for source in range(size):
        order = order_ref[:, source * slots : (source + 1) * slots]
        place = base + lax.broadcasted_iota(jnp.int32, (slots, slots), 0)
        total += dot(one_hot(order == place), sources[source][...])
    out_ref[...] = total


def unsort_kernel(order_ref, *refs, size):
    sources, out_ref = refs[:size], refs[size]
    slots = sources[0].shape[0]
    mine = lax.axis_index("ctx")
    total = jnp.zeros(out_ref.shape, F32)
    for source in range(size):
        place = (mine ^ source) * slots + lax.broadcasted_iota(jnp.int32, (slots, slots), 1)
        total += dot(one_hot(order_ref[...] == place), sources[source][...])
    out_ref[...] = total


def wsh_rows(index, rows):
    target = (lax.axis_index("wsh") ^ index) * rows
    return pl.ds(pl.multiple_of(target, rows), rows)


def piece_rows(index, piece):
    target = lax.axis_index("wsh") ^ index ^ (lax.axis_index("ctx") // 2)
    return pl.ds(pl.multiple_of(target * piece, piece), piece)


def place_attention(blocks, wq, wk, wv, wo, rows, piece):
    for index, block in enumerate(blocks):
        for part, full in enumerate((wq, wk, wv)):
            full[wsh_rows(index, rows), :] = block[part * rows : (part + 1) * rows, :]
        cols = block.shape[1]
        for chunk in range(wo.shape[1] // cols):
            at = 3 * rows + chunk * piece
            wo[piece_rows(index, piece), chunk * cols : (chunk + 1) * cols] = block[at : at + piece, :]


def project_kernel(hat_ref, *refs, groups, rows, piece):
    blocks = refs[:groups]
    wq, wk, wv, wo, norms, normed_ref, q_ref, k_ref, v_ref = refs[groups:]
    place_attention(blocks, wq, wk, wv, wo, rows, piece)
    for index, block in enumerate(blocks):
        last = block.shape[0] - 16
        norms[:, wsh_rows(index, rows)] = block[last:, :rows].astype(F32)[:8]
    tile = 256

    def step(index, carry):
        at = pl.ds(pl.multiple_of(index * tile, tile), tile)
        normed = (hat_ref[at, :] * norms[0:1, :] + norms[4:5, :]).astype(BF)
        normed_ref[at, :] = normed
        for full, out in ((wq, q_ref), (wk, k_ref), (wv, v_ref)):
            out[at, :] = dot(normed, full[...]).astype(BF)
        return carry

    lax.fori_loop(0, hat_ref.shape[0] // tile, step, 0)


def cross_prepare_kernel(blocks, *refs, size, rows, piece):
    encoder = refs[:size]
    wq, wk, wv, wo, key_ref, value_ref = refs[size:]
    groups, cols = blocks.shape[0], blocks.shape[2]
    for index in range(groups):
        for part, full in enumerate((wq, wk, wv)):
            full[index * rows : (index + 1) * rows, :] = blocks[index, part * rows : (part + 1) * rows, :]
        target = (index ^ (lax.axis_index("ctx") // 2)) * piece
        there = pl.ds(pl.multiple_of(target, piece), piece)
        for chunk in range(wo.shape[1] // cols):
            at = 3 * rows + chunk * piece
            wo[there, chunk * cols : (chunk + 1) * cols] = blocks[index, at : at + piece, :]
    slots = encoder[0].shape[0]
    for index, part in enumerate(encoder):
        at = slice(index * slots, (index + 1) * slots)
        key_ref[at, :] = dot(part[...], wk[...]).astype(BF)
        value_ref[at, :] = dot(part[...], wv[...]).astype(BF)


def attend(split, low, high, first, last, flip, k_ref, v_ref, top, total, mixed, heads, chunk):
    tile = mixed.shape[1]
    top[...] = jnp.full_like(top, -1e30)
    total[...] = jnp.zeros_like(total)
    mixed[...] = jnp.zeros_like(mixed)

    def step(index, carry):
        start = pl.multiple_of((index ^ flip) * chunk, chunk)
        keys = k_ref[pl.ds(start, chunk), :]
        values = jnp.transpose(v_ref[pl.ds(start, chunk), :])
        scores = dot_right(keys, split)
        scores = jnp.where(allowed_keys(index * chunk, chunk, low, high), scores, -1e30)
        before = top[...]
        now = jnp.maximum(before, jnp.max(scores, axis=0, keepdims=True))
        decay = jnp.exp(before - now)
        weight = jnp.exp(scores - now)
        top[...] = now
        total[...] = total[...] * decay + jnp.sum(weight, axis=0, keepdims=True)
        weight = weight.astype(BF)
        for h in range(heads):
            rows, cols = slice(h * HEAD, (h + 1) * HEAD), slice(h * tile, (h + 1) * tile)
            mixed[rows, :] = mixed[rows, :] * decay[:, cols] + dot(values[rows, :], weight[:, cols])
        return carry

    lax.fori_loop(first, last, step, 0)
    amount = total[...]
    for h in range(heads):
        rows, cols = slice(h * HEAD, (h + 1) * HEAD), slice(h * tile, (h + 1) * tile)
        mixed[rows, :] = mixed[rows, :] / amount[:, cols]
    return top[...] + jnp.log(amount)


def attend_forward_kernel(meta, *refs, own_queries, parts, offset, count, chunk):
    if own_queries:
        sources, wq = refs[:parts], refs[parts]
        k_ref, v_ref, rows_ref, wo, q_ref, mixed_ref, lse_ref = refs[parts + 1 : parts + 8]
        rest = refs[parts + 8 :]
        for index, source in enumerate(sources):
            slots = source.shape[0]
            q_ref[index * slots : (index + 1) * slots, :] = dot(source[...], wq[...]).astype(BF)
        shift = 0
    else:
        q_ref, k_ref, v_ref, rows_ref, wo, mixed_ref, lse_ref = refs[:7]
        rest = refs[7:]
        shift = offset
    outs, (top, total, mixed) = rest[:parts], rest[parts:]
    tile = mixed.shape[1]
    heads = q_ref.shape[1] // HEAD

    def block(index, carry):
        at = pl.ds(pl.multiple_of((index + shift) * tile, tile), tile)
        split = split_heads(q_ref[at, :].astype(F32) * 0.125, heads, HEAD)
        low = spread(rows_ref[index + offset, 0:1, :], heads)
        high = spread(rows_ref[index + offset, 1:2, :], heads)
        first, last = meta[1 + index + offset], meta[1 + count + index + offset]
        lse_ref[index] = attend(split, low, high, first, last, meta[0], k_ref, v_ref, top, total, mixed, heads, chunk)
        here = pl.ds(pl.multiple_of(index * tile, tile), tile)
        mixed_ref[here, :] = jnp.transpose(mixed[...]).astype(BF)
        return carry

    lax.fori_loop(0, mixed_ref.shape[0] // tile, block, 0)
    for index, out in enumerate(outs):
        slots = out.shape[0]
        out[...] = dot(mixed_ref[index * slots : (index + 1) * slots, :], wo[...]).astype(BF)


def attend_backward_kernel(meta, *refs, own_queries, parts, offset, count, chunk, fresh):
    sources = refs[:parts]
    q_ref, mixed_ref, lse_ref, rows_ref, k_ref, v_ref, wo = refs[parts : parts + 7]
    rest = refs[parts + 7 :]
    if own_queries:
        wq, rest = rest[0], rest[1:]
    if not fresh:
        rest = rest[3:]
    dq_ref, dk_ref, dv_ref, dwo_ref = rest[:4]
    outs = rest[4 : 4 + parts] if own_queries else ()
    grad_ref, dq_sum = rest[-2:]
    tile = dq_sum.shape[1]
    heads = q_ref.shape[1] // HEAD
    shift = 0 if own_queries else offset
    if fresh:
        dk_ref[...] = jnp.zeros_like(dk_ref)
        dv_ref[...] = jnp.zeros_like(dv_ref)
    change = None
    for index, source in enumerate(sources):
        slots = source.shape[0]
        at = slice(index * slots, (index + 1) * slots)
        grad_ref[at, :] = dot_right(source[...], wo[...]).astype(BF)
        part = dot_left(mixed_ref[at, :], source[...])
        change = part if change is None else change + part
    dwo_ref[...] = change if fresh else dwo_ref[...] + change

    def block(index, carry):
        at = pl.ds(pl.multiple_of((index + shift) * tile, tile), tile)
        here = pl.ds(pl.multiple_of(index * tile, tile), tile)
        split = split_heads(q_ref[at, :].astype(F32) * 0.125, heads, HEAD)
        grads = split_heads(grad_ref[here, :], heads, HEAD)
        low = spread(rows_ref[index + offset, 0:1, :], heads)
        high = spread(rows_ref[index + offset, 1:2, :], heads)
        lse = lse_ref[index]
        product = jnp.transpose(grad_ref[here, :].astype(F32) * mixed_ref[here, :].astype(F32))
        inner = jnp.concatenate(
            [jnp.sum(product[h * HEAD : (h + 1) * HEAD], axis=0, keepdims=True) for h in range(heads)], 1
        )
        dq_sum[...] = jnp.zeros_like(dq_sum)

        def step(number, carry):
            start = pl.multiple_of((number ^ meta[0]) * chunk, chunk)
            keys = k_ref[pl.ds(start, chunk), :]
            scores = dot_right(keys, split)
            scores = jnp.where(allowed_keys(number * chunk, chunk, low, high), scores, -1e30)
            weight = jnp.exp(scores - lse)
            slope = dot_right(v_ref[pl.ds(start, chunk), :], grads)
            slope = (weight * (slope - inner)).astype(BF)
            dv_ref[pl.ds(start, chunk), :] += dot(weight.astype(BF), grads)
            dk_ref[pl.ds(start, chunk), :] += dot(slope, split)
            turned = jnp.transpose(keys)
            for h in range(heads):
                rows, cols = slice(h * HEAD, (h + 1) * HEAD), slice(h * tile, (h + 1) * tile)
                dq_sum[rows, :] += dot(turned[rows, :], slope[:, cols])
            return carry

        lax.fori_loop(meta[1 + index + offset], meta[1 + count + index + offset], step, 0)
        dq_ref[here, :] = (jnp.transpose(dq_sum[...]) * 0.125).astype(BF)
        return carry

    lax.fori_loop(0, dq_ref.shape[0] // tile, block, 0)
    for index, out in enumerate(outs):
        slots = out.shape[0]
        out[...] = dot_right(dq_ref[index * slots : (index + 1) * slots, :], wq[...]).astype(BF)


def total_of(base, parts):
    value = base[...]
    for part in parts:
        value = value + part[...].astype(F32)
    return value


def norm_kernel(norms, base, *refs, which):
    parts, (sum_ref, normed_ref) = refs[:-2], refs[-2:]
    value = total_of(base, parts)
    sum_ref[...] = value
    hat, unused = norm_parts(value)
    normed_ref[...] = (hat * norms[which : which + 1, :] + norms[4 + which : 5 + which, :]).astype(BF)


def norm_back_kernel(norms, value_ref, grad_ref, *refs, which):
    parts, (out_ref, sent_ref, terms_ref) = refs[:-3], refs[-3:]
    hat, rate = norm_parts(value_ref[...])
    grad = parts[0][...].astype(F32)
    for part in parts[1:]:
        grad = grad + part[...].astype(F32)
    change, gain, shift = norm_back(hat, rate, norms[which : which + 1, :], grad)
    result = grad_ref[...] + change
    out_ref[...] = result
    sent_ref[...] = result.astype(BF)
    terms_ref[0:1, :] = gain[None]
    terms_ref[1:2, :] = shift[None]


def norm_turn_kernel(norms, base, outside, *refs):
    parts, (result_ref, out_ref, sent_ref, terms_ref) = refs[:-4], refs[-4:]
    hat, rate = norm_parts(total_of(base, parts))
    result_ref[...] = (hat * norms[3:4, :] + norms[7:8, :]).astype(BF)
    change, gain, shift = norm_back(hat, rate, norms[3:4, :], outside[...])
    out_ref[...] = change
    sent_ref[...] = change.astype(BF)
    terms_ref[0:1, :] = gain[None]
    terms_ref[1:2, :] = shift[None]


def feed_halves(feed):
    groups, rows, cols = feed.shape
    rows = rows // 2
    return feed[:, :rows, :].reshape(groups * rows, cols), feed[:, rows:, :].reshape(groups * rows, cols)


def feed_forward_kernel(*refs, parts):
    sources, (feed, hidden_ref, slope_ref), outs = refs[:parts], refs[parts : parts + 3], refs[parts + 3 :]
    rate = 0.7978845608028654
    first, second = feed_halves(feed)
    for index, (source, out) in enumerate(zip(sources, outs)):
        slots = source.shape[0]
        at = slice(index * slots, (index + 1) * slots)
        pre = dot(source[...], first)
        square = pre * pre
        bend = jnp.tanh(rate * pre * (1.0 + 0.044715 * square))
        half = 0.5 * (1.0 + bend)
        slope_ref[at, :] = (half + 0.5 * pre * (1.0 - bend * bend) * rate * (1.0 + 0.134145 * square)).astype(BF)
        hidden_ref[at, :] = (pre * half).astype(BF)
        out[...] = dot(hidden_ref[at, :], second).astype(BF)


def feed_backward_kernel(*refs, parts):
    sources, (feed, slope_ref, change_ref), outs = refs[:parts], refs[parts : parts + 3], refs[parts + 3 :]
    first, second = feed_halves(feed)
    for index, (source, out) in enumerate(zip(sources, outs)):
        slots = source.shape[0]
        at = slice(index * slots, (index + 1) * slots)
        change = dot_right(source[...], second) * slope_ref[at, :].astype(F32)
        change_ref[at, :] = change.astype(BF)
        out[...] = dot_right(change_ref[at, :], first).astype(BF)


def feed_grad_kernel(*refs, size, rows):
    normed, (change_low, change_high, hidden_low, hidden_high) = refs[:size], refs[size : size + 4]
    grads, (out_ref, send) = refs[size + 4 : 2 * size + 4], refs[-2:]
    middle, slots = size // 2, normed[0].shape[0]
    wide = 2 * rows

    def step(index, carry):
        lanes = pl.ds(pl.multiple_of(index * wide, wide), wide)
        first, second = None, None
        for block in range(size):
            side, at = block // middle, (block % middle) * slots
            change = (change_low, change_high)[side][at : at + slots, :]
            hidden = (hidden_low, hidden_high)[side][at : at + slots, lanes]
            one = dot_left(normed[block][:, lanes], change)
            two = dot_left(hidden, grads[block][...])
            first, second = (one, two) if first is None else (first + one, second + two)
        for part in range(2):
            at = slice(part * rows, (part + 1) * rows)
            out_ref[2 * index + part, 0:rows, :] = first[at, :].astype(BF)
            out_ref[2 * index + part, rows : 2 * rows, :] = second[at, :].astype(BF)
        send(index)
        return carry

    lax.fori_loop(0, out_ref.shape[0] // 2, step, 0)


def weight_grad_kernel(*refs, terms, odd, rows, piece, count):
    send = None
    if odd is None:
        *refs, send = refs
    operands, extra, out_ref = refs[:-2], refs[-2], refs[-1]
    height = out_ref.shape[0] // count
    cols = out_ref.shape[1]
    mine = lax.axis_index("wsh")

    def step(index, carry):
        relative = index ^ mine if odd is None else 2 * index + odd
        target = mine ^ relative
        lanes = pl.ds(pl.multiple_of(target * rows, rows), rows)
        for part in range(3):
            value = None
            for which, left, left_at, right, right_at, length in terms:
                if which == part:
                    one = dot_left(
                        operands[left][left_at : left_at + length, lanes],
                        operands[right][right_at : right_at + length, :].astype(BF),
                    )
                    value = one if value is None else value + one
            at = pl.ds(pl.multiple_of(index * height + part * rows, rows), rows)
            out_ref[at, :] = value.astype(out_ref.dtype)
        taken = piece_rows(relative, piece)
        for chunk in range(extra.shape[1] // cols):
            at = pl.ds(pl.multiple_of(index * height + 3 * rows + chunk * piece, piece), piece)
            out_ref[at, :] = extra[taken, chunk * cols : (chunk + 1) * cols].astype(out_ref.dtype)
        if send is not None:
            send(index)
        return carry

    lax.fori_loop(0, count, step, 0)


def sum_kernel(even, odd, terms, other_terms, *outs, rows, height):
    total = terms[...] + other_terms[...]
    for index, out in enumerate(outs):
        at = slice(index * height, (index + 1) * height)
        out[:height, :] = (even[at, :] + odd[at, :].astype(F32)).astype(out.dtype)
        lanes = (lax.axis_index("wsh") ^ (2 * index)) * rows
        taken = jnp.zeros((8, rows), F32)
        for block in range(total.shape[1] // rows):
            taken = jnp.where(lanes == block * rows, total[:, block * rows : (block + 1) * rows], taken)
        taken = jnp.concatenate([taken, jnp.zeros((8, rows), F32)], 0)
        taken = jnp.concatenate([taken, jnp.zeros((16, out.shape[1] - rows), F32)], 1)
        out[height:, :] = taken.astype(out.dtype)


def back_project_kernel(dq_ref, dk_ref, dv_ref, wq, wk, wv, *outs, first):
    for index, out in enumerate(outs):
        slots = out.shape[0]
        at = slice(index * slots, (index + 1) * slots)
        there = slice(first + index * slots, first + (index + 1) * slots)
        value = dot_right(dq_ref[at, :], wq[...])
        value += dot_right(dk_ref[there, :].astype(BF), wk[...])
        value += dot_right(dv_ref[there, :].astype(BF), wv[...])
        out[...] = value.astype(BF)


def encoder_grad_kernel(dk_ref, dv_ref, wk, wv, *outs):
    for index, out in enumerate(outs):
        slots = out.shape[0]
        at = slice(index * slots, (index + 1) * slots)
        value = dot_right(dk_ref[at, :].astype(BF), wk[...]) + dot_right(dv_ref[at, :].astype(BF), wv[...])
        out[...] = value.astype(BF)


def place_square_kernel(*refs, count, rows, piece):
    mine = lax.axis_index("ctx")
    threes, (near, other), outs = refs[:count], refs[count : count + 2], refs[count + 2 :]
    cols = threes[0].shape[1]
    if len(outs) > 4:
        last = [three[3 * rows :, :rows].astype(F32) for three in threes]
        outs[4][...] = sum(last)
    span = HEAD * count
    blocks = [three[...].astype(F32) for three in threes]
    for group in range(count):
        wanted = mine ^ group
        chosen = blocks[0]
        for index in range(1, count):
            chosen = jnp.where(wanted == index, blocks[index], chosen)
        for part in range(3):
            for head in range(cols // HEAD):
                at = head * span + group * HEAD
                outs[part][:, at : at + HEAD] = chosen[
                    part * rows : (part + 1) * rows, head * HEAD : (head + 1) * HEAD
                ]
    core = mine % 2
    for source, place in ((near, core), (other, 1 - core)):
        for half in range(2):
            row = pl.ds(pl.multiple_of((2 * place + half) * piece, piece), piece)
            for chunk in range(outs[3].shape[1] // cols):
                at = (half * (outs[3].shape[1] // cols) + chunk) * piece
                outs[3][row, chunk * cols : (chunk + 1) * cols] = source[at : at + piece, :].astype(F32)


def place_feed_kernel(*refs, count, groups, rows, cols):
    mine = lax.axis_index("ctx")
    first, second = refs[count:]
    for index in range(count):
        target = mine ^ index
        for group in range(groups):
            column = pl.ds(pl.multiple_of(group * count * cols + target * cols, cols), cols)
            first[:, column] = refs[index][:rows, group * cols : (group + 1) * cols].astype(F32)
        row = pl.ds(pl.multiple_of(target * cols, cols), cols)
        second[row, :] = refs[index][rows:, :].astype(F32)


def fold(near, sent):
    arrived = swap(sent, "ctx", 1)
    return near, arrived


def after(value, *others):
    return lax.optimization_barrier((value,) + others)[0]


def far_hop(parts):
    arrived = swap(parts[1], "ctx", 1)
    sent = (parts[0].astype(F32) + arrived.astype(F32)).astype(BF)
    return sent, swap(sent, "ctx", 2)


def spread_ctx(own):
    far = swap(own, "ctx", 2)
    near = swap(own, "ctx", 1)
    return [own, near, far, swap(far, "ctx", 1)]


def start_ctx(own):
    return [own, swap(own, "ctx", 1), swap(own, "ctx", 2)]


def finish_ctx(blocks, *before):
    far = after(blocks[2], *before)
    return blocks[:2] + [far, swap(far, "ctx", 1)]


def send_z(own):
    size = lax.axis_size("wsh")
    blocks = {0: own, 1: swap(own, "wsh", 1)}
    for bit in range(2, size, 2):
        blocks[bit] = swap(own, "wsh", bit)
    return blocks


def pass_y(blocks):
    size = lax.axis_size("wsh")
    for bit in range(2, size, 2):
        blocks[bit + 1] = swap(blocks[bit], "wsh", 1)
    return [blocks[bit] for bit in range(size)]


class Ranges:
    def __init__(self, low, high, tile, chunk, flip):
        self.tile, self.chunk, self.count = tile, chunk, low.shape[0] // tile
        low, high = low.reshape(self.count, tile), high.reshape(self.count, tile)
        self.rows = jnp.stack([low, high], 1)
        first, last = jnp.min(low, 1) // chunk, (jnp.max(high, 1) - 1) // chunk + 1
        self.meta = jnp.concatenate([flip.reshape(1), first, last]).astype(jnp.int32)


def fast_body(
    inputs,
    enc_states,
    cotangent,
    slot_order,
    seq_lengths,
    enc_lengths,
    self_query,
    self_key,
    self_value,
    self_out,
    cross_query,
    cross_key,
    cross_value,
    cross_out,
    feed_in,
    feed_out,
    norm_gains,
    norm_shifts,
):
    size, groups = lax.axis_size("ctx"), lax.axis_size("wsh")
    mine, row = lax.axis_index("ctx"), lax.axis_index("wsh")
    slots = inputs.shape[1]
    total = slots * size
    enc_slots = enc_states.shape[1]
    width = inputs.shape[2]
    rows = self_query.shape[0]
    cols = width // size
    piece = rows // size
    ff_cols = feed_in.shape[1] // size
    ff_rows = feed_out.shape[0] // size
    heads = cols // HEAD
    middle = total // 2
    part = size // 2
    block_bf, block_f = ((slots, width), BF), ((slots, width), F32)
    terms_f = ((2, width), F32)

    given = call_packing(give_pieces_kernel, [((2 * piece, width), BF)], self_out, cross_out)[0]
    given = swap(given, "wsh", 1)
    height = 3 * rows + piece * (width // cols)
    self_block = call_packing(
        functools.partial(pack_kernel, size=size, which=0),
        [((height + 16, cols), BF)],
        self_query,
        self_key,
        self_value,
        self_out,
        given,
        jnp.transpose(norm_gains),
        jnp.transpose(norm_shifts),
    )[0]
    self_blocks = send_z(self_block)
    token_blocks = start_ctx(inputs[0])
    self_blocks = pass_y(self_blocks)
    token_blocks = finish_ctx(token_blocks)
    cross_block = call_packing(
        functools.partial(pack_kernel, size=size, which=1),
        [((height, cols), BF)],
        after(cross_query, self_block),
        cross_key,
        cross_value,
        cross_out,
        given,
    )[0]
    packed = cross_block
    cross_block = gather_wsh(cross_block).reshape(groups, height, cols)
    feed = call_packing(
        functools.partial(pack_feed_kernel, groups=groups, size=size),
        [((2 * rows, ff_cols), BF)],
        after(feed_in, self_block),
        feed_out,
    )[0]
    feed = gather_wsh(after(feed, packed, self_blocks[2])).reshape(groups, 2 * rows, ff_cols)

    relative = jnp.arange(size, dtype=jnp.int32) ^ mine
    order = jnp.take(slot_order[0].reshape(size, slots), relative, axis=0).reshape(1, total)
    own_order = lax.dynamic_slice_in_dim(slot_order[0], mine * slots, slots).reshape(slots, 1)
    place = (relative[:, None] * slots + jnp.arange(slots, dtype=jnp.int32)).reshape(total)
    lower = jnp.arange(seq_lengths.shape[1])
    lower = lower[None, :] <= lower[:, None]
    ends = jnp.sum(jnp.where(lower, seq_lengths[0][None, :], 0), 1)
    enc_ends = jnp.sum(jnp.where(lower, enc_lengths[0][None, :], 0), 1)
    passed = ends[None, :] <= place[:, None]
    starts = jnp.max(jnp.where(passed, ends[None, :], 0), 1)
    enc_from = jnp.max(jnp.where(passed, enc_ends[None, :], 0), 1)
    enc_to = jnp.min(jnp.where(passed, enc_slots * size, enc_ends[None, :]), 1)
    self_range = Ranges(starts, place + 1, 256, 256, mine * (slots // 256))
    cross_range = Ranges(enc_from, enc_to, 256, 128, mine * (enc_slots // 128))
    half = total // 512

    def unsort(blocks):
        return call(functools.partial(unsort_kernel, size=size), [block_f], (), own_order, *blocks)[0]

    hat_all, tokens = call(
        functools.partial(sort_kernel, size=size), [((total, width), F32), block_f], (), order, *token_blocks
    )

    square, tall = ((width, cols), BF), ((total, cols), BF)
    wq, wk, wv, wo, norms, normed_one, queries, keys, values = call(
        functools.partial(project_kernel, groups=groups, rows=rows, piece=piece),
        [square] * 3 + [((cols, width), BF), ((8, width), F32), ((total, width), BF)] + [tall] * 3,
        (),
        hat_all,
        *self_blocks,
    )
    lanes = heads * 256
    half_outs = [((middle, cols), BF), ((half, 1, lanes), F32)] + [block_bf] * part
    scratch = [pltpu.VMEM((1, lanes), F32), pltpu.VMEM((1, lanes), F32), pltpu.VMEM((cols, 256), F32)]

    def self_forward(side, queries):
        body = functools.partial(
            attend_forward_kernel,
            own_queries=False,
            parts=part,
            offset=side * half,
            count=self_range.count,
            chunk=self_range.chunk,
        )
        return call(
            body, half_outs, (self_range.meta,), queries, keys, values, self_range.rows, wo, scratch=scratch
        )

    encoder = spread_ctx(after(enc_states[0], normed_one))
    mixed_high, lse_high, *far = self_forward(1, queries)
    sent, arrived = far_hop(far)
    mixed_low, lse_low, *near = self_forward(0, after(queries, sent))

    def normalize(base, near, arrived, which):
        return call(
            functools.partial(norm_kernel, which=which),
            [block_f, block_bf],
            (),
            norms,
            base,
            near[0],
            swap(near[1], "ctx", 1),
            arrived,
        )

    after_self, normed = normalize(tokens, near, arrived, 1)
    outside = spread_ctx(after(cotangent[0], arrived))
    outside = call(functools.partial(pick_kernel, size=size), [block_f], (), order, *outside)[0]

    normed_two = start_ctx(normed)
    cq, ck, cv, co, enc_keys, enc_values = call(
        functools.partial(cross_prepare_kernel, size=size, rows=rows, piece=piece),
        [square] * 3 + [((cols, width), BF)] + [((enc_slots * size, cols), BF)] * 2,
        (),
        cross_block,
        *encoder,
    )

    def cross_forward(side):
        body = functools.partial(
            attend_forward_kernel,
            own_queries=True,
            parts=part,
            offset=side * half,
            count=cross_range.count,
            chunk=cross_range.chunk,
        )
        return call(
            body,
            [((middle, cols), BF)] + half_outs,
            (cross_range.meta,),
            *normed_two[side * part : (side + 1) * part],
            cq,
            enc_keys,
            enc_values,
            cross_range.rows,
            co,
            scratch=scratch,
        )

    cross_low = cross_forward(0)
    normed_two = finish_ctx(normed_two, cross_low[3])
    cross_high = cross_forward(1)
    sent, arrived = far_hop(cross_high[3:])
    after_cross, normed = normalize(after_self, cross_low[3:], arrived, 2)

    normed_three = start_ctx(normed)
    def feed_forward(side):
        return call(
            functools.partial(feed_forward_kernel, parts=part),
            [((middle, ff_cols), BF)] * 2 + [block_bf] * part,
            (),
            *normed_three[side * part : (side + 1) * part],
            feed,
        )

    hidden_low, slope_low, *near = feed_forward(0)
    normed_three = finish_ctx(normed_three, near[0])
    hidden_high, slope_high, *far = feed_forward(1)
    sent, arrived = far_hop(far)
    result, grad_ffn, grad, terms_three = call(
        norm_turn_kernel,
        [block_bf, block_f, block_bf, terms_f],
        (),
        norms,
        after_cross,
        outside,
        near[0],
        swap(near[1], "ctx", 1),
        arrived,
    )

    def denormalize(value, grad, near, arrived, which):
        return call(
            functools.partial(norm_back_kernel, which=which),
            [block_f, block_bf, terms_f],
            (),
            norms,
            value,
            grad,
            near[0],
            swap(near[1], "ctx", 1),
            arrived,
        )

    grad_in = start_ctx(grad)

    def feed_backward(side, slope):
        return call(
            functools.partial(feed_backward_kernel, parts=part),
            [((middle, ff_cols), BF)] + [block_bf] * part,
            (),
            *grad_in[side * part : (side + 1) * part],
            feed,
            slope,
        )

    change_low, *near = feed_backward(0, slope_low)
    grad_in = finish_ctx(grad_in, near[0])
    change_high, *far = feed_backward(1, slope_high)
    sent, arrived = far_hop(far)
    feed_grads = call_streaming(
        functools.partial(feed_grad_kernel, size=size, rows=rows),
        ((groups, 2 * rows, width), BF),
        groups // 2,
        *normed_three,
        change_low,
        after(change_high, sent),
        hidden_low,
        hidden_high,
        *grad_in,
    )
    grad_cross, grad, terms_two = denormalize(after_cross, grad_ffn, near, after(arrived, feed_grads), 2)
    feed_grads = scatter_wsh(after(feed_grads, arrived).reshape(groups * 2 * rows, width))

    def weight_grads(terms, operands, out_grad, odd):
        height = 3 * rows + piece * (width // cols)
        count = groups if odd is None else groups // 2
        body = functools.partial(weight_grad_kernel, terms=terms, odd=odd, rows=rows, piece=piece, count=count)
        outs = [((count * height, cols), F32 if odd == 0 else BF)]
        if odd is None:
            return call_streaming(body, outs[0], count, *operands, out_grad)
        return call(body, outs, (), *operands, out_grad)[0]

    def backward(span, side, own_queries, sources, queries, mixed, lse, keys, values, wo, wq, before):
        body = functools.partial(
            attend_backward_kernel,
            own_queries=own_queries,
            parts=part,
            offset=side * half,
            count=span.count,
            chunk=span.chunk,
            fresh=before is None,
        )
        operands = [*sources, queries, mixed, lse, span.rows, keys, values, wo]
        if own_queries:
            operands.append(wq)
        aliases = {}
        if before is not None:
            aliases = {1 + len(operands) + i: 1 + i for i in range(3)}
            operands += before
        outs = [((middle, cols), BF), (keys.shape, F32), (keys.shape, F32), ((cols, width), F32)]
        if own_queries:
            outs += [block_bf] * part
        return call(
            body,
            outs,
            (span.meta,),
            *operands,
            scratch=[pltpu.VMEM((middle, cols), BF), pltpu.VMEM((cols, 256), F32)],
            aliases=aliases,
        )

    grad_in = start_ctx(grad)
    low = backward(
        cross_range, 0, True, grad_in[:part], *cross_low[:3], enc_keys, enc_values, co, cq, None
    )
    grad_in = finish_ctx(grad_in, low[4])
    high = backward(
        cross_range, 1, True, grad_in[part:], *cross_high[:3], enc_keys, enc_values, co, cq, list(low[1:4])
    )
    sent, arrived = far_hop(high[4:])
    dk, dv, dwo = high[1:4]
    operands = [*normed_two, low[0], high[0], *encoder, dk, dv]
    terms = []
    for index in range(size):
        side = index // part
        terms.append((0, index, 0, size + side, (index % part) * slots, slots))
    for index in range(size):
        for which in (1, 2):
            terms.append((which, size + 2 + index, 0, 2 * size + 1 + which, index * enc_slots, enc_slots))
    dk = after(dk, sent)
    operands[-2] = dk
    cross_share_local = weight_grads(tuple(terms), operands, dwo, None)
    enc_parts = call(encoder_grad_kernel, [((enc_slots, width), BF)] * size, (), dk, dv, ck, cv)
    cross_share = scatter_wsh(after(cross_share_local, arrived))
    arrived = after(arrived, cross_share_local, *enc_parts)
    grad_self, grad, terms_one = denormalize(after_self, grad_cross, low[4:], arrived, 1)

    grad_in = start_ctx(grad)
    low = backward(
        self_range, 0, False, grad_in[:part], queries, mixed_low, lse_low, keys, values, wo, None, None
    )
    grad_in = finish_ctx(grad_in, low[0])
    result = start_ctx(after(result, grad_in[2]))
    enc_sent, enc_far = far_hop([after(enc_parts[2], grad_in[2]), enc_parts[3]])
    enc_near = swap(enc_parts[1], "ctx", 1)
    enc_grad = enc_parts[0].astype(F32) + enc_near.astype(F32) + enc_far.astype(F32)
    high = backward(
        self_range, 1, False, grad_in[part:], queries, mixed_high, lse_high, keys, values, wo, None, list(low[1:4])
    )
    dk, dv, dwo = high[1:4]

    def back_project(side, dq):
        body = functools.partial(back_project_kernel, first=side * middle)
        return call(body, [block_bf] * part, (), dq, dk, dv, wq, wk, wv)

    far = back_project(1, high[0])
    operands = [normed_one, low[0], high[0], after(dk, result[2]), dv]
    terms = ((0, 0, 0, 1, 0, middle), (0, 0, middle, 2, 0, middle), (1, 0, 0, 3, 0, total), (2, 0, 0, 4, 0, total))
    odd = weight_grads(terms, operands, dwo, 1)
    sent, arrived = far_hop(far)
    self_odd = swap(odd, "wsh", 1)
    near = back_project(0, after(low[0], sent, odd))
    self_even = weight_grads(terms, operands, after(dwo, *near), 0)

    feed_blocks = start_ctx(after(feed_grads, sent))
    unused, grad, terms_zero = denormalize(tokens, grad_self, near, after(arrived, self_even), 0)
    input_grad = start_ctx(grad)

    def finish(result, extra=0):
        fourth = result[3 * rows : height]
        pair = jnp.concatenate([fourth, swap(fourth, "wsh", 1)], 0)
        pair = jnp.where(row % 2 == mine // 2, pair, swap(pair, "ctx", 2))
        three = result[: 3 * rows]
        outs = [((rows, width), F32)] * 4
        if extra:
            three = jnp.concatenate([three, result[height:]], 0)
            outs.append(((extra, rows), F32))
        return call(
            functools.partial(place_square_kernel, count=size, rows=rows, piece=piece),
            outs,
            (),
            *spread_ctx(three),
            pair,
            swap(pair, "ctx", 1),
        )

    terms = jnp.concatenate([terms_zero, terms_one, terms_two, terms_three], 0)
    tall = (height + 16, cols)
    share, *sent = call(
        functools.partial(sum_kernel, rows=rows, height=height),
        [(tall, F32)] + [(tall, BF)] * (groups // 2 - 1),
        (),
        after(self_even, feed_blocks[2], input_grad[2]),
        after(self_odd, grad),
        terms,
        swap(terms, "wsh", 1),
    )
    parts = [swap(value, "wsh", 2 * index + 2) for index, value in enumerate(sent)]
    feed_in_grad, feed_out_grad = call(
        functools.partial(place_feed_kernel, count=size, groups=groups, rows=rows, cols=ff_rows),
        [((rows, groups * size * ff_rows), F32), ((size * ff_rows, width), F32)],
        (),
        *finish_ctx(feed_blocks, sent[0]),
    )
    result = unsort(finish_ctx(result, sent[0]))
    input_grad = unsort(finish_ctx(input_grad, sent[0]))
    parts = after(tuple(parts), result, input_grad, feed_in_grad)
    for part in parts:
        share = share + part.astype(F32)
    share = share.astype(BF)
    *self_grads, terms = finish(share, 16)
    terms = jnp.transpose(terms[:8])
    cross_grads = finish(after(cross_share, share))
    return (
        result[None],
        input_grad[None],
        enc_grad[None],
        *self_grads,
        *cross_grads,
        feed_in_grad,
        feed_out_grad,
        terms[:, 0::2],
        terms[:, 1::2],
    )


def solution(mesh):
    token, weight = P("wsh", "ctx", None), P("wsh", None)
    in_specs = (token,) * 3 + (weight,) * 15
    out_specs = (token,) * 3 + (weight,) * 12
    body = fast_body if mesh.shape["ctx"] == 4 else plain_body
    return jax.shard_map(body, mesh=mesh, in_specs=in_specs, out_specs=out_specs, check_vma=False)
```

```python
import functools

import jax
import jax.numpy as jnp
from jax import lax
from jax.experimental import pallas as pl
from jax.experimental.pallas import tpu as pltpu
from jax.sharding import PartitionSpec as P

HEAD = 64
BF = jnp.bfloat16
F32 = jnp.float32


def dot(left, right):
    return jnp.dot(left, right, preferred_element_type=F32)


def dot_left(left, right):
    return lax.dot_general(left, right, (((0,), (0,)), ((), ())), preferred_element_type=F32)


def dot_right(left, right):
    return lax.dot_general(left, right, (((1,), (1,)), ((), ())), preferred_element_type=F32)


def swap(value, axis, bit):
    size = lax.axis_size(axis)
    return lax.ppermute(value, axis, [(i, i ^ bit) for i in range(size)])


def gather_ctx(own):
    size = lax.axis_size("ctx")
    blocks = {0: own}
    bit = size // 2
    while bit:
        for index in sorted(blocks):
            blocks[index | bit] = swap(blocks[index], "ctx", bit)
        bit //= 2
    return [blocks[index] for index in range(size)]


def scatter_ctx(blocks):
    blocks = dict(enumerate(blocks))
    size, bit = len(blocks), 1
    while bit < size:
        for index in sorted(blocks, reverse=True):
            if index & bit:
                arrived = swap(blocks.pop(index).astype(BF), "ctx", bit)
                blocks[index ^ bit] = blocks[index ^ bit] + arrived.astype(F32)
        bit *= 2
    return blocks[0]


def halves(blocks):
    middle = len(blocks) // 2
    return (jnp.concatenate(blocks[:middle], 0), jnp.concatenate(blocks[middle:], 0))


def scatter_halves(low, high, rows):
    count = low.shape[0] // rows
    cut = [low[i * rows : (i + 1) * rows] for i in range(count)]
    return scatter_ctx(cut + [high[i * rows : (i + 1) * rows] for i in range(count)])


def norm_parts(values):
    center = values - jnp.mean(values, axis=-1, keepdims=True)
    rate = lax.rsqrt(jnp.mean(center * center, axis=-1, keepdims=True) + 1e-05)
    return center * rate, rate


def norm_back(hat, rate, gain, grad):
    scaled = grad * gain
    inner = jnp.mean(scaled * hat, axis=-1, keepdims=True)
    result = rate * (scaled - jnp.mean(scaled, axis=-1, keepdims=True) - hat * inner)
    return result, jnp.sum(grad * hat, axis=0), jnp.sum(grad, axis=0)


def gelu_back(values, grad):
    unused, pullback = jax.vjp(lambda u: jax.nn.gelu(u, approximate=True), values)
    return pullback(grad)[0]


def split_heads(block, heads, head):
    wide = block.astype(F32)
    lane = lax.broadcasted_iota(jnp.int32, wide.shape, 1) // head
    parts = [jnp.where(lane == h, wide, 0.0).astype(BF) for h in range(heads)]
    return jnp.concatenate(parts, 0)


def spread(row, heads):
    return jnp.concatenate([row] * heads, 1)


def allowed_keys(first, chunk, low, high):
    index = first + lax.broadcasted_iota(jnp.int32, (chunk, low.shape[1]), 0)
    return (index >= low) & (index < high)


def forward_kernel(meta, q_ref, k_ref, v_ref, rows_ref, o_ref, lse_ref, top, total, mixed, *, heads, head, chunk, count, offset):
    block = pl.program_id(0) + offset
    queries = q_ref.shape[0]
    split = split_heads(q_ref[...].astype(F32) * 0.125, heads, head)
    low = spread(rows_ref[0, 0:1, :], heads)
    high = spread(rows_ref[0, 1:2, :], heads)
    top[...] = jnp.full_like(top, -1e30)
    total[...] = jnp.zeros_like(total)
    mixed[...] = jnp.zeros_like(mixed)

    def step(index, carry):
        start = pl.multiple_of((index ^ meta[0]) * chunk, chunk)
        keys = k_ref[pl.ds(start, chunk), :]
        values = jnp.transpose(v_ref[pl.ds(start, chunk), :])
        scores = dot_right(keys, split)
        scores = jnp.where(allowed_keys(index * chunk, chunk, low, high), scores, -1e30)
        before = top[...]
        now = jnp.maximum(before, jnp.max(scores, axis=0, keepdims=True))
        decay = jnp.exp(before - now)
        weight = jnp.exp(scores - now)
        top[...] = now
        total[...] = total[...] * decay + jnp.sum(weight, axis=0, keepdims=True)
        weight = weight.astype(BF)
        for h in range(heads):
            rows, cols = slice(h * head, (h + 1) * head), slice(h * queries, (h + 1) * queries)
            mixed[rows, :] = mixed[rows, :] * decay[:, cols] + dot(values[rows, :], weight[:, cols])
        return carry

    lax.fori_loop(meta[1 + block], meta[1 + count + block], step, 0)
    amount = total[...]
    for h in range(heads):
        rows, cols = slice(h * head, (h + 1) * head), slice(h * queries, (h + 1) * queries)
        mixed[rows, :] = mixed[rows, :] / amount[:, cols]
    o_ref[...] = jnp.transpose(mixed[...]).astype(BF)
    lse_ref[0] = top[...] + jnp.log(amount)


def backward_kernel(meta, q_ref, g_ref, o_ref, lse_ref, rows_ref, k_ref, v_ref, dq_ref, dk_ref, dv_ref, dq_sum, *, heads, head, chunk, count, offset):
    block = pl.program_id(0) + offset
    queries = q_ref.shape[0]

    @pl.when(pl.program_id(0) == 0)
    def _():
        dk_ref[...] = jnp.zeros_like(dk_ref)
        dv_ref[...] = jnp.zeros_like(dv_ref)

    split = split_heads(q_ref[...].astype(F32) * 0.125, heads, head)
    grads = split_heads(g_ref[...], heads, head)
    low = spread(rows_ref[0, 0:1, :], heads)
    high = spread(rows_ref[0, 1:2, :], heads)
    lse = lse_ref[0]
    product = jnp.transpose(g_ref[...].astype(F32) * o_ref[...].astype(F32))
    inner = jnp.concatenate(
        [jnp.sum(product[h * head : (h + 1) * head], axis=0, keepdims=True) for h in range(heads)], 1
    )
    dq_sum[...] = jnp.zeros_like(dq_sum)

    def step(index, carry):
        start = pl.multiple_of((index ^ meta[0]) * chunk, chunk)
        keys = k_ref[pl.ds(start, chunk), :]
        scores = dot_right(keys, split)
        scores = jnp.where(allowed_keys(index * chunk, chunk, low, high), scores, -1e30)
        weight = jnp.exp(scores - lse)
        slope = dot_right(v_ref[pl.ds(start, chunk), :], grads)
        slope = (weight * (slope - inner)).astype(BF)
        dv_ref[pl.ds(start, chunk), :] += dot(weight.astype(BF), grads)
        dk_ref[pl.ds(start, chunk), :] += dot(slope, split)
        turned = jnp.transpose(keys)
        for h in range(heads):
            rows, cols = slice(h * head, (h + 1) * head), slice(h * queries, (h + 1) * queries)
            dq_sum[rows, :] += dot(turned[rows, :], slope[:, cols])
        return carry

    lax.fori_loop(meta[1 + block], meta[1 + count + block], step, 0)
    dq_ref[...] = (jnp.transpose(dq_sum[...]) * 0.125).astype(BF)


class Attention:
    def __init__(self, low, high, tile, chunk, flip):
        self.tile, self.chunk = tile, chunk
        self.count = low.shape[0] // tile
        low, high = low.reshape(self.count, tile), high.reshape(self.count, tile)
        self.rows = jnp.stack([low, high], 1)
        first, last = jnp.min(low, 1) // chunk, (jnp.max(high, 1) - 1) // chunk + 1
        self.meta = jnp.concatenate([flip.reshape(1), first, last]).astype(jnp.int32)

    def specs(self, width, heads, offset, queries_at):
        tile = self.tile
        tall = pl.BlockSpec((tile, width), lambda i, m: (i + queries_at, 0))
        rows = pl.BlockSpec((1, 2, tile), lambda i, m: (i + offset, 0, 0))
        return tall, rows

    def forward(self, queries, keys, values, offset, steps, queries_at):
        width, heads = queries.shape[1], queries.shape[1] // HEAD
        tall, rows = self.specs(width, heads, offset, queries_at)
        whole = pl.BlockSpec(keys.shape, lambda i, m: (0, 0))
        lanes = heads * self.tile
        body = functools.partial(
            forward_kernel, heads=heads, head=HEAD, chunk=self.chunk, count=self.count, offset=offset
        )
        pairs = steps * self.tile * keys.shape[0] * heads
        return pl.pallas_call(
            body,
            grid_spec=pltpu.PrefetchScalarGridSpec(
                num_scalar_prefetch=1,
                grid=(steps,),
                in_specs=[tall, whole, whole, rows],
                out_specs=[
                    pl.BlockSpec((self.tile, width), lambda i, m: (i, 0)),
                    pl.BlockSpec((1, 1, lanes), lambda i, m: (i, 0, 0)),
                ],
                scratch_shapes=[
                    pltpu.VMEM((1, lanes), F32),
                    pltpu.VMEM((1, lanes), F32),
                    pltpu.VMEM((width, self.tile), F32),
                ],
            ),
            out_shape=[
                jax.ShapeDtypeStruct((steps * self.tile, width), BF),
                jax.ShapeDtypeStruct((steps, 1, lanes), F32),
            ],
            cost_estimate=pl.CostEstimate(flops=pairs * 256, transcendentals=pairs // 2, bytes_accessed=2 << 20),
            compiler_params=pltpu.CompilerParams(vmem_limit_bytes=24 << 20),
        )(self.meta, queries, keys, values, self.rows)

    def backward(self, queries, grads, mixed, lse, keys, values, offset, steps, queries_at):
        width, heads = queries.shape[1], queries.shape[1] // HEAD
        tall, rows = self.specs(width, heads, offset, queries_at)
        near = pl.BlockSpec((self.tile, width), lambda i, m: (i, 0))
        whole = pl.BlockSpec(keys.shape, lambda i, m: (0, 0))
        lanes = heads * self.tile
        body = functools.partial(
            backward_kernel, heads=heads, head=HEAD, chunk=self.chunk, count=self.count, offset=offset
        )
        pairs = steps * self.tile * keys.shape[0] * heads
        return pl.pallas_call(
            body,
            grid_spec=pltpu.PrefetchScalarGridSpec(
                num_scalar_prefetch=1,
                grid=(steps,),
                in_specs=[tall, near, near, pl.BlockSpec((1, 1, lanes), lambda i, m: (i, 0, 0)), rows, whole, whole],
                out_specs=[near, whole, whole],
                scratch_shapes=[pltpu.VMEM((width, self.tile), F32)],
            ),
            out_shape=[
                jax.ShapeDtypeStruct((steps * self.tile, width), BF),
                jax.ShapeDtypeStruct(keys.shape, F32),
                jax.ShapeDtypeStruct(keys.shape, F32),
            ],
            cost_estimate=pl.CostEstimate(flops=pairs * 640, transcendentals=pairs // 2, bytes_accessed=4 << 20),
            compiler_params=pltpu.CompilerParams(vmem_limit_bytes=32 << 20),
        )(self.meta, queries, grads, mixed, lse, self.rows, keys, values)


def gather_wsh(part):
    return lax.all_gather(part, "wsh", axis=0, tiled=True)


def scatter_wsh(whole):
    return lax.psum_scatter(whole.astype(BF), "wsh", scatter_dimension=0, tiled=True)


def piece_moves(groups, size):
    return [((g % size) * groups + g // size, g) for g in range(groups * size)]


def plain_body(
    inputs,
    enc_states,
    cotangent,
    slot_order,
    seq_lengths,
    enc_lengths,
    self_query,
    self_key,
    self_value,
    self_out,
    cross_query,
    cross_key,
    cross_value,
    cross_out,
    feed_in,
    feed_out,
    norm_gains,
    norm_shifts,
):
    size, groups = lax.axis_size("ctx"), lax.axis_size("wsh")
    mine, row = lax.axis_index("ctx"), lax.axis_index("wsh")
    slots = inputs.shape[1]
    total = slots * size
    enc_slots = enc_states.shape[1]
    width = inputs.shape[2]
    rows = self_query.shape[0]
    cols = width // size
    piece = rows // size
    ff_cols = feed_in.shape[1] // size
    ff_rows = feed_out.shape[0] // size

    def columns(matrix):
        return lax.dynamic_slice_in_dim(matrix, mine * cols, cols, 1)

    norms = jnp.concatenate([norm_gains, norm_shifts, jnp.zeros((rows, 120), BF)], 1)
    self_full = gather_wsh(jnp.concatenate([columns(self_query), columns(self_key), columns(self_value), norms], 1))
    q_full, k_full, v_full = (self_full[:, i * cols : (i + 1) * cols] for i in range(3))
    norm_rows = jnp.transpose(self_full[:, 3 * cols : 3 * cols + 8].astype(F32))
    gains, shifts = norm_rows[:4, None, :], norm_rows[4:, None, :]

    def out_piece(matrix):
        return lax.dynamic_slice_in_dim(matrix, mine * piece, piece, 0)

    pieces = jnp.concatenate([out_piece(self_out), out_piece(cross_out)], 0)
    pieces = lax.ppermute(pieces, ("ctx", "wsh"), piece_moves(groups, size))
    pieces = gather_wsh(pieces).reshape(groups, 2, piece, width)
    out_full, cross_o_full = pieces[:, 0].reshape(cols, width), pieces[:, 1].reshape(cols, width)
    cross_full = gather_wsh(jnp.concatenate([columns(cross_query), columns(cross_key), columns(cross_value)], 1))
    cq_full, ck_full, cv_full = (cross_full[:, i * cols : (i + 1) * cols] for i in range(3))
    first_part = lax.dynamic_slice_in_dim(feed_in.reshape(rows, groups, size, ff_rows), mine, 1, 2)
    second_part = lax.dynamic_slice_in_dim(feed_out, mine * ff_rows, ff_rows, 0)
    feed = jnp.concatenate([first_part.reshape(rows, ff_cols), second_part.reshape(rows, ff_cols)], 0)
    feed = gather_wsh(feed).reshape(groups, 2, rows, ff_cols)
    first_full = feed[:, 0].reshape(groups * rows, ff_cols)
    second_full = feed[:, 1].reshape(groups * ff_rows, width)

    relative = jnp.arange(size, dtype=jnp.int32) ^ mine
    order = jnp.take(slot_order[0].reshape(size, slots), relative, axis=0).reshape(total)
    place = (relative[:, None] * slots + jnp.arange(slots, dtype=jnp.int32)).reshape(total)
    lower = jnp.arange(seq_lengths.shape[1])
    lower = lower[None, :] <= lower[:, None]
    ends = jnp.sum(jnp.where(lower, seq_lengths[0][None, :], 0), 1)
    enc_ends = jnp.sum(jnp.where(lower, enc_lengths[0][None, :], 0), 1)
    passed = ends[None, :] <= place[:, None]
    starts = jnp.max(jnp.where(passed, ends[None, :], 0), 1)
    enc_from = jnp.max(jnp.where(passed, enc_ends[None, :], 0), 1)
    enc_to = jnp.min(jnp.where(passed, enc_slots * size, enc_ends[None, :]), 1)
    self_att = Attention(starts, place + 1, 256, 256, mine * (slots // 256))
    cross_att = Attention(enc_from, enc_to, 256, 128, mine * (enc_slots // 128))
    tiles = total // 256
    half = tiles // 2

    to_place = (order[None, :] == place[:, None]).astype(BF)
    to_slot = (order[:slots, None] == place[None, :]).astype(BF)
    tokens_all = jnp.concatenate(gather_ctx(inputs[0]), 0)
    tokens_all = dot(to_place, tokens_all)
    tokens = tokens_all[:slots]
    encoder = jnp.concatenate(gather_ctx(enc_states[0]), 0)
    outside = jnp.concatenate(gather_ctx(cotangent[0]), 0)
    outside = dot(to_place[:slots], outside)

    hat_all, unused = norm_parts(tokens_all)
    normed_one = (hat_all * gains[0] + shifts[0]).astype(BF)
    queries = dot(normed_one, q_full).astype(BF)
    keys = dot(normed_one, k_full).astype(BF)
    values = dot(normed_one, v_full).astype(BF)
    mixed_high, lse_high = self_att.forward(queries, keys, values, half, half, half)
    mixed_low, lse_low = self_att.forward(queries, keys, values, 0, half, 0)
    after_self = tokens + scatter_halves(dot(mixed_low, out_full), dot(mixed_high, out_full), slots)

    hat_two, rate_two = norm_parts(after_self)
    normed_two = halves(gather_ctx((hat_two * gains[1] + shifts[1]).astype(BF)))
    enc_keys = dot(encoder, ck_full).astype(BF)
    enc_values = dot(encoder, cv_full).astype(BF)
    queries_two = [dot(part, cq_full).astype(BF) for part in normed_two]
    mixed_two = [
        cross_att.forward(queries_two[side], enc_keys, enc_values, side * half, half, 0) for side in range(2)
    ]
    after_cross = after_self + scatter_halves(*(dot(part[0], cross_o_full) for part in mixed_two), slots)

    hat_three, rate_three = norm_parts(after_cross)
    normed_three = halves(gather_ctx((hat_three * gains[2] + shifts[2]).astype(BF)))
    pre_act = [dot(part, first_full) for part in normed_three]
    hidden = [jax.nn.gelu(part, approximate=True).astype(BF) for part in pre_act]
    after_ffn = after_cross + scatter_halves(*(dot(part, second_full) for part in hidden), slots)
    hat_four, rate_four = norm_parts(after_ffn)
    result = hat_four * gains[3] + shifts[3]
    result = jnp.concatenate(gather_ctx(result.astype(BF)), 0)
    result = dot(to_slot, result)

    grad_ffn, gain_three, shift_three = norm_back(hat_four, rate_four, gains[3], outside)
    grad_in = halves(gather_ctx(grad_ffn.astype(BF)))
    grad_pre = [
        gelu_back(part, dot_right(grad, second_full)).astype(BF)
        for part, grad in zip(pre_act, grad_in)
    ]
    arrived = scatter_halves(*(dot_right(grad, first_full) for grad in grad_pre), slots)
    norm_part, gain_two, shift_two = norm_back(hat_three, rate_three, gains[2], arrived)
    grad_cross = grad_ffn + norm_part
    grad_first = sum(dot_left(n, g) for n, g in zip(normed_three, grad_pre))
    grad_second = sum(dot_left(n, g) for n, g in zip(hidden, grad_in))
    feed_grads = jnp.concatenate(
        [
            grad_first.astype(BF).reshape(groups, rows, ff_cols),
            grad_second.astype(BF).reshape(groups, rows, ff_cols),
        ],
        1,
    )
    feed_grads = scatter_wsh(feed_grads.reshape(groups * 2 * rows, ff_cols))
    feed_grads = lax.all_gather(feed_grads, "ctx", axis=0).reshape(size, 2, rows, ff_cols)
    feed_in_grad = jnp.transpose(feed_grads[:, 0].reshape(size, rows, groups, ff_rows), (1, 2, 0, 3))
    feed_in_grad = feed_in_grad.reshape(rows, groups * size * ff_rows).astype(F32)
    feed_out_grad = feed_grads[:, 1].reshape(size * ff_rows, width).astype(F32)

    def share(query_grad, key_grad, value_grad, out_grad):
        packed = [
            query_grad.astype(BF),
            key_grad.astype(BF),
            value_grad.astype(BF),
            out_grad.astype(BF).reshape(groups * rows, cols),
        ]
        packed = scatter_wsh(jnp.concatenate(packed, 1))
        moved = packed[:, 3 * cols :].reshape(piece, width)
        moved = lax.ppermute(moved, ("ctx", "wsh"), [(b, a) for a, b in piece_moves(groups, size)])
        packed = jnp.concatenate([packed[:, : 3 * cols], moved.reshape(rows, cols)], 1)
        packed = lax.all_gather(packed, "ctx", axis=0)
        three = [
            jnp.transpose(packed[:, :, i * cols : (i + 1) * cols], (1, 0, 2)).reshape(rows, width).astype(F32)
            for i in range(3)
        ]
        return three + [packed[:, :, 3 * cols :].reshape(size, piece, width).reshape(rows, width).astype(F32)]

    grad_in = halves(gather_ctx(grad_cross.astype(BF)))
    grad_mixed = [dot_right(grad, cross_o_full).astype(BF) for grad in grad_in]
    back = [
        cross_att.backward(
            queries_two[side], grad_mixed[side], *mixed_two[side], enc_keys, enc_values, side * half, half, 0
        )
        for side in range(2)
    ]
    arrived = scatter_halves(*(dot_right(part[0], cq_full) for part in back), slots)
    norm_part, gain_one, shift_one = norm_back(hat_two, rate_two, gains[1], arrived)
    grad_self = grad_cross + norm_part
    grad_ek = (back[0][1] + back[1][1]).astype(BF)
    grad_ev = (back[0][2] + back[1][2]).astype(BF)
    enc_part = dot_right(grad_ek, ck_full) + dot_right(grad_ev, cv_full)
    enc_grad = scatter_ctx([enc_part[i * enc_slots : (i + 1) * enc_slots] for i in range(size)])
    cross_q_grad, cross_k_grad, cross_v_grad, cross_o_grad = share(
        sum(dot_left(n, part[0]) for n, part in zip(normed_two, back)),
        dot_left(encoder, grad_ek),
        dot_left(encoder, grad_ev),
        sum(dot_left(part[0], g) for part, g in zip(mixed_two, grad_in)),
    )

    grad_in = halves(gather_ctx(grad_self.astype(BF)))
    grad_mixed = [dot_right(grad, out_full).astype(BF) for grad in grad_in]
    back_low = self_att.backward(queries, grad_mixed[0], mixed_low, lse_low, keys, values, 0, half, 0)
    back_high = self_att.backward(queries, grad_mixed[1], mixed_high, lse_high, keys, values, half, half, half)
    grad_q = jnp.concatenate([back_low[0], back_high[0]], 0)
    grad_k = (back_low[1] + back_high[1]).astype(BF)
    grad_v = (back_low[2] + back_high[2]).astype(BF)
    arrived = dot_right(grad_q, q_full) + dot_right(grad_k, k_full) + dot_right(grad_v, v_full)
    arrived = scatter_ctx([arrived[i * slots : (i + 1) * slots] for i in range(size)])
    hat_one, rate_one = norm_parts(tokens)
    norm_part, gain_zero, shift_zero = norm_back(hat_one, rate_one, gains[0], arrived)
    input_grad = grad_self + norm_part
    input_grad = jnp.concatenate(gather_ctx(input_grad.astype(BF)), 0)
    input_grad = dot(to_slot, input_grad)
    query_grad, key_grad, value_grad, out_grad = share(
        dot_left(normed_one, grad_q),
        dot_left(normed_one, grad_k),
        dot_left(normed_one, grad_v),
        dot_left(mixed_low, grad_in[0]) + dot_left(mixed_high, grad_in[1]),
    )

    terms = jnp.stack(
        [gain_zero, gain_one, gain_two, gain_three, shift_zero, shift_one, shift_two, shift_three], 0
    )
    for axis, amount in (("ctx", size), ("wsh", groups)):
        bit = 1
        while bit < amount:
            terms = terms + swap(terms, axis, bit)
            bit *= 2
    terms = jnp.transpose(lax.dynamic_slice_in_dim(terms, row * rows, rows, 1))
    return (
        result[None],
        input_grad[None],
        enc_grad[None],
        query_grad,
        key_grad,
        value_grad,
        out_grad,
        cross_q_grad,
        cross_k_grad,
        cross_v_grad,
        cross_o_grad,
        feed_in_grad,
        feed_out_grad,
        terms[:, :4],
        terms[:, 4:],
    )


SMALL = pl.CostEstimate(flops=1 << 20, transcendentals=0, bytes_accessed=1 << 16)


def call(kernel, outs, scalars, *operands, scratch=(), aliases=None, vmem=12, space=pltpu.VMEM, out_space=pltpu.VMEM):
    specs = [pl.BlockSpec(memory_space=pltpu.SMEM)] * len(scalars)
    specs += [pl.BlockSpec(memory_space=space)] * len(operands)
    return pl.pallas_call(
        kernel,
        in_specs=specs,
        out_specs=[pl.BlockSpec(memory_space=out_space)] * len(outs),
        out_shape=[jax.ShapeDtypeStruct(shape, kind) for shape, kind in outs],
        scratch_shapes=list(scratch),
        input_output_aliases=aliases or {},
        cost_estimate=SMALL,
        compiler_params=pltpu.CompilerParams(vmem_limit_bytes=vmem << 20),
    )(*scalars, *operands)


def call_packing(kernel, outs, *operands):
    scratch = [pltpu.VMEM(operand.shape, operand.dtype) for operand in operands]
    count = len(operands)

    def fetching(*refs):
        sources, outs, held, done = refs[:count], refs[count : -count - 1], refs[-count - 1 : -1], refs[-1]
        copies = [pltpu.make_async_copy(sources[i], held[i], done.at[i]) for i in range(count)]
        for copy in copies:
            copy.start()
        for copy in copies:
            copy.wait()
        kernel(*held, *outs)

    operands = [pltpu.with_memory_space_constraint(operand, pltpu.HBM) for operand in operands]
    scratch.append(pltpu.SemaphoreType.DMA((count,)))
    return call(fetching, outs, (), *operands, scratch=scratch, space=pltpu.HBM)


def call_streaming(kernel, out, steps, *operands, vmem=20):
    shape, kind = out
    part = shape[0] // steps

    def streaming(*refs):
        *sources, out_ref, held, done = refs

        def copy(index):
            at = pl.ds(index * part, part)
            return pltpu.make_async_copy(held.at[at], out_ref.at[at], done.at[index])

        kernel(*sources, held, lambda index: copy(index).start())
        for index in range(steps):
            copy(index).wait()

    scratch = [pltpu.VMEM(shape, kind), pltpu.SemaphoreType.DMA((steps,))]
    return call(streaming, [out], (), *operands, scratch=scratch, vmem=vmem, out_space=pltpu.HBM)[0]


def one_hot(hit):
    return jnp.where(hit, 1.0, 0.0).astype(BF)


def ctx_part(size):
    return pl.ds(pl.multiple_of(lax.axis_index("ctx") * size, size), size)


def my_heads(matrix, size):
    cols = matrix.shape[1] // size
    heads = cols // HEAD
    span = HEAD * size
    source = lax.broadcasted_iota(jnp.int32, (span, cols), 0) - lax.axis_index("ctx") * HEAD
    target = lax.broadcasted_iota(jnp.int32, (span, cols), 1)
    total = None
    for head in range(heads):
        part = dot(matrix[:, head * span : (head + 1) * span], one_hot((source >= 0) & (source < HEAD) & (source == target - head * HEAD)))
        total = part if total is None else total + part
    return total.astype(BF)


def give_pieces_kernel(one, two, out_ref):
    piece = out_ref.shape[0] // 2
    start = pl.multiple_of((lax.axis_index("ctx") % 2) * 2 * piece + piece, piece)
    out_ref[:piece, :] = one[pl.ds(start, piece), :]
    out_ref[piece:, :] = two[pl.ds(start, piece), :]


def my_piece(matrix, given, which):
    piece = given.shape[0] // 2
    mine = lax.axis_index("ctx")
    start = pl.multiple_of((mine % 2) * 2 * piece, piece)
    own = matrix[pl.ds(start, piece), :].astype(F32)
    other = given[which * piece : (which + 1) * piece, :].astype(F32)
    same = lax.axis_index("wsh") % 2 == mine // 2
    return jnp.where(same, own, other).astype(BF)


def pack_kernel(wq, wk, wv, wo, given, *refs, size, which):
    *norm_refs, out_ref = refs
    rows, cols = wq.shape[0], out_ref.shape[1]
    for part, full in enumerate((wq, wk, wv)):
        out_ref[part * rows : (part + 1) * rows, :] = my_heads(full, size)
    taken = my_piece(wo, given, which)
    piece = taken.shape[0]
    for chunk in range(taken.shape[1] // cols):
        at = 3 * rows + chunk * piece
        out_ref[at : at + piece, :] = taken[:, chunk * cols : (chunk + 1) * cols]
    if norm_refs:
        gains, shifts = norm_refs
        norms = jnp.concatenate([gains[...], shifts[...]], 0).astype(F32)
        norms = jnp.concatenate([norms, jnp.zeros((8, rows), F32)], 0)
        norms = jnp.concatenate([norms, jnp.zeros((16, cols - rows), F32)], 1)
        out_ref[out_ref.shape[0] - 16 :, :] = norms.astype(BF)


def pack_feed_kernel(first, second, out_ref, groups, size):
    rows, width = first.shape[0], first.shape[1] // groups
    cols = width // size
    mine = lax.axis_index("ctx")
    for group in range(groups):
        at = pl.ds(pl.multiple_of(group * width + mine * cols, cols), cols)
        out_ref[:rows, group * cols : (group + 1) * cols] = first[:, at]
    out_ref[rows:, :] = second[ctx_part(cols), :]


def sort_kernel(order_ref, *refs, size):
    sources, (hat_ref, own_ref) = refs[:size], refs[size:]
    slots = sources[0].shape[0]
    mine = lax.axis_index("ctx")

    def block(index, carry):
        base = (mine ^ index) * slots
        total = jnp.zeros(own_ref.shape, F32)
        for source in range(size):
            order = order_ref[:, source * slots : (source + 1) * slots]
            place = base + lax.broadcasted_iota(jnp.int32, (slots, slots), 0)
            total += dot(one_hot(order == place), sources[source][...])

        @pl.when(index == 0)
        def _():
            own_ref[...] = total

        hat, unused = norm_parts(total)
        hat_ref[pl.ds(pl.multiple_of(index * slots, slots), slots), :] = hat
        return carry

    lax.fori_loop(0, size, block, 0)


def pick_kernel(order_ref, *refs, size):
    sources, out_ref = refs[:size], refs[size]
    slots = sources[0].shape[0]
    base = lax.axis_index("ctx") * slots
    total = jnp.zeros(out_ref.shape, F32)
    for source in range(size):
        order = order_ref[:, source * slots : (source + 1) * slots]
        place = base + lax.broadcasted_iota(jnp.int32, (slots, slots), 0)
        total += dot(one_hot(order == place), sources[source][...])
    out_ref[...] = total


def unsort_kernel(order_ref, *refs, size):
    count = len(refs) - 1 if len(refs) % size == 1 else len(refs) - 2
    sources, out_ref = refs[:count], refs[count]
    slots = out_ref.shape[0]
    pieces = count // size
    length = slots // pieces
    mine = lax.axis_index("ctx")
    total = jnp.zeros(out_ref.shape, F32)
    for index, source in enumerate(sources):
        first = (mine ^ (index // pieces)) * slots + (index % pieces) * length
        place = first + lax.broadcasted_iota(jnp.int32, (slots, length), 1)
        total += dot(one_hot(order_ref[...] == place), source[:length, :])
    out_ref[...] = total
    if count + 1 < len(refs):
        refs[count + 1][...] = sum(source[slots:, :].astype(F32) for source in sources)


def wsh_rows(index, rows):
    target = (lax.axis_index("wsh") ^ index) * rows
    return pl.ds(pl.multiple_of(target, rows), rows)


def piece_rows(index, piece):
    target = lax.axis_index("wsh") ^ index ^ (lax.axis_index("ctx") // 2)
    return pl.ds(pl.multiple_of(target * piece, piece), piece)


def place_attention(blocks, wq, wk, wv, wo, rows, piece):
    for index, block in enumerate(blocks):
        for part, full in enumerate((wq, wk, wv)):
            full[wsh_rows(index, rows), :] = block[part * rows : (part + 1) * rows, :]
        cols = block.shape[1]
        for chunk in range(wo.shape[1] // cols):
            at = 3 * rows + chunk * piece
            wo[piece_rows(index, piece), chunk * cols : (chunk + 1) * cols] = block[at : at + piece, :]


def project_kernel(hat_ref, *refs, groups, rows, piece):
    blocks = refs[:groups]
    wq, wk, wv, wo, norms, normed_ref, q_ref, k_ref, v_ref = refs[groups:]
    place_attention(blocks, wq, wk, wv, wo, rows, piece)
    for index, block in enumerate(blocks):
        last = block.shape[0] - 16
        norms[:, wsh_rows(index, rows)] = block[last:, :rows].astype(F32)[:8]
    tile = 256

    def step(index, carry):
        at = pl.ds(pl.multiple_of(index * tile, tile), tile)
        normed = (hat_ref[at, :] * norms[0:1, :] + norms[4:5, :]).astype(BF)
        normed_ref[at, :] = normed
        for full, out in ((wq, q_ref), (wk, k_ref), (wv, v_ref)):
            out[at, :] = dot(normed, full[...]).astype(BF)
        return carry

    lax.fori_loop(0, hat_ref.shape[0] // tile, step, 0)


def cross_prepare_kernel(blocks, *refs, size, rows, piece):
    encoder = refs[:size]
    wq, wk, wv, wo, key_ref, value_ref = refs[size:]
    groups, cols = blocks.shape[0], blocks.shape[2]
    for index in range(groups):
        for part, full in enumerate((wq, wk, wv)):
            full[index * rows : (index + 1) * rows, :] = blocks[index, part * rows : (part + 1) * rows, :]
        target = (index ^ (lax.axis_index("ctx") // 2)) * piece
        there = pl.ds(pl.multiple_of(target, piece), piece)
        for chunk in range(wo.shape[1] // cols):
            at = 3 * rows + chunk * piece
            wo[there, chunk * cols : (chunk + 1) * cols] = blocks[index, at : at + piece, :]
    slots = encoder[0].shape[0]
    for index, part in enumerate(encoder):
        at = slice(index * slots, (index + 1) * slots)
        key_ref[at, :] = dot(part[...], wk[...]).astype(BF)
        value_ref[at, :] = dot(part[...], wv[...]).astype(BF)


def attend(split, low, high, first, last, flip, k_ref, v_ref, top, total, mixed, heads, chunk):
    tile = mixed.shape[1]
    top[...] = jnp.full_like(top, -1e30)
    total[...] = jnp.zeros_like(total)
    mixed[...] = jnp.zeros_like(mixed)

    def step(index, carry):
        start = pl.multiple_of((index ^ flip) * chunk, chunk)
        keys = k_ref[pl.ds(start, chunk), :]
        values = jnp.transpose(v_ref[pl.ds(start, chunk), :])
        scores = dot_right(keys, split)
        scores = jnp.where(allowed_keys(index * chunk, chunk, low, high), scores, -1e30)
        before = top[...]
        now = jnp.maximum(before, jnp.max(scores, axis=0, keepdims=True))
        decay = jnp.exp(before - now)
        weight = jnp.exp(scores - now)
        top[...] = now
        total[...] = total[...] * decay + jnp.sum(weight, axis=0, keepdims=True)
        weight = weight.astype(BF)
        for h in range(heads):
            rows, cols = slice(h * HEAD, (h + 1) * HEAD), slice(h * tile, (h + 1) * tile)
            mixed[rows, :] = mixed[rows, :] * decay[:, cols] + dot(values[rows, :], weight[:, cols])
        return carry

    lax.fori_loop(first, last, step, 0)
    amount = total[...]
    for h in range(heads):
        rows, cols = slice(h * HEAD, (h + 1) * HEAD), slice(h * tile, (h + 1) * tile)
        mixed[rows, :] = mixed[rows, :] / amount[:, cols]
    return top[...] + jnp.log(amount)


def attend_forward_kernel(meta, *refs, own_queries, parts, offset, count, chunk):
    if own_queries:
        sources, wq = refs[:parts], refs[parts]
        k_ref, v_ref, rows_ref, wo, q_ref, mixed_ref, lse_ref = refs[parts + 1 : parts + 8]
        rest = refs[parts + 8 :]
        for index, source in enumerate(sources):
            slots = source.shape[0]
            q_ref[index * slots : (index + 1) * slots, :] = dot(source[...], wq[...]).astype(BF)
        shift = 0
    else:
        q_ref, k_ref, v_ref, rows_ref, wo, mixed_ref, lse_ref = refs[:7]
        rest = refs[7:]
        shift = offset
    outs, (top, total, mixed) = rest[:parts], rest[parts:]
    tile = mixed.shape[1]
    heads = q_ref.shape[1] // HEAD

    def block(index, carry):
        at = pl.ds(pl.multiple_of((index + shift) * tile, tile), tile)
        split = split_heads(q_ref[at, :].astype(F32) * 0.125, heads, HEAD)
        low = spread(rows_ref[index + offset, 0:1, :], heads)
        high = spread(rows_ref[index + offset, 1:2, :], heads)
        first, last = meta[1 + index + offset], meta[1 + count + index + offset]
        lse_ref[index] = attend(split, low, high, first, last, meta[0], k_ref, v_ref, top, total, mixed, heads, chunk)
        here = pl.ds(pl.multiple_of(index * tile, tile), tile)
        mixed_ref[here, :] = jnp.transpose(mixed[...]).astype(BF)
        return carry

    lax.fori_loop(0, mixed_ref.shape[0] // tile, block, 0)
    for index, out in enumerate(outs):
        slots = out.shape[0]
        out[...] = dot(mixed_ref[index * slots : (index + 1) * slots, :], wo[...]).astype(BF)


def attend_backward_kernel(meta, *refs, own_queries, parts, offset, count, chunk, fresh):
    sources = refs[:parts]
    q_ref, mixed_ref, lse_ref, rows_ref, k_ref, v_ref, wo = refs[parts : parts + 7]
    rest = refs[parts + 7 :]
    if own_queries:
        wq, rest = rest[0], rest[1:]
    if not fresh:
        rest = rest[3:]
    dq_ref, dk_ref, dv_ref, dwo_ref = rest[:4]
    outs = rest[4 : 4 + parts] if own_queries else ()
    grad_ref, dq_sum = rest[-2:]
    tile = dq_sum.shape[1]
    heads = q_ref.shape[1] // HEAD
    shift = 0 if own_queries else offset
    if fresh:
        dk_ref[...] = jnp.zeros_like(dk_ref)
        dv_ref[...] = jnp.zeros_like(dv_ref)
    change = None
    for index, source in enumerate(sources):
        slots = source.shape[0]
        at = slice(index * slots, (index + 1) * slots)
        grad_ref[at, :] = dot_right(source[...], wo[...]).astype(BF)
        part = dot_left(mixed_ref[at, :], source[...])
        change = part if change is None else change + part
    dwo_ref[...] = change if fresh else dwo_ref[...] + change

    def block(index, carry):
        at = pl.ds(pl.multiple_of((index + shift) * tile, tile), tile)
        here = pl.ds(pl.multiple_of(index * tile, tile), tile)
        split = split_heads(q_ref[at, :].astype(F32) * 0.125, heads, HEAD)
        grads = split_heads(grad_ref[here, :], heads, HEAD)
        low = spread(rows_ref[index + offset, 0:1, :], heads)
        high = spread(rows_ref[index + offset, 1:2, :], heads)
        lse = lse_ref[index]
        product = jnp.transpose(grad_ref[here, :].astype(F32) * mixed_ref[here, :].astype(F32))
        inner = jnp.concatenate(
            [jnp.sum(product[h * HEAD : (h + 1) * HEAD], axis=0, keepdims=True) for h in range(heads)], 1
        )
        dq_sum[...] = jnp.zeros_like(dq_sum)

        def step(number, carry):
            start = pl.multiple_of((number ^ meta[0]) * chunk, chunk)
            keys = k_ref[pl.ds(start, chunk), :]
            scores = dot_right(keys, split)
            scores = jnp.where(allowed_keys(number * chunk, chunk, low, high), scores, -1e30)
            weight = jnp.exp(scores - lse)
            slope = dot_right(v_ref[pl.ds(start, chunk), :], grads)
            slope = (weight * (slope - inner)).astype(BF)
            dv_ref[pl.ds(start, chunk), :] += dot(weight.astype(BF), grads)
            dk_ref[pl.ds(start, chunk), :] += dot(slope, split)
            turned = jnp.transpose(keys)
            for h in range(heads):
                rows, cols = slice(h * HEAD, (h + 1) * HEAD), slice(h * tile, (h + 1) * tile)
                dq_sum[rows, :] += dot(turned[rows, :], slope[:, cols])
            return carry

        lax.fori_loop(meta[1 + index + offset], meta[1 + count + index + offset], step, 0)
        dq_ref[here, :] = (jnp.transpose(dq_sum[...]) * 0.125).astype(BF)
        return carry

    lax.fori_loop(0, dq_ref.shape[0] // tile, block, 0)
    for index, out in enumerate(outs):
        slots = out.shape[0]
        out[...] = dot_right(dq_ref[index * slots : (index + 1) * slots, :], wq[...]).astype(BF)


def total_of(base, parts):
    value = base[...]
    for part in parts:
        value = value + part[...].astype(F32)
    return value


def norm_kernel(norms, base, *refs, which):
    parts, (sum_ref, normed_ref) = refs[:-2], refs[-2:]
    value = total_of(base, parts)
    sum_ref[...] = value
    hat, unused = norm_parts(value)
    normed_ref[...] = (hat * norms[which : which + 1, :] + norms[4 + which : 5 + which, :]).astype(BF)


def norm_back_kernel(norms, value_ref, grad_ref, *refs, which):
    parts, (out_ref, sent_ref, terms_ref) = refs[:-3], refs[-3:]
    hat, rate = norm_parts(value_ref[...])
    grad = parts[0][...].astype(F32)
    for part in parts[1:]:
        grad = grad + part[...].astype(F32)
    change, gain, shift = norm_back(hat, rate, norms[which : which + 1, :], grad)
    result = grad_ref[...] + change
    out_ref[...] = result
    sent_ref[...] = result.astype(BF)
    terms_ref[0:1, :] = gain[None]
    terms_ref[1:2, :] = shift[None]


def norm_first_kernel(norms, value_ref, grad_ref, near, other, far, one, two, three, sent_ref):
    slots = value_ref.shape[0]
    hat, rate = norm_parts(value_ref[...])
    grad = near[...].astype(F32) + other[...].astype(F32) + far[...].astype(F32)
    change, gain, shift = norm_back(hat, rate, norms[0:1, :], grad)
    sent_ref[:slots, :] = (grad_ref[...] + change).astype(BF)
    sums = [gain[None], shift[None], one[...], two[...], three[...], jnp.zeros((8, gain.shape[0]), F32)]
    sent_ref[slots:, :] = jnp.concatenate(sums, 0).astype(BF)


def norm_turn_kernel(norms, base, outside, *refs):
    parts, (low_ref, high_ref, out_ref, sent_ref, terms_ref) = refs[:-5], refs[-5:]
    hat, rate = norm_parts(total_of(base, parts))
    result = (hat * norms[3:4, :] + norms[7:8, :]).astype(BF)
    low_ref[...] = result[: low_ref.shape[0]]
    high_ref[...] = result[low_ref.shape[0] :]
    change, gain, shift = norm_back(hat, rate, norms[3:4, :], outside[...])
    out_ref[...] = change
    sent_ref[...] = change.astype(BF)
    terms_ref[0:1, :] = gain[None]
    terms_ref[1:2, :] = shift[None]


def feed_halves(feed):
    groups, rows, cols = feed.shape
    rows = rows // 2
    return feed[:, :rows, :].reshape(groups * rows, cols), feed[:, rows:, :].reshape(groups * rows, cols)


def feed_forward_kernel(*refs, parts):
    sources, (feed, hidden_ref, slope_ref), outs = refs[:parts], refs[parts : parts + 3], refs[parts + 3 :]
    rate = 0.7978845608028654
    first, second = feed_halves(feed)
    for index, (source, out) in enumerate(zip(sources, outs)):
        slots = source.shape[0]
        at = slice(index * slots, (index + 1) * slots)
        pre = dot(source[...], first)
        square = pre * pre
        bend = jnp.tanh(rate * pre * (1.0 + 0.044715 * square))
        half = 0.5 * (1.0 + bend)
        slope_ref[at, :] = (half + 0.5 * pre * (1.0 - bend * bend) * rate * (1.0 + 0.134145 * square)).astype(BF)
        hidden_ref[at, :] = (pre * half).astype(BF)
        out[...] = dot(hidden_ref[at, :], second).astype(BF)


def feed_backward_kernel(*refs, parts):
    sources, (feed, slope_ref, change_ref), outs = refs[:parts], refs[parts : parts + 3], refs[parts + 3 :]
    first, second = feed_halves(feed)
    for index, (source, out) in enumerate(zip(sources, outs)):
        slots = source.shape[0]
        at = slice(index * slots, (index + 1) * slots)
        change = dot_right(source[...], second) * slope_ref[at, :].astype(F32)
        change_ref[at, :] = change.astype(BF)
        out[...] = dot_right(change_ref[at, :], first).astype(BF)


def feed_grad_kernel(*refs, size, rows):
    normed, (change_low, change_high, hidden_low, hidden_high) = refs[:size], refs[size : size + 4]
    grads, (out_ref, send) = refs[size + 4 : 2 * size + 4], refs[-2:]
    middle, slots = size // 2, normed[0].shape[0]
    wide = 2 * rows

    def step(index, carry):
        lanes = pl.ds(pl.multiple_of(index * wide, wide), wide)
        first, second = None, None
        for block in range(size):
            side, at = block // middle, (block % middle) * slots
            change = (change_low, change_high)[side][at : at + slots, :]
            hidden = (hidden_low, hidden_high)[side][at : at + slots, lanes]
            one = dot_left(normed[block][:, lanes], change)
            two = dot_left(hidden, grads[block][...])
            first, second = (one, two) if first is None else (first + one, second + two)
        for part in range(2):
            at = slice(part * rows, (part + 1) * rows)
            out_ref[2 * index + part, 0:rows, :] = first[at, :].astype(BF)
            out_ref[2 * index + part, rows : 2 * rows, :] = second[at, :].astype(BF)
        send(index)
        return carry

    lax.fori_loop(0, out_ref.shape[0] // 2, step, 0)


def weight_grad_kernel(*refs, terms, odd, rows, piece, count):
    operands, extra, outs, held = refs[: -count - 2], refs[-count - 2], refs[-count - 1 : -1], refs[-1]
    height, cols = outs[0].shape
    mine = lax.axis_index("wsh")

    def step(index, carry):
        target = mine ^ (2 * index + odd)
        lanes = pl.ds(pl.multiple_of(target * rows, rows), rows)
        for part in range(3):
            value = None
            for which, left, left_at, right, right_at, length in terms:
                if which == part:
                    one = dot_left(
                        operands[left][left_at : left_at + length, lanes],
                        operands[right][right_at : right_at + length, :].astype(BF),
                    )
                    value = one if value is None else value + one
            held[index, part * rows : (part + 1) * rows, :] = value.astype(held.dtype)
        taken = piece_rows(2 * index + odd, piece)
        for chunk in range(extra.shape[1] // cols):
            at = 3 * rows + chunk * piece
            held[index, at : at + piece, :] = extra[taken, chunk * cols : (chunk + 1) * cols].astype(held.dtype)
        return carry

    lax.fori_loop(0, count, step, 0)
    for index, out in enumerate(outs):
        out[...] = held[index]


def back_project_kernel(dq_ref, dk_ref, dv_ref, wq, wk, wv, *outs, first):
    for index, out in enumerate(outs):
        slots = out.shape[0]
        at = slice(index * slots, (index + 1) * slots)
        there = slice(first + index * slots, first + (index + 1) * slots)
        value = dot_right(dq_ref[at, :], wq[...])
        value += dot_right(dk_ref[there, :].astype(BF), wk[...])
        value += dot_right(dv_ref[there, :].astype(BF), wv[...])
        out[...] = value.astype(BF)


def encoder_grad_kernel(dk_ref, dv_ref, wk, wv, *outs):
    for index, out in enumerate(outs):
        slots = out.shape[0]
        at = slice(index * slots, (index + 1) * slots)
        value = dot_right(dk_ref[at, :].astype(BF), wk[...]) + dot_right(dv_ref[at, :].astype(BF), wv[...])
        out[...] = value.astype(BF)


def place_square_kernel(*refs, count, rows, piece):
    mine = lax.axis_index("ctx")
    threes, (near, other), outs = refs[:count], refs[count : count + 2], refs[count + 2 :]
    cols = threes[0].shape[1]
    span = HEAD * count
    blocks = [three[...].astype(F32) for three in threes]
    for group in range(count):
        wanted = mine ^ group
        chosen = blocks[0]
        for index in range(1, count):
            chosen = jnp.where(wanted == index, blocks[index], chosen)
        for part in range(3):
            for head in range(cols // HEAD):
                at = head * span + group * HEAD
                outs[part][:, at : at + HEAD] = chosen[
                    part * rows : (part + 1) * rows, head * HEAD : (head + 1) * HEAD
                ]
    core = mine % 2
    for source, place in ((near, core), (other, 1 - core)):
        for half in range(2):
            row = pl.ds(pl.multiple_of((2 * place + half) * piece, piece), piece)
            for chunk in range(outs[3].shape[1] // cols):
                at = (half * (outs[3].shape[1] // cols) + chunk) * piece
                outs[3][row, chunk * cols : (chunk + 1) * cols] = source[at : at + piece, :].astype(F32)


def place_feed_kernel(*refs, count, groups, rows, cols):
    mine = lax.axis_index("ctx")
    first, second = refs[count:]
    for index in range(count):
        target = mine ^ index
        for group in range(groups):
            column = pl.ds(pl.multiple_of(group * count * cols + target * cols, cols), cols)
            first[:, column] = refs[index][:rows, group * cols : (group + 1) * cols].astype(F32)
        row = pl.ds(pl.multiple_of(target * cols, cols), cols)
        second[row, :] = refs[index][rows:, :].astype(F32)


def fold(near, sent):
    arrived = swap(sent, "ctx", 1)
    return near, arrived


def after(value, *others):
    return lax.optimization_barrier((value,) + others)[0]


def far_hop(parts):
    arrived = swap(parts[1], "ctx", 1)
    sent = (parts[0].astype(F32) + arrived.astype(F32)).astype(BF)
    return sent, swap(sent, "ctx", 2)


def spread_ctx(own):
    far = swap(own, "ctx", 2)
    near = swap(own, "ctx", 1)
    return [own, near, far, swap(far, "ctx", 1)]


def start_ctx(own):
    return [own, swap(own, "ctx", 1), swap(own, "ctx", 2)]


def finish_ctx(blocks, *before):
    far = after(blocks[2], *before)
    return blocks[:2] + [far, swap(far, "ctx", 1)]


def send_z(own):
    size = lax.axis_size("wsh")
    blocks = {0: own, 1: swap(own, "wsh", 1)}
    for bit in range(2, size, 2):
        blocks[bit] = swap(own, "wsh", bit)
    return blocks


def pass_y(blocks):
    size = lax.axis_size("wsh")
    for bit in range(2, size, 2):
        blocks[bit + 1] = swap(blocks[bit], "wsh", 1)
    return [blocks[bit] for bit in range(size)]


class Ranges:
    def __init__(self, low, high, tile, chunk, flip):
        self.tile, self.chunk, self.count = tile, chunk, low.shape[0] // tile
        low, high = low.reshape(self.count, tile), high.reshape(self.count, tile)
        self.rows = jnp.stack([low, high], 1)
        first, last = jnp.min(low, 1) // chunk, (jnp.max(high, 1) - 1) // chunk + 1
        self.meta = jnp.concatenate([flip.reshape(1), first, last]).astype(jnp.int32)


def fast_body(
    inputs,
    enc_states,
    cotangent,
    slot_order,
    seq_lengths,
    enc_lengths,
    self_query,
    self_key,
    self_value,
    self_out,
    cross_query,
    cross_key,
    cross_value,
    cross_out,
    feed_in,
    feed_out,
    norm_gains,
    norm_shifts,
):
    size, groups = lax.axis_size("ctx"), lax.axis_size("wsh")
    mine, row = lax.axis_index("ctx"), lax.axis_index("wsh")
    slots = inputs.shape[1]
    total = slots * size
    enc_slots = enc_states.shape[1]
    width = inputs.shape[2]
    rows = self_query.shape[0]
    cols = width // size
    piece = rows // size
    ff_cols = feed_in.shape[1] // size
    ff_rows = feed_out.shape[0] // size
    heads = cols // HEAD
    middle = total // 2
    part = size // 2
    block_bf, block_f = ((slots, width), BF), ((slots, width), F32)
    terms_f = ((2, width), F32)

    given = call_packing(give_pieces_kernel, [((2 * piece, width), BF)], self_out, cross_out)[0]
    given = swap(given, "wsh", 1)
    height = 3 * rows + piece * (width // cols)
    self_block = call_packing(
        functools.partial(pack_kernel, size=size, which=0),
        [((height + 16, cols), BF)],
        self_query,
        self_key,
        self_value,
        self_out,
        given,
        jnp.transpose(norm_gains),
        jnp.transpose(norm_shifts),
    )[0]
    self_blocks = send_z(self_block)
    token_blocks = start_ctx(inputs[0])
    self_blocks = pass_y(self_blocks)
    token_blocks = finish_ctx(token_blocks)
    cross_block = call_packing(
        functools.partial(pack_kernel, size=size, which=1),
        [((height, cols), BF)],
        after(cross_query, self_block),
        cross_key,
        cross_value,
        cross_out,
        given,
    )[0]
    packed = cross_block
    cross_block = gather_wsh(cross_block).reshape(groups, height, cols)
    feed = call_packing(
        functools.partial(pack_feed_kernel, groups=groups, size=size),
        [((2 * rows, ff_cols), BF)],
        after(feed_in, self_block),
        feed_out,
    )[0]
    feed = gather_wsh(after(feed, packed, self_blocks[2])).reshape(groups, 2 * rows, ff_cols)

    relative = jnp.arange(size, dtype=jnp.int32) ^ mine
    order = jnp.take(slot_order[0].reshape(size, slots), relative, axis=0).reshape(1, total)
    own_order = lax.dynamic_slice_in_dim(slot_order[0], mine * slots, slots).reshape(slots, 1)
    place = (relative[:, None] * slots + jnp.arange(slots, dtype=jnp.int32)).reshape(total)
    lower = jnp.arange(seq_lengths.shape[1])
    lower = lower[None, :] <= lower[:, None]
    ends = jnp.sum(jnp.where(lower, seq_lengths[0][None, :], 0), 1)
    enc_ends = jnp.sum(jnp.where(lower, enc_lengths[0][None, :], 0), 1)
    passed = ends[None, :] <= place[:, None]
    starts = jnp.max(jnp.where(passed, ends[None, :], 0), 1)
    enc_from = jnp.max(jnp.where(passed, enc_ends[None, :], 0), 1)
    enc_to = jnp.min(jnp.where(passed, enc_slots * size, enc_ends[None, :]), 1)
    self_range = Ranges(starts, place + 1, 256, 256, mine * (slots // 256))
    cross_range = Ranges(enc_from, enc_to, 256, 128, mine * (enc_slots // 128))
    half = total // 512

    def unsort(blocks):
        outs = [block_f]
        if blocks[0].shape[0] > slots:
            outs.append(((blocks[0].shape[0] - slots, width), F32))
        return call(functools.partial(unsort_kernel, size=size), outs, (), own_order, *blocks)

    hat_all, tokens = call(
        functools.partial(sort_kernel, size=size), [((total, width), F32), block_f], (), order, *token_blocks
    )

    square, tall = ((width, cols), BF), ((total, cols), BF)
    wq, wk, wv, wo, norms, normed_one, queries, keys, values = call(
        functools.partial(project_kernel, groups=groups, rows=rows, piece=piece),
        [square] * 3 + [((cols, width), BF), ((8, width), F32), ((total, width), BF)] + [tall] * 3,
        (),
        hat_all,
        *self_blocks,
    )
    lanes = heads * 256
    half_outs = [((middle, cols), BF), ((half, 1, lanes), F32)] + [block_bf] * part
    scratch = [pltpu.VMEM((1, lanes), F32), pltpu.VMEM((1, lanes), F32), pltpu.VMEM((cols, 256), F32)]

    def self_forward(side, queries):
        body = functools.partial(
            attend_forward_kernel,
            own_queries=False,
            parts=part,
            offset=side * half,
            count=self_range.count,
            chunk=self_range.chunk,
        )
        return call(
            body, half_outs, (self_range.meta,), queries, keys, values, self_range.rows, wo, scratch=scratch
        )

    encoder = spread_ctx(after(enc_states[0], normed_one))
    mixed_high, lse_high, *far = self_forward(1, queries)
    sent, arrived = far_hop(far)
    mixed_low, lse_low, *near = self_forward(0, after(queries, sent))

    def normalize(base, near, arrived, which):
        return call(
            functools.partial(norm_kernel, which=which),
            [block_f, block_bf],
            (),
            norms,
            base,
            near[0],
            swap(near[1], "ctx", 1),
            arrived,
        )

    after_self, normed = normalize(tokens, near, arrived, 1)
    outside = spread_ctx(after(cotangent[0], arrived))
    outside = call(functools.partial(pick_kernel, size=size), [block_f], (), order, *outside)[0]

    normed_two = start_ctx(normed)
    cq, ck, cv, co, enc_keys, enc_values = call(
        functools.partial(cross_prepare_kernel, size=size, rows=rows, piece=piece),
        [square] * 3 + [((cols, width), BF)] + [((enc_slots * size, cols), BF)] * 2,
        (),
        cross_block,
        *encoder,
    )

    def cross_forward(side):
        body = functools.partial(
            attend_forward_kernel,
            own_queries=True,
            parts=part,
            offset=side * half,
            count=cross_range.count,
            chunk=cross_range.chunk,
        )
        return call(
            body,
            [((middle, cols), BF)] + half_outs,
            (cross_range.meta,),
            *normed_two[side * part : (side + 1) * part],
            cq,
            enc_keys,
            enc_values,
            cross_range.rows,
            co,
            scratch=scratch,
        )

    cross_low = cross_forward(0)
    normed_two = finish_ctx(normed_two, cross_low[3])
    cross_high = cross_forward(1)
    sent, arrived = far_hop(cross_high[3:])
    after_cross, normed = normalize(after_self, cross_low[3:], arrived, 2)

    normed_three = start_ctx(normed)
    def feed_forward(side):
        return call(
            functools.partial(feed_forward_kernel, parts=part),
            [((middle, ff_cols), BF)] * 2 + [block_bf] * part,
            (),
            *normed_three[side * part : (side + 1) * part],
            feed,
        )

    hidden_low, slope_low, *near = feed_forward(0)
    normed_three = finish_ctx(normed_three, near[0])
    hidden_high, slope_high, *far = feed_forward(1)
    sent, arrived = far_hop(far)
    result_low, result_high, grad_ffn, grad, terms_three = call(
        norm_turn_kernel,
        [((slots // 2, width), BF)] * 2 + [block_f, block_bf, terms_f],
        (),
        norms,
        after_cross,
        outside,
        near[0],
        swap(near[1], "ctx", 1),
        arrived,
    )

    def denormalize(value, grad, near, arrived, which):
        return call(
            functools.partial(norm_back_kernel, which=which),
            [block_f, block_bf, terms_f],
            (),
            norms,
            value,
            grad,
            near[0],
            swap(near[1], "ctx", 1),
            arrived,
        )

    grad_in = start_ctx(grad)

    def feed_backward(side, slope):
        return call(
            functools.partial(feed_backward_kernel, parts=part),
            [((middle, ff_cols), BF)] + [block_bf] * part,
            (),
            *grad_in[side * part : (side + 1) * part],
            feed,
            slope,
        )

    change_low, *near = feed_backward(0, slope_low)
    grad_in = finish_ctx(grad_in, near[0])
    change_high, *far = feed_backward(1, slope_high)
    sent, arrived = far_hop(far)
    feed_grads = call_streaming(
        functools.partial(feed_grad_kernel, size=size, rows=rows),
        ((groups, 2 * rows, width), BF),
        groups // 2,
        *normed_three,
        change_low,
        after(change_high, sent),
        hidden_low,
        hidden_high,
        *grad_in,
    )
    grad_cross, grad, terms_two = denormalize(after_cross, grad_ffn, near, after(arrived, feed_grads), 2)
    feed_grads = scatter_wsh(after(feed_grads, arrived).reshape(groups * 2 * rows, width))

    def weight_grads(terms, operands, out_grad, odd):
        count = groups // 2
        kind = BF if odd else F32
        body = functools.partial(weight_grad_kernel, terms=terms, odd=odd, rows=rows, piece=piece, count=count)
        outs = [((height, cols), kind)] * count
        return call(body, outs, (), *operands, out_grad, scratch=[pltpu.VMEM((count, height, cols), kind)])

    def pass_z(even, odd, index):
        value = (even[index] + odd[index].astype(F32)).astype(BF)
        return swap(value, "wsh", 2 * index)

    def backward(span, side, own_queries, sources, queries, mixed, lse, keys, values, wo, wq, before):
        body = functools.partial(
            attend_backward_kernel,
            own_queries=own_queries,
            parts=part,
            offset=side * half,
            count=span.count,
            chunk=span.chunk,
            fresh=before is None,
        )
        operands = [*sources, queries, mixed, lse, span.rows, keys, values, wo]
        if own_queries:
            operands.append(wq)
        aliases = {}
        if before is not None:
            aliases = {1 + len(operands) + i: 1 + i for i in range(3)}
            operands += before
        outs = [((middle, cols), BF), (keys.shape, F32), (keys.shape, F32), ((cols, width), F32)]
        if own_queries:
            outs += [block_bf] * part
        return call(
            body,
            outs,
            (span.meta,),
            *operands,
            scratch=[pltpu.VMEM((middle, cols), BF), pltpu.VMEM((cols, 256), F32)],
            aliases=aliases,
        )

    grad_in = start_ctx(grad)
    low = backward(
        cross_range, 0, True, grad_in[:part], *cross_low[:3], enc_keys, enc_values, co, cq, None
    )
    grad_in = finish_ctx(grad_in, low[4])
    result_low = start_ctx(after(result_low, grad_in[2]))
    high = backward(
        cross_range, 1, True, grad_in[part:], *cross_high[:3], enc_keys, enc_values, co, cq, list(low[1:4])
    )
    sent, arrived = far_hop([high[4], after(high[5], result_low[2])])
    dk, dv, dwo = high[1:4]
    operands = [*normed_two, low[0], high[0], *encoder, dk, dv]
    terms = []
    for index in range(size):
        side = index // part
        terms.append((0, index, 0, size + side, (index % part) * slots, slots))
    for index in range(size):
        for which in (1, 2):
            terms.append((which, size + 2 + index, 0, 2 * size + 1 + which, index * enc_slots, enc_slots))
    dk = after(dk, sent)
    operands[-2] = dk
    odd = weight_grads(tuple(terms), operands, dwo, 1)
    cross_even = weight_grads(tuple(terms), operands, dwo, 0)
    enc_parts = call(encoder_grad_kernel, [((enc_slots, width), BF)] * size, (), dk, dv, ck, cv)
    cross_odd = [swap(block, "wsh", 1) for block in odd]
    cross_far = pass_z(cross_even, cross_odd, 3)
    arrived = after(arrived, cross_even[0], cross_odd[3], *enc_parts)
    grad_self, grad, terms_one = denormalize(after_self, grad_cross, low[4:], arrived, 1)

    grad_in = start_ctx(grad)
    low = backward(
        self_range, 0, False, grad_in[:part], queries, mixed_low, lse_low, keys, values, wo, None, None
    )
    grad_in = finish_ctx(grad_in, low[0], cross_odd[2])
    cross_middle = pass_z(cross_even, cross_odd, 2)
    result_high = start_ctx(after(result_high, grad_in[2]))
    enc_sent, enc_far = far_hop([after(enc_parts[2], grad_in[2]), enc_parts[3]])
    enc_near = swap(enc_parts[1], "ctx", 1)
    enc_grad = enc_parts[0].astype(F32) + enc_near.astype(F32) + enc_far.astype(F32)
    high = backward(
        self_range, 1, False, grad_in[part:], queries, mixed_high, lse_high, keys, values, wo, None, list(low[1:4])
    )
    dk, dv, dwo = high[1:4]

    def back_project(side, dq):
        body = functools.partial(back_project_kernel, first=side * middle)
        return call(body, [block_bf] * part, (), dq, dk, dv, wq, wk, wv)

    far = back_project(1, after(high[0], cross_odd[1], cross_far))
    cross_near = pass_z(cross_even, cross_odd, 1)
    operands = [normed_one, low[0], high[0], after(dk, result_high[2]), dv]
    terms = ((0, 0, 0, 1, 0, middle), (0, 0, middle, 2, 0, middle), (1, 0, 0, 3, 0, total), (2, 0, 0, 4, 0, total))
    odd = weight_grads(terms, operands, dwo, 1)
    sent, arrived = far_hop(far)
    self_odd = [swap(block, "wsh", 1) for block in odd]
    near = back_project(0, after(low[0], sent, odd[0]))
    self_even = weight_grads(terms, operands, after(dwo, *near), 0)
    self_far = pass_z(self_even, self_odd, 3)

    feed_blocks = start_ctx(after(feed_grads, sent))
    grad = call(
        norm_first_kernel,
        [((slots + 16, width), BF)],
        (),
        norms,
        tokens,
        grad_self,
        near[0],
        swap(near[1], "ctx", 1),
        after(arrived, self_even[0]),
        terms_one,
        terms_two,
        terms_three,
    )[0]
    input_grad = start_ctx(grad)

    def finish(even, odd, *parts):
        share = even[0] + odd[0].astype(F32)
        for value in parts:
            share = share + value.astype(F32)
        share = share.astype(BF)
        three, fourth = share[: 3 * rows], share[3 * rows :]
        pair = jnp.concatenate([fourth, swap(fourth, "wsh", 1)], 0)
        pair = jnp.where(row % 2 == mine // 2, pair, swap(pair, "ctx", 2))
        return call(
            functools.partial(place_square_kernel, count=size, rows=rows, piece=piece),
            [((rows, width), F32)] * 4,
            (),
            *spread_ctx(three),
            pair,
            swap(pair, "ctx", 1),
        )

    result_low = finish_ctx(result_low, self_odd[3], grad)
    result_high = finish_ctx(result_high)
    result = unsort([half for pair in zip(result_low, result_high) for half in pair])[0]
    self_middle = pass_z(self_even, self_odd, 2)
    self_near = pass_z(self_even, self_odd, 1)
    feed_in_grad, feed_out_grad = call(
        functools.partial(place_feed_kernel, count=size, groups=groups, rows=rows, cols=ff_rows),
        [((rows, groups * size * ff_rows), F32), ((size * ff_rows, width), F32)],
        (),
        *finish_ctx(feed_blocks, self_odd[2], result, cross_near),
    )
    input_grad, terms = unsort(finish_ctx(input_grad, self_odd[1], self_far, feed_in_grad))
    terms = terms[:8]
    terms = terms + swap(terms, "wsh", 1)
    pieces = [lax.dynamic_slice_in_dim(terms, (row ^ bit) * rows, rows, 1) for bit in range(0, groups, 2)]
    terms = pieces[0]
    for index in range(1, groups // 2):
        terms = terms + swap(pieces[index], "wsh", 2 * index)
    terms = jnp.transpose(terms)
    cross_odd[0] = after(cross_odd[0], input_grad, self_middle, self_near)
    cross_grads = finish(cross_even, cross_odd, cross_near, cross_middle, cross_far)
    self_grads = finish(self_even, self_odd, self_near, self_middle, self_far)
    return (
        result[None],
        input_grad[None],
        enc_grad[None],
        *self_grads,
        *cross_grads,
        feed_in_grad,
        feed_out_grad,
        terms[:, 0::2],
        terms[:, 1::2],
    )


def solution(mesh):
    token, weight = P("wsh", "ctx", None), P("wsh", None)
    in_specs = (token,) * 3 + (weight,) * 15
    out_specs = (token,) * 3 + (weight,) * 12
    body = fast_body if mesh.shape["ctx"] == 4 else plain_body
    return jax.shard_map(body, mesh=mesh, in_specs=in_specs, out_specs=out_specs, check_vma=False)
```

```python
import functools

import jax
import jax.numpy as jnp
from jax import lax
from jax.experimental import pallas as pl
from jax.experimental.pallas import tpu as pltpu
from jax.sharding import PartitionSpec as P

HEAD = 64
BF = jnp.bfloat16
F32 = jnp.float32


def dot(left, right):
    return jnp.dot(left, right, preferred_element_type=F32)


def dot_left(left, right):
    return lax.dot_general(left, right, (((0,), (0,)), ((), ())), preferred_element_type=F32)


def dot_right(left, right):
    return lax.dot_general(left, right, (((1,), (1,)), ((), ())), preferred_element_type=F32)


def swap(value, axis, bit):
    size = lax.axis_size(axis)
    return lax.ppermute(value, axis, [(i, i ^ bit) for i in range(size)])


def gather_ctx(own):
    size = lax.axis_size("ctx")
    blocks = {0: own}
    bit = size // 2
    while bit:
        for index in sorted(blocks):
            blocks[index | bit] = swap(blocks[index], "ctx", bit)
        bit //= 2
    return [blocks[index] for index in range(size)]


def scatter_ctx(blocks):
    blocks = dict(enumerate(blocks))
    size, bit = len(blocks), 1
    while bit < size:
        for index in sorted(blocks, reverse=True):
            if index & bit:
                arrived = swap(blocks.pop(index).astype(BF), "ctx", bit)
                blocks[index ^ bit] = blocks[index ^ bit] + arrived.astype(F32)
        bit *= 2
    return blocks[0]


def halves(blocks):
    middle = len(blocks) // 2
    return (jnp.concatenate(blocks[:middle], 0), jnp.concatenate(blocks[middle:], 0))


def scatter_halves(low, high, rows):
    count = low.shape[0] // rows
    cut = [low[i * rows : (i + 1) * rows] for i in range(count)]
    return scatter_ctx(cut + [high[i * rows : (i + 1) * rows] for i in range(count)])


def norm_parts(values):
    center = values - jnp.mean(values, axis=-1, keepdims=True)
    rate = lax.rsqrt(jnp.mean(center * center, axis=-1, keepdims=True) + 1e-05)
    return center * rate, rate


def norm_back(hat, rate, gain, grad):
    scaled = grad * gain
    inner = jnp.mean(scaled * hat, axis=-1, keepdims=True)
    result = rate * (scaled - jnp.mean(scaled, axis=-1, keepdims=True) - hat * inner)
    return result, jnp.sum(grad * hat, axis=0), jnp.sum(grad, axis=0)


def gelu_back(values, grad):
    unused, pullback = jax.vjp(lambda u: jax.nn.gelu(u, approximate=True), values)
    return pullback(grad)[0]


def split_heads(block, heads, head):
    wide = block.astype(F32)
    lane = lax.broadcasted_iota(jnp.int32, wide.shape, 1) // head
    parts = [jnp.where(lane == h, wide, 0.0).astype(BF) for h in range(heads)]
    return jnp.concatenate(parts, 0)


def spread(row, heads):
    return jnp.concatenate([row] * heads, 1)


def allowed_keys(first, chunk, low, high):
    index = first + lax.broadcasted_iota(jnp.int32, (chunk, low.shape[1]), 0)
    return (index >= low) & (index < high)


def forward_kernel(meta, q_ref, k_ref, v_ref, rows_ref, o_ref, lse_ref, top, total, mixed, *, heads, head, chunk, count, offset):
    block = pl.program_id(0) + offset
    queries = q_ref.shape[0]
    split = split_heads(q_ref[...].astype(F32) * 0.125, heads, head)
    low = spread(rows_ref[0, 0:1, :], heads)
    high = spread(rows_ref[0, 1:2, :], heads)
    top[...] = jnp.full_like(top, -1e30)
    total[...] = jnp.zeros_like(total)
    mixed[...] = jnp.zeros_like(mixed)

    def step(index, carry):
        start = pl.multiple_of((index ^ meta[0]) * chunk, chunk)
        keys = k_ref[pl.ds(start, chunk), :]
        values = jnp.transpose(v_ref[pl.ds(start, chunk), :])
        scores = dot_right(keys, split)
        scores = jnp.where(allowed_keys(index * chunk, chunk, low, high), scores, -1e30)
        before = top[...]
        now = jnp.maximum(before, jnp.max(scores, axis=0, keepdims=True))
        decay = jnp.exp(before - now)
        weight = jnp.exp(scores - now)
        top[...] = now
        total[...] = total[...] * decay + jnp.sum(weight, axis=0, keepdims=True)
        weight = weight.astype(BF)
        for h in range(heads):
            rows, cols = slice(h * head, (h + 1) * head), slice(h * queries, (h + 1) * queries)
            mixed[rows, :] = mixed[rows, :] * decay[:, cols] + dot(values[rows, :], weight[:, cols])
        return carry

    lax.fori_loop(meta[1 + block], meta[1 + count + block], step, 0)
    amount = total[...]
    for h in range(heads):
        rows, cols = slice(h * head, (h + 1) * head), slice(h * queries, (h + 1) * queries)
        mixed[rows, :] = mixed[rows, :] / amount[:, cols]
    o_ref[...] = jnp.transpose(mixed[...]).astype(BF)
    lse_ref[0] = top[...] + jnp.log(amount)


def backward_kernel(meta, q_ref, g_ref, o_ref, lse_ref, rows_ref, k_ref, v_ref, dq_ref, dk_ref, dv_ref, dq_sum, *, heads, head, chunk, count, offset):
    block = pl.program_id(0) + offset
    queries = q_ref.shape[0]

    @pl.when(pl.program_id(0) == 0)
    def _():
        dk_ref[...] = jnp.zeros_like(dk_ref)
        dv_ref[...] = jnp.zeros_like(dv_ref)

    split = split_heads(q_ref[...].astype(F32) * 0.125, heads, head)
    grads = split_heads(g_ref[...], heads, head)
    low = spread(rows_ref[0, 0:1, :], heads)
    high = spread(rows_ref[0, 1:2, :], heads)
    lse = lse_ref[0]
    product = jnp.transpose(g_ref[...].astype(F32) * o_ref[...].astype(F32))
    inner = jnp.concatenate(
        [jnp.sum(product[h * head : (h + 1) * head], axis=0, keepdims=True) for h in range(heads)], 1
    )
    dq_sum[...] = jnp.zeros_like(dq_sum)

    def step(index, carry):
        start = pl.multiple_of((index ^ meta[0]) * chunk, chunk)
        keys = k_ref[pl.ds(start, chunk), :]
        scores = dot_right(keys, split)
        scores = jnp.where(allowed_keys(index * chunk, chunk, low, high), scores, -1e30)
        weight = jnp.exp(scores - lse)
        slope = dot_right(v_ref[pl.ds(start, chunk), :], grads)
        slope = (weight * (slope - inner)).astype(BF)
        dv_ref[pl.ds(start, chunk), :] += dot(weight.astype(BF), grads)
        dk_ref[pl.ds(start, chunk), :] += dot(slope, split)
        turned = jnp.transpose(keys)
        for h in range(heads):
            rows, cols = slice(h * head, (h + 1) * head), slice(h * queries, (h + 1) * queries)
            dq_sum[rows, :] += dot(turned[rows, :], slope[:, cols])
        return carry

    lax.fori_loop(meta[1 + block], meta[1 + count + block], step, 0)
    dq_ref[...] = (jnp.transpose(dq_sum[...]) * 0.125).astype(BF)


class Attention:
    def __init__(self, low, high, tile, chunk, flip):
        self.tile, self.chunk = tile, chunk
        self.count = low.shape[0] // tile
        low, high = low.reshape(self.count, tile), high.reshape(self.count, tile)
        self.rows = jnp.stack([low, high], 1)
        first, last = jnp.min(low, 1) // chunk, (jnp.max(high, 1) - 1) // chunk + 1
        self.meta = jnp.concatenate([flip.reshape(1), first, last]).astype(jnp.int32)

    def specs(self, width, heads, offset, queries_at):
        tile = self.tile
        tall = pl.BlockSpec((tile, width), lambda i, m: (i + queries_at, 0))
        rows = pl.BlockSpec((1, 2, tile), lambda i, m: (i + offset, 0, 0))
        return tall, rows

    def forward(self, queries, keys, values, offset, steps, queries_at):
        width, heads = queries.shape[1], queries.shape[1] // HEAD
        tall, rows = self.specs(width, heads, offset, queries_at)
        whole = pl.BlockSpec(keys.shape, lambda i, m: (0, 0))
        lanes = heads * self.tile
        body = functools.partial(
            forward_kernel, heads=heads, head=HEAD, chunk=self.chunk, count=self.count, offset=offset
        )
        pairs = steps * self.tile * keys.shape[0] * heads
        return pl.pallas_call(
            body,
            grid_spec=pltpu.PrefetchScalarGridSpec(
                num_scalar_prefetch=1,
                grid=(steps,),
                in_specs=[tall, whole, whole, rows],
                out_specs=[
                    pl.BlockSpec((self.tile, width), lambda i, m: (i, 0)),
                    pl.BlockSpec((1, 1, lanes), lambda i, m: (i, 0, 0)),
                ],
                scratch_shapes=[
                    pltpu.VMEM((1, lanes), F32),
                    pltpu.VMEM((1, lanes), F32),
                    pltpu.VMEM((width, self.tile), F32),
                ],
            ),
            out_shape=[
                jax.ShapeDtypeStruct((steps * self.tile, width), BF),
                jax.ShapeDtypeStruct((steps, 1, lanes), F32),
            ],
            cost_estimate=pl.CostEstimate(flops=pairs * 256, transcendentals=pairs // 2, bytes_accessed=2 << 20),
            compiler_params=pltpu.CompilerParams(vmem_limit_bytes=24 << 20),
        )(self.meta, queries, keys, values, self.rows)

    def backward(self, queries, grads, mixed, lse, keys, values, offset, steps, queries_at):
        width, heads = queries.shape[1], queries.shape[1] // HEAD
        tall, rows = self.specs(width, heads, offset, queries_at)
        near = pl.BlockSpec((self.tile, width), lambda i, m: (i, 0))
        whole = pl.BlockSpec(keys.shape, lambda i, m: (0, 0))
        lanes = heads * self.tile
        body = functools.partial(
            backward_kernel, heads=heads, head=HEAD, chunk=self.chunk, count=self.count, offset=offset
        )
        pairs = steps * self.tile * keys.shape[0] * heads
        return pl.pallas_call(
            body,
            grid_spec=pltpu.PrefetchScalarGridSpec(
                num_scalar_prefetch=1,
                grid=(steps,),
                in_specs=[tall, near, near, pl.BlockSpec((1, 1, lanes), lambda i, m: (i, 0, 0)), rows, whole, whole],
                out_specs=[near, whole, whole],
                scratch_shapes=[pltpu.VMEM((width, self.tile), F32)],
            ),
            out_shape=[
                jax.ShapeDtypeStruct((steps * self.tile, width), BF),
                jax.ShapeDtypeStruct(keys.shape, F32),
                jax.ShapeDtypeStruct(keys.shape, F32),
            ],
            cost_estimate=pl.CostEstimate(flops=pairs * 640, transcendentals=pairs // 2, bytes_accessed=4 << 20),
            compiler_params=pltpu.CompilerParams(vmem_limit_bytes=32 << 20),
        )(self.meta, queries, grads, mixed, lse, self.rows, keys, values)


def gather_wsh(part):
    return lax.all_gather(part, "wsh", axis=0, tiled=True)


def scatter_wsh(whole):
    return lax.psum_scatter(whole.astype(BF), "wsh", scatter_dimension=0, tiled=True)


def piece_moves(groups, size):
    return [((g % size) * groups + g // size, g) for g in range(groups * size)]


def plain_body(
    inputs,
    enc_states,
    cotangent,
    slot_order,
    seq_lengths,
    enc_lengths,
    self_query,
    self_key,
    self_value,
    self_out,
    cross_query,
    cross_key,
    cross_value,
    cross_out,
    feed_in,
    feed_out,
    norm_gains,
    norm_shifts,
):
    size, groups = lax.axis_size("ctx"), lax.axis_size("wsh")
    mine, row = lax.axis_index("ctx"), lax.axis_index("wsh")
    slots = inputs.shape[1]
    total = slots * size
    enc_slots = enc_states.shape[1]
    width = inputs.shape[2]
    rows = self_query.shape[0]
    cols = width // size
    piece = rows // size
    ff_cols = feed_in.shape[1] // size
    ff_rows = feed_out.shape[0] // size

    def columns(matrix):
        return lax.dynamic_slice_in_dim(matrix, mine * cols, cols, 1)

    norms = jnp.concatenate([norm_gains, norm_shifts, jnp.zeros((rows, 120), BF)], 1)
    self_full = gather_wsh(jnp.concatenate([columns(self_query), columns(self_key), columns(self_value), norms], 1))
    q_full, k_full, v_full = (self_full[:, i * cols : (i + 1) * cols] for i in range(3))
    norm_rows = jnp.transpose(self_full[:, 3 * cols : 3 * cols + 8].astype(F32))
    gains, shifts = norm_rows[:4, None, :], norm_rows[4:, None, :]

    def out_piece(matrix):
        return lax.dynamic_slice_in_dim(matrix, mine * piece, piece, 0)

    pieces = jnp.concatenate([out_piece(self_out), out_piece(cross_out)], 0)
    pieces = lax.ppermute(pieces, ("ctx", "wsh"), piece_moves(groups, size))
    pieces = gather_wsh(pieces).reshape(groups, 2, piece, width)
    out_full, cross_o_full = pieces[:, 0].reshape(cols, width), pieces[:, 1].reshape(cols, width)
    cross_full = gather_wsh(jnp.concatenate([columns(cross_query), columns(cross_key), columns(cross_value)], 1))
    cq_full, ck_full, cv_full = (cross_full[:, i * cols : (i + 1) * cols] for i in range(3))
    first_part = lax.dynamic_slice_in_dim(feed_in.reshape(rows, groups, size, ff_rows), mine, 1, 2)
    second_part = lax.dynamic_slice_in_dim(feed_out, mine * ff_rows, ff_rows, 0)
    feed = jnp.concatenate([first_part.reshape(rows, ff_cols), second_part.reshape(rows, ff_cols)], 0)
    feed = gather_wsh(feed).reshape(groups, 2, rows, ff_cols)
    first_full = feed[:, 0].reshape(groups * rows, ff_cols)
    second_full = feed[:, 1].reshape(groups * ff_rows, width)

    relative = jnp.arange(size, dtype=jnp.int32) ^ mine
    order = jnp.take(slot_order[0].reshape(size, slots), relative, axis=0).reshape(total)
    place = (relative[:, None] * slots + jnp.arange(slots, dtype=jnp.int32)).reshape(total)
    lower = jnp.arange(seq_lengths.shape[1])
    lower = lower[None, :] <= lower[:, None]
    ends = jnp.sum(jnp.where(lower, seq_lengths[0][None, :], 0), 1)
    enc_ends = jnp.sum(jnp.where(lower, enc_lengths[0][None, :], 0), 1)
    passed = ends[None, :] <= place[:, None]
    starts = jnp.max(jnp.where(passed, ends[None, :], 0), 1)
    enc_from = jnp.max(jnp.where(passed, enc_ends[None, :], 0), 1)
    enc_to = jnp.min(jnp.where(passed, enc_slots * size, enc_ends[None, :]), 1)
    self_att = Attention(starts, place + 1, 256, 256, mine * (slots // 256))
    cross_att = Attention(enc_from, enc_to, 256, 128, mine * (enc_slots // 128))
    tiles = total // 256
    half = tiles // 2

    to_place = (order[None, :] == place[:, None]).astype(BF)
    to_slot = (order[:slots, None] == place[None, :]).astype(BF)
    tokens_all = jnp.concatenate(gather_ctx(inputs[0]), 0)
    tokens_all = dot(to_place, tokens_all)
    tokens = tokens_all[:slots]
    encoder = jnp.concatenate(gather_ctx(enc_states[0]), 0)
    outside = jnp.concatenate(gather_ctx(cotangent[0]), 0)
    outside = dot(to_place[:slots], outside)

    hat_all, unused = norm_parts(tokens_all)
    normed_one = (hat_all * gains[0] + shifts[0]).astype(BF)
    queries = dot(normed_one, q_full).astype(BF)
    keys = dot(normed_one, k_full).astype(BF)
    values = dot(normed_one, v_full).astype(BF)
    mixed_high, lse_high = self_att.forward(queries, keys, values, half, half, half)
    mixed_low, lse_low = self_att.forward(queries, keys, values, 0, half, 0)
    after_self = tokens + scatter_halves(dot(mixed_low, out_full), dot(mixed_high, out_full), slots)

    hat_two, rate_two = norm_parts(after_self)
    normed_two = halves(gather_ctx((hat_two * gains[1] + shifts[1]).astype(BF)))
    enc_keys = dot(encoder, ck_full).astype(BF)
    enc_values = dot(encoder, cv_full).astype(BF)
    queries_two = [dot(part, cq_full).astype(BF) for part in normed_two]
    mixed_two = [
        cross_att.forward(queries_two[side], enc_keys, enc_values, side * half, half, 0) for side in range(2)
    ]
    after_cross = after_self + scatter_halves(*(dot(part[0], cross_o_full) for part in mixed_two), slots)

    hat_three, rate_three = norm_parts(after_cross)
    normed_three = halves(gather_ctx((hat_three * gains[2] + shifts[2]).astype(BF)))
    pre_act = [dot(part, first_full) for part in normed_three]
    hidden = [jax.nn.gelu(part, approximate=True).astype(BF) for part in pre_act]
    after_ffn = after_cross + scatter_halves(*(dot(part, second_full) for part in hidden), slots)
    hat_four, rate_four = norm_parts(after_ffn)
    result = hat_four * gains[3] + shifts[3]
    result = jnp.concatenate(gather_ctx(result.astype(BF)), 0)
    result = dot(to_slot, result)

    grad_ffn, gain_three, shift_three = norm_back(hat_four, rate_four, gains[3], outside)
    grad_in = halves(gather_ctx(grad_ffn.astype(BF)))
    grad_pre = [
        gelu_back(part, dot_right(grad, second_full)).astype(BF)
        for part, grad in zip(pre_act, grad_in)
    ]
    arrived = scatter_halves(*(dot_right(grad, first_full) for grad in grad_pre), slots)
    norm_part, gain_two, shift_two = norm_back(hat_three, rate_three, gains[2], arrived)
    grad_cross = grad_ffn + norm_part
    grad_first = sum(dot_left(n, g) for n, g in zip(normed_three, grad_pre))
    grad_second = sum(dot_left(n, g) for n, g in zip(hidden, grad_in))
    feed_grads = jnp.concatenate(
        [
            grad_first.astype(BF).reshape(groups, rows, ff_cols),
            grad_second.astype(BF).reshape(groups, rows, ff_cols),
        ],
        1,
    )
    feed_grads = scatter_wsh(feed_grads.reshape(groups * 2 * rows, ff_cols))
    feed_grads = lax.all_gather(feed_grads, "ctx", axis=0).reshape(size, 2, rows, ff_cols)
    feed_in_grad = jnp.transpose(feed_grads[:, 0].reshape(size, rows, groups, ff_rows), (1, 2, 0, 3))
    feed_in_grad = feed_in_grad.reshape(rows, groups * size * ff_rows).astype(F32)
    feed_out_grad = feed_grads[:, 1].reshape(size * ff_rows, width).astype(F32)

    def share(query_grad, key_grad, value_grad, out_grad):
        packed = [
            query_grad.astype(BF),
            key_grad.astype(BF),
            value_grad.astype(BF),
            out_grad.astype(BF).reshape(groups * rows, cols),
        ]
        packed = scatter_wsh(jnp.concatenate(packed, 1))
        moved = packed[:, 3 * cols :].reshape(piece, width)
        moved = lax.ppermute(moved, ("ctx", "wsh"), [(b, a) for a, b in piece_moves(groups, size)])
        packed = jnp.concatenate([packed[:, : 3 * cols], moved.reshape(rows, cols)], 1)
        packed = lax.all_gather(packed, "ctx", axis=0)
        three = [
            jnp.transpose(packed[:, :, i * cols : (i + 1) * cols], (1, 0, 2)).reshape(rows, width).astype(F32)
            for i in range(3)
        ]
        return three + [packed[:, :, 3 * cols :].reshape(size, piece, width).reshape(rows, width).astype(F32)]

    grad_in = halves(gather_ctx(grad_cross.astype(BF)))
    grad_mixed = [dot_right(grad, cross_o_full).astype(BF) for grad in grad_in]
    back = [
        cross_att.backward(
            queries_two[side], grad_mixed[side], *mixed_two[side], enc_keys, enc_values, side * half, half, 0
        )
        for side in range(2)
    ]
    arrived = scatter_halves(*(dot_right(part[0], cq_full) for part in back), slots)
    norm_part, gain_one, shift_one = norm_back(hat_two, rate_two, gains[1], arrived)
    grad_self = grad_cross + norm_part
    grad_ek = (back[0][1] + back[1][1]).astype(BF)
    grad_ev = (back[0][2] + back[1][2]).astype(BF)
    enc_part = dot_right(grad_ek, ck_full) + dot_right(grad_ev, cv_full)
    enc_grad = scatter_ctx([enc_part[i * enc_slots : (i + 1) * enc_slots] for i in range(size)])
    cross_q_grad, cross_k_grad, cross_v_grad, cross_o_grad = share(
        sum(dot_left(n, part[0]) for n, part in zip(normed_two, back)),
        dot_left(encoder, grad_ek),
        dot_left(encoder, grad_ev),
        sum(dot_left(part[0], g) for part, g in zip(mixed_two, grad_in)),
    )

    grad_in = halves(gather_ctx(grad_self.astype(BF)))
    grad_mixed = [dot_right(grad, out_full).astype(BF) for grad in grad_in]
    back_low = self_att.backward(queries, grad_mixed[0], mixed_low, lse_low, keys, values, 0, half, 0)
    back_high = self_att.backward(queries, grad_mixed[1], mixed_high, lse_high, keys, values, half, half, half)
    grad_q = jnp.concatenate([back_low[0], back_high[0]], 0)
    grad_k = (back_low[1] + back_high[1]).astype(BF)
    grad_v = (back_low[2] + back_high[2]).astype(BF)
    arrived = dot_right(grad_q, q_full) + dot_right(grad_k, k_full) + dot_right(grad_v, v_full)
    arrived = scatter_ctx([arrived[i * slots : (i + 1) * slots] for i in range(size)])
    hat_one, rate_one = norm_parts(tokens)
    norm_part, gain_zero, shift_zero = norm_back(hat_one, rate_one, gains[0], arrived)
    input_grad = grad_self + norm_part
    input_grad = jnp.concatenate(gather_ctx(input_grad.astype(BF)), 0)
    input_grad = dot(to_slot, input_grad)
    query_grad, key_grad, value_grad, out_grad = share(
        dot_left(normed_one, grad_q),
        dot_left(normed_one, grad_k),
        dot_left(normed_one, grad_v),
        dot_left(mixed_low, grad_in[0]) + dot_left(mixed_high, grad_in[1]),
    )

    terms = jnp.stack(
        [gain_zero, gain_one, gain_two, gain_three, shift_zero, shift_one, shift_two, shift_three], 0
    )
    for axis, amount in (("ctx", size), ("wsh", groups)):
        bit = 1
        while bit < amount:
            terms = terms + swap(terms, axis, bit)
            bit *= 2
    terms = jnp.transpose(lax.dynamic_slice_in_dim(terms, row * rows, rows, 1))
    return (
        result[None],
        input_grad[None],
        enc_grad[None],
        query_grad,
        key_grad,
        value_grad,
        out_grad,
        cross_q_grad,
        cross_k_grad,
        cross_v_grad,
        cross_o_grad,
        feed_in_grad,
        feed_out_grad,
        terms[:, :4],
        terms[:, 4:],
    )


SMALL = pl.CostEstimate(flops=1 << 20, transcendentals=0, bytes_accessed=1 << 16)


def call(kernel, outs, scalars, *operands, scratch=(), aliases=None, vmem=12, space=pltpu.VMEM, out_space=pltpu.VMEM):
    specs = [pl.BlockSpec(memory_space=pltpu.SMEM)] * len(scalars)
    specs += [pl.BlockSpec(memory_space=space)] * len(operands)
    return pl.pallas_call(
        kernel,
        in_specs=specs,
        out_specs=[pl.BlockSpec(memory_space=out_space)] * len(outs),
        out_shape=[jax.ShapeDtypeStruct(shape, kind) for shape, kind in outs],
        scratch_shapes=list(scratch),
        input_output_aliases=aliases or {},
        cost_estimate=SMALL,
        compiler_params=pltpu.CompilerParams(vmem_limit_bytes=vmem << 20),
    )(*scalars, *operands)


def call_packing(kernel, outs, *operands):
    scratch = [pltpu.VMEM(operand.shape, operand.dtype) for operand in operands]
    count = len(operands)

    def fetching(*refs):
        sources, outs, held, done = refs[:count], refs[count : -count - 1], refs[-count - 1 : -1], refs[-1]
        copies = [pltpu.make_async_copy(sources[i], held[i], done.at[i]) for i in range(count)]
        for copy in copies:
            copy.start()
        for copy in copies:
            copy.wait()
        kernel(*held, *outs)

    operands = [pltpu.with_memory_space_constraint(operand, pltpu.HBM) for operand in operands]
    scratch.append(pltpu.SemaphoreType.DMA((count,)))
    return call(fetching, outs, (), *operands, scratch=scratch, space=pltpu.HBM)


def call_streaming(kernel, out, steps, *operands, vmem=20):
    shape, kind = out
    part = shape[0] // steps

    def streaming(*refs):
        *sources, out_ref, held, done = refs

        def copy(index):
            at = pl.ds(index * part, part)
            return pltpu.make_async_copy(held.at[at], out_ref.at[at], done.at[index])

        kernel(*sources, held, lambda index: copy(index).start())
        for index in range(steps):
            copy(index).wait()

    scratch = [pltpu.VMEM(shape, kind), pltpu.SemaphoreType.DMA((steps,))]
    return call(streaming, [out], (), *operands, scratch=scratch, vmem=vmem, out_space=pltpu.HBM)[0]


def one_hot(hit):
    return jnp.where(hit, 1.0, 0.0).astype(BF)


def ctx_part(size):
    return pl.ds(pl.multiple_of(lax.axis_index("ctx") * size, size), size)


def my_heads(matrix, size):
    cols = matrix.shape[1] // size
    heads = cols // HEAD
    span = HEAD * size
    source = lax.broadcasted_iota(jnp.int32, (span, cols), 0) - lax.axis_index("ctx") * HEAD
    target = lax.broadcasted_iota(jnp.int32, (span, cols), 1)
    total = None
    for head in range(heads):
        part = dot(matrix[:, head * span : (head + 1) * span], one_hot((source >= 0) & (source < HEAD) & (source == target - head * HEAD)))
        total = part if total is None else total + part
    return total.astype(BF)


def give_pieces_kernel(one, two, out_ref):
    piece = out_ref.shape[0] // 2
    start = pl.multiple_of((lax.axis_index("ctx") % 2) * 2 * piece + piece, piece)
    out_ref[:piece, :] = one[pl.ds(start, piece), :]
    out_ref[piece:, :] = two[pl.ds(start, piece), :]


def my_piece(matrix, given, which):
    piece = given.shape[0] // 2
    mine = lax.axis_index("ctx")
    start = pl.multiple_of((mine % 2) * 2 * piece, piece)
    own = matrix[pl.ds(start, piece), :].astype(F32)
    other = given[which * piece : (which + 1) * piece, :].astype(F32)
    same = lax.axis_index("wsh") % 2 == mine // 2
    return jnp.where(same, own, other).astype(BF)


def pack_kernel(wq, wk, wv, wo, given, *refs, size, which):
    *norm_refs, out_ref = refs
    rows, cols = wq.shape[0], out_ref.shape[1]
    for part, full in enumerate((wq, wk, wv)):
        out_ref[part * rows : (part + 1) * rows, :] = my_heads(full, size)
    taken = my_piece(wo, given, which)
    piece = taken.shape[0]
    for chunk in range(taken.shape[1] // cols):
        at = 3 * rows + chunk * piece
        out_ref[at : at + piece, :] = taken[:, chunk * cols : (chunk + 1) * cols]
    if norm_refs:
        gains, shifts = norm_refs
        norms = jnp.concatenate([gains[...], shifts[...]], 0).astype(F32)
        norms = jnp.concatenate([norms, jnp.zeros((8, rows), F32)], 0)
        norms = jnp.concatenate([norms, jnp.zeros((16, cols - rows), F32)], 1)
        out_ref[out_ref.shape[0] - 16 :, :] = norms.astype(BF)


def pack_feed_kernel(first, second, out_ref, groups, size):
    rows, width = first.shape[0], first.shape[1] // groups
    cols = width // size
    mine = lax.axis_index("ctx")
    for group in range(groups):
        at = pl.ds(pl.multiple_of(group * width + mine * cols, cols), cols)
        out_ref[:rows, group * cols : (group + 1) * cols] = first[:, at]
    out_ref[rows:, :] = second[ctx_part(cols), :]


def sort_kernel(order_ref, *refs, size):
    sources, (hat_ref, own_ref) = refs[:size], refs[size:]
    slots = sources[0].shape[0]
    mine = lax.axis_index("ctx")

    def block(index, carry):
        base = (mine ^ index) * slots
        total = jnp.zeros(own_ref.shape, F32)
        for source in range(size):
            order = order_ref[:, source * slots : (source + 1) * slots]
            place = base + lax.broadcasted_iota(jnp.int32, (slots, slots), 0)
            total += dot(one_hot(order == place), sources[source][...])

        @pl.when(index == 0)
        def _():
            own_ref[...] = total

        hat, unused = norm_parts(total)
        hat_ref[pl.ds(pl.multiple_of(index * slots, slots), slots), :] = hat
        return carry

    lax.fori_loop(0, size, block, 0)


def pick_kernel(order_ref, *refs, size):
    sources, out_ref = refs[:size], refs[size]
    slots = sources[0].shape[0]
    base = lax.axis_index("ctx") * slots
    def columns(tile, carry):
        lanes = pl.ds(pl.multiple_of(tile * 256, 256), 256)
        total = jnp.zeros((slots, 256), F32)
        for source in range(size):
            order = order_ref[:, source * slots : (source + 1) * slots]
            place = base + lax.broadcasted_iota(jnp.int32, (slots, slots), 0)
            total += dot(one_hot(order == place), sources[source][:, lanes])
        out_ref[:, lanes] = total
        return carry

    lax.fori_loop(0, out_ref.shape[1] // 256, columns, 0)


def unsort_kernel(order_ref, *refs, size):
    count = len(refs) - 1 if len(refs) % size == 1 else len(refs) - 2
    sources, out_ref = refs[:count], refs[count]
    slots = out_ref.shape[0]
    pieces = count // size
    length = slots // pieces
    mine = lax.axis_index("ctx")

    def columns(tile, carry):
        lanes = pl.ds(pl.multiple_of(tile * 256, 256), 256)
        total = jnp.zeros((slots, 256), F32)
        for index, source in enumerate(sources):
            first = (mine ^ (index // pieces)) * slots + (index % pieces) * length
            place = first + lax.broadcasted_iota(jnp.int32, (slots, length), 1)
            total += dot(one_hot(order_ref[...] == place), source[:length, lanes])
        out_ref[:, lanes] = total
        return carry

    lax.fori_loop(0, out_ref.shape[1] // 256, columns, 0)
    if count + 1 < len(refs):
        refs[count + 1][...] = sum(source[slots:, :].astype(F32) for source in sources)


def wsh_rows(index, rows):
    target = (lax.axis_index("wsh") ^ index) * rows
    return pl.ds(pl.multiple_of(target, rows), rows)


def piece_rows(index, piece):
    target = lax.axis_index("wsh") ^ index ^ (lax.axis_index("ctx") // 2)
    return pl.ds(pl.multiple_of(target * piece, piece), piece)


def place_attention(blocks, wq, wk, wv, wo, rows, piece):
    for index, block in enumerate(blocks):
        for part, full in enumerate((wq, wk, wv)):
            full[wsh_rows(index, rows), :] = block[part * rows : (part + 1) * rows, :]
        cols = block.shape[1]
        for chunk in range(wo.shape[1] // cols):
            at = 3 * rows + chunk * piece
            wo[piece_rows(index, piece), chunk * cols : (chunk + 1) * cols] = block[at : at + piece, :]


def project_kernel(hat_ref, *refs, groups, rows, piece):
    blocks = refs[:groups]
    wq, wk, wv, wo, norms, normed_ref, q_ref, k_ref, v_ref = refs[groups:]
    place_attention(blocks, wq, wk, wv, wo, rows, piece)
    for index, block in enumerate(blocks):
        last = block.shape[0] - 16
        norms[:, wsh_rows(index, rows)] = block[last:, :rows].astype(F32)[:8]
    tile = 256

    def step(index, carry):
        at = pl.ds(pl.multiple_of(index * tile, tile), tile)
        normed = (hat_ref[at, :] * norms[0:1, :] + norms[4:5, :]).astype(BF)
        normed_ref[at, :] = normed
        for full, out in ((wq, q_ref), (wk, k_ref), (wv, v_ref)):
            out[at, :] = dot(normed, full[...]).astype(BF)
        return carry

    lax.fori_loop(0, hat_ref.shape[0] // tile, step, 0)


def cross_prepare_kernel(blocks, *refs, size, rows, piece):
    encoder = refs[:size]
    wq, wk, wv, wo, key_ref, value_ref = refs[size:]
    groups, cols = blocks.shape[0], blocks.shape[2]
    for index in range(groups):
        for part, full in enumerate((wq, wk, wv)):
            full[index * rows : (index + 1) * rows, :] = blocks[index, part * rows : (part + 1) * rows, :]
        target = (index ^ (lax.axis_index("ctx") // 2)) * piece
        there = pl.ds(pl.multiple_of(target, piece), piece)
        for chunk in range(wo.shape[1] // cols):
            at = 3 * rows + chunk * piece
            wo[there, chunk * cols : (chunk + 1) * cols] = blocks[index, at : at + piece, :]
    slots = encoder[0].shape[0]
    for index, part in enumerate(encoder):
        at = slice(index * slots, (index + 1) * slots)
        key_ref[at, :] = dot(part[...], wk[...]).astype(BF)
        value_ref[at, :] = dot(part[...], wv[...]).astype(BF)


def attend(split, low, high, first, last, flip, k_ref, v_ref, top, total, mixed, heads, chunk):
    tile = mixed.shape[1]
    top[...] = jnp.full_like(top, -1e30)
    total[...] = jnp.zeros_like(total)
    mixed[...] = jnp.zeros_like(mixed)

    def step(index, carry):
        start = pl.multiple_of((index ^ flip) * chunk, chunk)
        keys = k_ref[pl.ds(start, chunk), :]
        values = jnp.transpose(v_ref[pl.ds(start, chunk), :])
        scores = dot_right(keys, split)
        scores = jnp.where(allowed_keys(index * chunk, chunk, low, high), scores, -1e30)
        before = top[...]
        now = jnp.maximum(before, jnp.max(scores, axis=0, keepdims=True))
        decay = jnp.exp(before - now)
        weight = jnp.exp(scores - now)
        top[...] = now
        total[...] = total[...] * decay + jnp.sum(weight, axis=0, keepdims=True)
        weight = weight.astype(BF)
        for h in range(heads):
            rows, cols = slice(h * HEAD, (h + 1) * HEAD), slice(h * tile, (h + 1) * tile)
            mixed[rows, :] = mixed[rows, :] * decay[:, cols] + dot(values[rows, :], weight[:, cols])
        return carry

    lax.fori_loop(first, last, step, 0)
    amount = total[...]
    for h in range(heads):
        rows, cols = slice(h * HEAD, (h + 1) * HEAD), slice(h * tile, (h + 1) * tile)
        mixed[rows, :] = mixed[rows, :] / amount[:, cols]
    return top[...] + jnp.log(amount)


def attend_forward_kernel(meta, *refs, own_queries, parts, offset, count, chunk):
    if own_queries:
        sources, wq = refs[:parts], refs[parts]
        k_ref, v_ref, rows_ref, wo, q_ref, mixed_ref, lse_ref = refs[parts + 1 : parts + 8]
        rest = refs[parts + 8 :]
        for index, source in enumerate(sources):
            slots = source.shape[0]
            q_ref[index * slots : (index + 1) * slots, :] = dot(source[...], wq[...]).astype(BF)
        shift = 0
    else:
        q_ref, k_ref, v_ref, rows_ref, wo, mixed_ref, lse_ref = refs[:7]
        rest = refs[7:]
        shift = offset
    outs, (top, total, mixed) = rest[:parts], rest[parts:]
    tile = mixed.shape[1]
    heads = q_ref.shape[1] // HEAD

    def block(index, carry):
        at = pl.ds(pl.multiple_of((index + shift) * tile, tile), tile)
        split = split_heads(q_ref[at, :].astype(F32) * 0.125, heads, HEAD)
        low = spread(rows_ref[index + offset, 0:1, :], heads)
        high = spread(rows_ref[index + offset, 1:2, :], heads)
        first, last = meta[1 + index + offset], meta[1 + count + index + offset]
        lse_ref[index] = attend(split, low, high, first, last, meta[0], k_ref, v_ref, top, total, mixed, heads, chunk)
        here = pl.ds(pl.multiple_of(index * tile, tile), tile)
        mixed_ref[here, :] = jnp.transpose(mixed[...]).astype(BF)
        return carry

    lax.fori_loop(0, mixed_ref.shape[0] // tile, block, 0)
    for index, out in enumerate(outs):
        slots = out.shape[0]
        out[...] = dot(mixed_ref[index * slots : (index + 1) * slots, :], wo[...]).astype(BF)


def attend_backward_kernel(meta, *refs, own_queries, parts, offset, count, chunk, fresh):
    sources = refs[:parts]
    q_ref, mixed_ref, lse_ref, rows_ref, k_ref, v_ref, wo = refs[parts : parts + 7]
    rest = refs[parts + 7 :]
    if own_queries:
        wq, rest = rest[0], rest[1:]
    if not fresh:
        rest = rest[3:]
    dq_ref, dk_ref, dv_ref, dwo_ref = rest[:4]
    outs = rest[4 : 4 + parts] if own_queries else ()
    grad_ref, dq_sum = rest[-2:]
    tile = dq_sum.shape[1]
    heads = q_ref.shape[1] // HEAD
    shift = 0 if own_queries else offset
    if fresh:
        dk_ref[...] = jnp.zeros_like(dk_ref)
        dv_ref[...] = jnp.zeros_like(dv_ref)
    change = None
    for index, source in enumerate(sources):
        slots = source.shape[0]
        at = slice(index * slots, (index + 1) * slots)
        grad_ref[at, :] = dot_right(source[...], wo[...]).astype(BF)
        part = dot_left(mixed_ref[at, :], source[...])
        change = part if change is None else change + part
    dwo_ref[...] = change if fresh else dwo_ref[...] + change

    def block(index, carry):
        at = pl.ds(pl.multiple_of((index + shift) * tile, tile), tile)
        here = pl.ds(pl.multiple_of(index * tile, tile), tile)
        split = split_heads(q_ref[at, :].astype(F32) * 0.125, heads, HEAD)
        grads = split_heads(grad_ref[here, :], heads, HEAD)
        low = spread(rows_ref[index + offset, 0:1, :], heads)
        high = spread(rows_ref[index + offset, 1:2, :], heads)
        lse = lse_ref[index]
        product = jnp.transpose(grad_ref[here, :].astype(F32) * mixed_ref[here, :].astype(F32))
        inner = jnp.concatenate(
            [jnp.sum(product[h * HEAD : (h + 1) * HEAD], axis=0, keepdims=True) for h in range(heads)], 1
        )
        dq_sum[...] = jnp.zeros_like(dq_sum)

        def step(number, carry):
            start = pl.multiple_of((number ^ meta[0]) * chunk, chunk)
            keys = k_ref[pl.ds(start, chunk), :]
            scores = dot_right(keys, split)
            scores = jnp.where(allowed_keys(number * chunk, chunk, low, high), scores, -1e30)
            weight = jnp.exp(scores - lse)
            slope = dot_right(v_ref[pl.ds(start, chunk), :], grads)
            slope = (weight * (slope - inner)).astype(BF)
            dv_ref[pl.ds(start, chunk), :] += dot(weight.astype(BF), grads)
            dk_ref[pl.ds(start, chunk), :] += dot(slope, split)
            turned = jnp.transpose(keys)
            for h in range(heads):
                rows, cols = slice(h * HEAD, (h + 1) * HEAD), slice(h * tile, (h + 1) * tile)
                dq_sum[rows, :] += dot(turned[rows, :], slope[:, cols])
            return carry

        lax.fori_loop(meta[1 + index + offset], meta[1 + count + index + offset], step, 0)
        dq_ref[here, :] = (jnp.transpose(dq_sum[...]) * 0.125).astype(BF)
        return carry

    lax.fori_loop(0, dq_ref.shape[0] // tile, block, 0)
    for index, out in enumerate(outs):
        slots = out.shape[0]
        out[...] = dot_right(dq_ref[index * slots : (index + 1) * slots, :], wq[...]).astype(BF)


def total_of(base, parts):
    value = base[...]
    for part in parts:
        value = value + part[...].astype(F32)
    return value


def norm_kernel(norms, base, *refs, which):
    parts, (sum_ref, normed_ref) = refs[:-2], refs[-2:]
    value = total_of(base, parts)
    sum_ref[...] = value
    hat, unused = norm_parts(value)
    normed_ref[...] = (hat * norms[which : which + 1, :] + norms[4 + which : 5 + which, :]).astype(BF)


def norm_back_kernel(norms, value_ref, grad_ref, *refs, which):
    parts, (out_ref, sent_ref, terms_ref) = refs[:-3], refs[-3:]
    hat, rate = norm_parts(value_ref[...])
    grad = parts[0][...].astype(F32)
    for part in parts[1:]:
        grad = grad + part[...].astype(F32)
    change, gain, shift = norm_back(hat, rate, norms[which : which + 1, :], grad)
    result = grad_ref[...] + change
    out_ref[...] = result
    sent_ref[...] = result.astype(BF)
    terms_ref[0:1, :] = gain[None]
    terms_ref[1:2, :] = shift[None]


def norm_first_kernel(norms, value_ref, grad_ref, near, other, far, one, two, three, sent_ref):
    slots = value_ref.shape[0]
    hat, rate = norm_parts(value_ref[...])
    grad = near[...].astype(F32) + other[...].astype(F32) + far[...].astype(F32)
    change, gain, shift = norm_back(hat, rate, norms[0:1, :], grad)
    sent_ref[:slots, :] = (grad_ref[...] + change).astype(BF)
    sums = [gain[None], shift[None], one[...], two[...], three[...], jnp.zeros((8, gain.shape[0]), F32)]
    sent_ref[slots:, :] = jnp.concatenate(sums, 0).astype(BF)


def norm_turn_kernel(norms, base, outside, *refs):
    parts, (low_ref, high_ref, out_ref, sent_ref, terms_ref) = refs[:-5], refs[-5:]
    hat, rate = norm_parts(total_of(base, parts))
    result = (hat * norms[3:4, :] + norms[7:8, :]).astype(BF)
    low_ref[...] = result[: low_ref.shape[0]]
    high_ref[...] = result[low_ref.shape[0] :]
    change, gain, shift = norm_back(hat, rate, norms[3:4, :], outside[...])
    out_ref[...] = change
    sent_ref[...] = change.astype(BF)
    terms_ref[0:1, :] = gain[None]
    terms_ref[1:2, :] = shift[None]


def feed_tile(feed, part, tile):
    groups, rows = feed.shape[0], feed.shape[1] // 2
    block = feed[:, part * rows : (part + 1) * rows, pl.ds(pl.multiple_of(tile * 256, 256), 256)]
    return block.reshape(groups * rows, 256)


def feed_forward_kernel(*refs, parts):
    sources, (feed, hidden_ref, slope_ref), outs = refs[:parts], refs[parts : parts + 3], refs[parts + 3 :]
    rate = 0.7978845608028654
    tiles = feed.shape[2] // 256
    for index, (source, out) in enumerate(zip(sources, outs)):
        slots = source.shape[0]
        at = slice(index * slots, (index + 1) * slots)

        def first(tile, carry):
            lanes = pl.ds(pl.multiple_of(tile * 256, 256), 256)
            pre = dot(source[...], feed_tile(feed, 0, tile))
            square = pre * pre
            bend = jnp.tanh(rate * pre * (1.0 + 0.044715 * square))
            half = 0.5 * (1.0 + bend)
            slope = half + 0.5 * pre * (1.0 - bend * bend) * rate * (1.0 + 0.134145 * square)
            slope_ref[at, lanes] = slope.astype(BF)
            hidden_ref[at, lanes] = (pre * half).astype(BF)
            return carry

        def second(tile, carry):
            lanes = pl.ds(pl.multiple_of(tile * 256, 256), 256)
            out[:, lanes] = dot(hidden_ref[at, :], feed_tile(feed, 1, tile)).astype(BF)
            return carry

        lax.fori_loop(0, tiles, first, 0)
        lax.fori_loop(0, tiles, second, 0)


def feed_rows(feed, part, tile):
    rows = feed.shape[1] // 2
    count = 256 // rows
    block = feed[pl.ds(tile * count, count), part * rows : (part + 1) * rows, :]
    return block.reshape(256, feed.shape[2])


def feed_backward_kernel(*refs, parts):
    sources, (feed, slope_ref, change_ref), outs = refs[:parts], refs[parts : parts + 3], refs[parts + 3 :]
    tiles = feed.shape[0] * feed.shape[1] // 512
    for index, (source, out) in enumerate(zip(sources, outs)):
        slots = source.shape[0]
        at = slice(index * slots, (index + 1) * slots)

        def second(tile, carry):
            lanes = pl.ds(pl.multiple_of(tile * 256, 256), 256)
            change = dot_right(source[...], feed_rows(feed, 1, tile)) * slope_ref[at, lanes].astype(F32)
            change_ref[at, lanes] = change.astype(BF)
            return carry

        def first(tile, carry):
            lanes = pl.ds(pl.multiple_of(tile * 256, 256), 256)
            out[:, lanes] = dot_right(change_ref[at, :], feed_rows(feed, 0, tile)).astype(BF)
            return carry

        lax.fori_loop(0, tiles, second, 0)
        lax.fori_loop(0, tiles, first, 0)


def feed_grad_kernel(*refs, size, rows):
    normed, (change_low, change_high, hidden_low, hidden_high) = refs[:size], refs[size : size + 4]
    grads, (out_ref, send) = refs[size + 4 : 2 * size + 4], refs[-2:]
    middle, slots = size // 2, normed[0].shape[0]
    wide = 2 * rows

    def step(index, carry):
        lanes = pl.ds(pl.multiple_of(index * wide, wide), wide)
        first, second = None, None
        for block in range(size):
            side, at = block // middle, (block % middle) * slots
            change = (change_low, change_high)[side][at : at + slots, :]
            hidden = (hidden_low, hidden_high)[side][at : at + slots, lanes]
            one = dot_left(normed[block][:, lanes], change)
            two = dot_left(hidden, grads[block][...])
            first, second = (one, two) if first is None else (first + one, second + two)
        for part in range(2):
            at = slice(part * rows, (part + 1) * rows)
            out_ref[2 * index + part, 0:rows, :] = first[at, :].astype(BF)
            out_ref[2 * index + part, rows : 2 * rows, :] = second[at, :].astype(BF)
        send(index)
        return carry

    lax.fori_loop(0, out_ref.shape[0] // 2, step, 0)


def weight_grad_kernel(*refs, terms, odd, rows, piece, count):
    operands, extra, outs, held = refs[: -count - 2], refs[-count - 2], refs[-count - 1 : -1], refs[-1]
    height, cols = outs[0].shape
    mine = lax.axis_index("wsh")

    def step(index, carry):
        target = mine ^ (2 * index + odd)
        lanes = pl.ds(pl.multiple_of(target * rows, rows), rows)
        for part in range(3):
            value = None
            for which, left, left_at, right, right_at, length in terms:
                if which == part:
                    one = dot_left(
                        operands[left][left_at : left_at + length, lanes],
                        operands[right][right_at : right_at + length, :].astype(BF),
                    )
                    value = one if value is None else value + one
            held[index, part * rows : (part + 1) * rows, :] = value.astype(held.dtype)
        taken = piece_rows(2 * index + odd, piece)
        for chunk in range(extra.shape[1] // cols):
            at = 3 * rows + chunk * piece
            held[index, at : at + piece, :] = extra[taken, chunk * cols : (chunk + 1) * cols].astype(held.dtype)
        return carry

    lax.fori_loop(0, count, step, 0)
    for index, out in enumerate(outs):
        out[...] = held[index]


def back_project_kernel(dq_ref, dk_ref, dv_ref, wq, wk, wv, *outs, first):
    for index, out in enumerate(outs):
        slots = out.shape[0]
        at = slice(index * slots, (index + 1) * slots)
        there = slice(first + index * slots, first + (index + 1) * slots)
        value = dot_right(dq_ref[at, :], wq[...])
        value += dot_right(dk_ref[there, :].astype(BF), wk[...])
        value += dot_right(dv_ref[there, :].astype(BF), wv[...])
        out[...] = value.astype(BF)


def encoder_grad_kernel(dk_ref, dv_ref, wk, wv, *outs):
    for index, out in enumerate(outs):
        slots = out.shape[0]
        at = slice(index * slots, (index + 1) * slots)
        value = dot_right(dk_ref[at, :].astype(BF), wk[...]) + dot_right(dv_ref[at, :].astype(BF), wv[...])
        out[...] = value.astype(BF)


def place_square_kernel(*refs, count, rows, piece):
    mine = lax.axis_index("ctx")
    threes, (near, other), outs = refs[:count], refs[count : count + 2], refs[count + 2 :]
    cols = threes[0].shape[1]
    span = HEAD * count
    blocks = [three[...].astype(F32) for three in threes]
    for group in range(count):
        wanted = mine ^ group
        chosen = blocks[0]
        for index in range(1, count):
            chosen = jnp.where(wanted == index, blocks[index], chosen)
        for part in range(3):
            for head in range(cols // HEAD):
                at = head * span + group * HEAD
                outs[part][:, at : at + HEAD] = chosen[
                    part * rows : (part + 1) * rows, head * HEAD : (head + 1) * HEAD
                ]
    core = mine % 2
    for source, place in ((near, core), (other, 1 - core)):
        for half in range(2):
            row = pl.ds(pl.multiple_of((2 * place + half) * piece, piece), piece)
            for chunk in range(outs[3].shape[1] // cols):
                at = (half * (outs[3].shape[1] // cols) + chunk) * piece
                outs[3][row, chunk * cols : (chunk + 1) * cols] = source[at : at + piece, :].astype(F32)


def place_feed_kernel(*refs, count, groups, rows, cols):
    mine = lax.axis_index("ctx")
    first, second = refs[count:]
    for index in range(count):
        target = mine ^ index
        for group in range(groups):
            column = pl.ds(pl.multiple_of(group * count * cols + target * cols, cols), cols)
            first[:, column] = refs[index][:rows, group * cols : (group + 1) * cols].astype(F32)
        row = pl.ds(pl.multiple_of(target * cols, cols), cols)
        second[row, :] = refs[index][rows:, :].astype(F32)


def fold(near, sent):
    arrived = swap(sent, "ctx", 1)
    return near, arrived


def after(value, *others):
    return lax.optimization_barrier((value,) + others)[0]


def far_hop(parts):
    arrived = swap(parts[1], "ctx", 1)
    sent = (parts[0].astype(F32) + arrived.astype(F32)).astype(BF)
    return sent, swap(sent, "ctx", 2)


def spread_ctx(own):
    far = swap(own, "ctx", 2)
    near = swap(own, "ctx", 1)
    return [own, near, far, swap(far, "ctx", 1)]


def start_ctx(own):
    return [own, swap(own, "ctx", 1), swap(own, "ctx", 2)]


def finish_ctx(blocks, *before):
    far = after(blocks[2], *before)
    return blocks[:2] + [far, swap(far, "ctx", 1)]


def send_z(own):
    size = lax.axis_size("wsh")
    blocks = {0: own, 1: swap(own, "wsh", 1)}
    for bit in range(2, size, 2):
        blocks[bit] = swap(own, "wsh", bit)
    return blocks


def pass_y(blocks):
    size = lax.axis_size("wsh")
    for bit in range(2, size, 2):
        blocks[bit + 1] = swap(blocks[bit], "wsh", 1)
    return [blocks[bit] for bit in range(size)]


class Ranges:
    def __init__(self, low, high, tile, chunk, flip):
        self.tile, self.chunk, self.count = tile, chunk, low.shape[0] // tile
        low, high = low.reshape(self.count, tile), high.reshape(self.count, tile)
        self.rows = jnp.stack([low, high], 1)
        first, last = jnp.min(low, 1) // chunk, (jnp.max(high, 1) - 1) // chunk + 1
        self.meta = jnp.concatenate([flip.reshape(1), first, last]).astype(jnp.int32)


def fast_body(
    inputs,
    enc_states,
    cotangent,
    slot_order,
    seq_lengths,
    enc_lengths,
    self_query,
    self_key,
    self_value,
    self_out,
    cross_query,
    cross_key,
    cross_value,
    cross_out,
    feed_in,
    feed_out,
    norm_gains,
    norm_shifts,
):
    size, groups = lax.axis_size("ctx"), lax.axis_size("wsh")
    mine, row = lax.axis_index("ctx"), lax.axis_index("wsh")
    slots = inputs.shape[1]
    total = slots * size
    enc_slots = enc_states.shape[1]
    width = inputs.shape[2]
    rows = self_query.shape[0]
    cols = width // size
    piece = rows // size
    ff_cols = feed_in.shape[1] // size
    ff_rows = feed_out.shape[0] // size
    heads = cols // HEAD
    middle = total // 2
    part = size // 2
    block_bf, block_f = ((slots, width), BF), ((slots, width), F32)
    terms_f = ((2, width), F32)

    given = call_packing(give_pieces_kernel, [((2 * piece, width), BF)], self_out, cross_out)[0]
    given = swap(given, "wsh", 1)
    height = 3 * rows + piece * (width // cols)
    self_block = call_packing(
        functools.partial(pack_kernel, size=size, which=0),
        [((height + 16, cols), BF)],
        self_query,
        self_key,
        self_value,
        self_out,
        given,
        jnp.transpose(norm_gains),
        jnp.transpose(norm_shifts),
    )[0]
    self_blocks = send_z(self_block)
    token_blocks = start_ctx(inputs[0])
    self_blocks = pass_y(self_blocks)
    token_blocks = finish_ctx(token_blocks)
    cross_block = call_packing(
        functools.partial(pack_kernel, size=size, which=1),
        [((height, cols), BF)],
        after(cross_query, self_block),
        cross_key,
        cross_value,
        cross_out,
        given,
    )[0]
    packed = cross_block
    cross_block = gather_wsh(cross_block).reshape(groups, height, cols)
    feed = call_packing(
        functools.partial(pack_feed_kernel, groups=groups, size=size),
        [((2 * rows, ff_cols), BF)],
        after(feed_in, self_block),
        feed_out,
    )[0]
    feed = gather_wsh(after(feed, packed, self_blocks[2])).reshape(groups, 2 * rows, ff_cols)

    relative = jnp.arange(size, dtype=jnp.int32) ^ mine
    order = jnp.take(slot_order[0].reshape(size, slots), relative, axis=0).reshape(1, total)
    own_order = lax.dynamic_slice_in_dim(slot_order[0], mine * slots, slots).reshape(slots, 1)
    place = (relative[:, None] * slots + jnp.arange(slots, dtype=jnp.int32)).reshape(total)
    lower = jnp.arange(seq_lengths.shape[1])
    lower = lower[None, :] <= lower[:, None]
    ends = jnp.sum(jnp.where(lower, seq_lengths[0][None, :], 0), 1)
    enc_ends = jnp.sum(jnp.where(lower, enc_lengths[0][None, :], 0), 1)
    passed = ends[None, :] <= place[:, None]
    starts = jnp.max(jnp.where(passed, ends[None, :], 0), 1)
    enc_from = jnp.max(jnp.where(passed, enc_ends[None, :], 0), 1)
    enc_to = jnp.min(jnp.where(passed, enc_slots * size, enc_ends[None, :]), 1)
    self_range = Ranges(starts, place + 1, 256, 256, mine * (slots // 256))
    cross_range = Ranges(enc_from, enc_to, 256, 128, mine * (enc_slots // 128))
    half = total // 512

    def unsort(blocks):
        outs = [block_f]
        if blocks[0].shape[0] > slots:
            outs.append(((blocks[0].shape[0] - slots, width), F32))
        return call(functools.partial(unsort_kernel, size=size), outs, (), own_order, *blocks)

    hat_all, tokens = call(
        functools.partial(sort_kernel, size=size), [((total, width), F32), block_f], (), order, *token_blocks
    )

    square, tall = ((width, cols), BF), ((total, cols), BF)
    wq, wk, wv, wo, norms, normed_one, queries, keys, values = call(
        functools.partial(project_kernel, groups=groups, rows=rows, piece=piece),
        [square] * 3 + [((cols, width), BF), ((8, width), F32), ((total, width), BF)] + [tall] * 3,
        (),
        hat_all,
        *self_blocks,
    )
    lanes = heads * 256
    half_outs = [((middle, cols), BF), ((half, 1, lanes), F32)] + [block_bf] * part
    scratch = [pltpu.VMEM((1, lanes), F32), pltpu.VMEM((1, lanes), F32), pltpu.VMEM((cols, 256), F32)]

    def self_forward(side, queries):
        body = functools.partial(
            attend_forward_kernel,
            own_queries=False,
            parts=part,
            offset=side * half,
            count=self_range.count,
            chunk=self_range.chunk,
        )
        return call(
            body, half_outs, (self_range.meta,), queries, keys, values, self_range.rows, wo, scratch=scratch
        )

    encoder = spread_ctx(after(enc_states[0], normed_one))
    mixed_high, lse_high, *far = self_forward(1, queries)
    sent, arrived = far_hop(far)
    mixed_low, lse_low, *near = self_forward(0, after(queries, sent))

    def normalize(base, near, arrived, which):
        return call(
            functools.partial(norm_kernel, which=which),
            [block_f, block_bf],
            (),
            norms,
            base,
            near[0],
            swap(near[1], "ctx", 1),
            arrived,
        )

    after_self, normed = normalize(tokens, near, arrived, 1)
    outside = spread_ctx(after(cotangent[0], arrived))
    outside = call(functools.partial(pick_kernel, size=size), [block_f], (), order, *outside)[0]

    normed_two = start_ctx(normed)
    cq, ck, cv, co, enc_keys, enc_values = call(
        functools.partial(cross_prepare_kernel, size=size, rows=rows, piece=piece),
        [square] * 3 + [((cols, width), BF)] + [((enc_slots * size, cols), BF)] * 2,
        (),
        cross_block,
        *encoder,
    )

    def cross_forward(side):
        body = functools.partial(
            attend_forward_kernel,
            own_queries=True,
            parts=part,
            offset=side * half,
            count=cross_range.count,
            chunk=cross_range.chunk,
        )
        return call(
            body,
            [((middle, cols), BF)] + half_outs,
            (cross_range.meta,),
            *normed_two[side * part : (side + 1) * part],
            cq,
            enc_keys,
            enc_values,
            cross_range.rows,
            co,
            scratch=scratch,
        )

    cross_low = cross_forward(0)
    normed_two = finish_ctx(normed_two, cross_low[3])
    cross_high = cross_forward(1)
    sent, arrived = far_hop(cross_high[3:])
    after_cross, normed = normalize(after_self, cross_low[3:], arrived, 2)

    normed_three = start_ctx(normed)
    def feed_forward(side):
        return call(
            functools.partial(feed_forward_kernel, parts=part),
            [((middle, ff_cols), BF)] * 2 + [block_bf] * part,
            (),
            *normed_three[side * part : (side + 1) * part],
            feed,
        )

    hidden_low, slope_low, *near = feed_forward(0)
    normed_three = finish_ctx(normed_three, near[0])
    hidden_high, slope_high, *far = feed_forward(1)
    sent, arrived = far_hop(far)
    result_low, result_high, grad_ffn, grad, terms_three = call(
        norm_turn_kernel,
        [((slots // 2, width), BF)] * 2 + [block_f, block_bf, terms_f],
        (),
        norms,
        after_cross,
        outside,
        near[0],
        swap(near[1], "ctx", 1),
        arrived,
    )

    def denormalize(value, grad, near, arrived, which):
        return call(
            functools.partial(norm_back_kernel, which=which),
            [block_f, block_bf, terms_f],
            (),
            norms,
            value,
            grad,
            near[0],
            swap(near[1], "ctx", 1),
            arrived,
        )

    grad_in = start_ctx(grad)

    def feed_backward(side, slope):
        return call(
            functools.partial(feed_backward_kernel, parts=part),
            [((middle, ff_cols), BF)] + [block_bf] * part,
            (),
            *grad_in[side * part : (side + 1) * part],
            feed,
            slope,
        )

    change_low, *near = feed_backward(0, slope_low)
    grad_in = finish_ctx(grad_in, near[0])
    change_high, *far = feed_backward(1, slope_high)
    sent, arrived = far_hop(far)
    feed_grads = call_streaming(
        functools.partial(feed_grad_kernel, size=size, rows=rows),
        ((groups, 2 * rows, width), BF),
        groups // 2,
        *normed_three,
        change_low,
        after(change_high, sent),
        hidden_low,
        hidden_high,
        *grad_in,
    )
    grad_cross, grad, terms_two = denormalize(after_cross, grad_ffn, near, after(arrived, feed_grads), 2)
    feed_grads = scatter_wsh(after(feed_grads, arrived).reshape(groups * 2 * rows, width))

    def weight_grads(terms, operands, out_grad, odd):
        count = groups // 2
        kind = BF if odd else F32
        body = functools.partial(weight_grad_kernel, terms=terms, odd=odd, rows=rows, piece=piece, count=count)
        outs = [((height, cols), kind)] * count
        return call(body, outs, (), *operands, out_grad, scratch=[pltpu.VMEM((count, height, cols), kind)])

    def pass_z(even, odd, index):
        value = (even[index] + odd[index].astype(F32)).astype(BF)
        return swap(value, "wsh", 2 * index)

    def backward(span, side, own_queries, sources, queries, mixed, lse, keys, values, wo, wq, before):
        body = functools.partial(
            attend_backward_kernel,
            own_queries=own_queries,
            parts=part,
            offset=side * half,
            count=span.count,
            chunk=span.chunk,
            fresh=before is None,
        )
        operands = [*sources, queries, mixed, lse, span.rows, keys, values, wo]
        if own_queries:
            operands.append(wq)
        aliases = {}
        if before is not None:
            aliases = {1 + len(operands) + i: 1 + i for i in range(3)}
            operands += before
        outs = [((middle, cols), BF), (keys.shape, F32), (keys.shape, F32), ((cols, width), F32)]
        if own_queries:
            outs += [block_bf] * part
        return call(
            body,
            outs,
            (span.meta,),
            *operands,
            scratch=[pltpu.VMEM((middle, cols), BF), pltpu.VMEM((cols, 256), F32)],
            aliases=aliases,
        )

    grad_in = start_ctx(grad)
    low = backward(
        cross_range, 0, True, grad_in[:part], *cross_low[:3], enc_keys, enc_values, co, cq, None
    )
    grad_in = finish_ctx(grad_in, low[4])
    result_low = start_ctx(after(result_low, grad_in[2]))
    high = backward(
        cross_range, 1, True, grad_in[part:], *cross_high[:3], enc_keys, enc_values, co, cq, list(low[1:4])
    )
    sent, arrived = far_hop([high[4], after(high[5], result_low[2])])
    dk, dv, dwo = high[1:4]
    operands = [*normed_two, low[0], high[0], *encoder, dk, dv]
    terms = []
    for index in range(size):
        side = index // part
        terms.append((0, index, 0, size + side, (index % part) * slots, slots))
    for index in range(size):
        for which in (1, 2):
            terms.append((which, size + 2 + index, 0, 2 * size + 1 + which, index * enc_slots, enc_slots))
    dk = after(dk, sent)
    operands[-2] = dk
    odd = weight_grads(tuple(terms), operands, dwo, 1)
    cross_even = weight_grads(tuple(terms), operands, dwo, 0)
    enc_parts = call(encoder_grad_kernel, [((enc_slots, width), BF)] * size, (), dk, dv, ck, cv)
    cross_odd = [swap(block, "wsh", 1) for block in odd]
    cross_far = pass_z(cross_even, cross_odd, 3)
    arrived = after(arrived, cross_even[0], cross_odd[3], *enc_parts)
    grad_self, grad, terms_one = denormalize(after_self, grad_cross, low[4:], arrived, 1)

    grad_in = start_ctx(grad)
    low = backward(
        self_range, 0, False, grad_in[:part], queries, mixed_low, lse_low, keys, values, wo, None, None
    )
    grad_in = finish_ctx(grad_in, low[0], cross_odd[2])
    cross_middle = pass_z(cross_even, cross_odd, 2)
    result_high = start_ctx(after(result_high, grad_in[2]))
    enc_sent, enc_far = far_hop([after(enc_parts[2], grad_in[2]), enc_parts[3]])
    enc_near = swap(enc_parts[1], "ctx", 1)
    enc_grad = enc_parts[0].astype(F32) + enc_near.astype(F32) + enc_far.astype(F32)
    high = backward(
        self_range, 1, False, grad_in[part:], queries, mixed_high, lse_high, keys, values, wo, None, list(low[1:4])
    )
    dk, dv, dwo = high[1:4]

    def back_project(side, dq):
        body = functools.partial(back_project_kernel, first=side * middle)
        return call(body, [block_bf] * part, (), dq, dk, dv, wq, wk, wv)

    far = back_project(1, after(high[0], cross_odd[1], cross_far))
    cross_near = pass_z(cross_even, cross_odd, 1)
    operands = [normed_one, low[0], high[0], after(dk, result_high[2]), dv]
    terms = ((0, 0, 0, 1, 0, middle), (0, 0, middle, 2, 0, middle), (1, 0, 0, 3, 0, total), (2, 0, 0, 4, 0, total))
    odd = weight_grads(terms, operands, dwo, 1)
    sent, arrived = far_hop(far)
    self_odd = [swap(block, "wsh", 1) for block in odd]
    near = back_project(0, after(low[0], sent, odd[0]))
    self_even = weight_grads(terms, operands, after(dwo, *near), 0)
    self_far = pass_z(self_even, self_odd, 3)

    feed_blocks = start_ctx(after(feed_grads, sent))
    grad = call(
        norm_first_kernel,
        [((slots + 16, width), BF)],
        (),
        norms,
        tokens,
        grad_self,
        near[0],
        swap(near[1], "ctx", 1),
        after(arrived, self_even[0]),
        terms_one,
        terms_two,
        terms_three,
    )[0]
    input_grad = start_ctx(grad)

    def finish(even, odd, *parts):
        share = even[0] + odd[0].astype(F32)
        for value in parts:
            share = share + value.astype(F32)
        share = share.astype(BF)
        three, fourth = share[: 3 * rows], share[3 * rows :]
        pair = jnp.concatenate([fourth, swap(fourth, "wsh", 1)], 0)
        pair = jnp.where(row % 2 == mine // 2, pair, swap(pair, "ctx", 2))
        return call(
            functools.partial(place_square_kernel, count=size, rows=rows, piece=piece),
            [((rows, width), F32)] * 4,
            (),
            *spread_ctx(three),
            pair,
            swap(pair, "ctx", 1),
        )

    result_low = finish_ctx(result_low, self_odd[3], grad)
    result_high = finish_ctx(result_high)
    result = unsort([half for pair in zip(result_low, result_high) for half in pair])[0]
    self_middle = pass_z(self_even, self_odd, 2)
    self_near = pass_z(self_even, self_odd, 1)
    feed_in_grad, feed_out_grad = call(
        functools.partial(place_feed_kernel, count=size, groups=groups, rows=rows, cols=ff_rows),
        [((rows, groups * size * ff_rows), F32), ((size * ff_rows, width), F32)],
        (),
        *finish_ctx(feed_blocks, self_odd[2], result, cross_near),
    )
    input_grad, terms = unsort(finish_ctx(input_grad, self_odd[1], self_far, feed_in_grad))
    terms = terms[:8]
    terms = terms + swap(terms, "wsh", 1)
    pieces = [lax.dynamic_slice_in_dim(terms, (row ^ bit) * rows, rows, 1) for bit in range(0, groups, 2)]
    terms = pieces[0]
    for index in range(1, groups // 2):
        terms = terms + swap(pieces[index], "wsh", 2 * index)
    terms = jnp.transpose(terms)
    cross_odd[0] = after(cross_odd[0], input_grad, self_near)
    cross_grads = finish(cross_even, cross_odd, cross_near, cross_middle, cross_far)
    self_grads = finish(self_even, self_odd, self_near, self_middle, self_far)
    return (
        result[None],
        input_grad[None],
        enc_grad[None],
        *self_grads,
        *cross_grads,
        feed_in_grad,
        feed_out_grad,
        terms[:, 0::2],
        terms[:, 1::2],
    )


def solution(mesh):
    token, weight = P("wsh", "ctx", None), P("wsh", None)
    in_specs = (token,) * 3 + (weight,) * 15
    out_specs = (token,) * 3 + (weight,) * 12
    body = fast_body if mesh.shape["ctx"] == 4 else plain_body
    return jax.shard_map(body, mesh=mesh, in_specs=in_specs, out_specs=out_specs, check_vma=False)
```

```python
import functools

import jax
import jax.numpy as jnp
from jax import lax
from jax.experimental import pallas as pl
from jax.experimental.pallas import tpu as pltpu
from jax.sharding import PartitionSpec as P

HEAD = 64
BF = jnp.bfloat16
F32 = jnp.float32


def dot(left, right):
    return jnp.dot(left, right, preferred_element_type=F32)


def dot_left(left, right):
    return lax.dot_general(left, right, (((0,), (0,)), ((), ())), preferred_element_type=F32)


def dot_right(left, right):
    return lax.dot_general(left, right, (((1,), (1,)), ((), ())), preferred_element_type=F32)


def swap(value, axis, bit):
    size = lax.axis_size(axis)
    return lax.ppermute(value, axis, [(i, i ^ bit) for i in range(size)])


def gather_ctx(own):
    size = lax.axis_size("ctx")
    blocks = {0: own}
    bit = size // 2
    while bit:
        for index in sorted(blocks):
            blocks[index | bit] = swap(blocks[index], "ctx", bit)
        bit //= 2
    return [blocks[index] for index in range(size)]


def scatter_ctx(blocks):
    blocks = dict(enumerate(blocks))
    size, bit = len(blocks), 1
    while bit < size:
        for index in sorted(blocks, reverse=True):
            if index & bit:
                arrived = swap(blocks.pop(index).astype(BF), "ctx", bit)
                blocks[index ^ bit] = blocks[index ^ bit] + arrived.astype(F32)
        bit *= 2
    return blocks[0]


def halves(blocks):
    middle = len(blocks) // 2
    return (jnp.concatenate(blocks[:middle], 0), jnp.concatenate(blocks[middle:], 0))


def scatter_halves(low, high, rows):
    count = low.shape[0] // rows
    cut = [low[i * rows : (i + 1) * rows] for i in range(count)]
    return scatter_ctx(cut + [high[i * rows : (i + 1) * rows] for i in range(count)])


def norm_parts(values):
    center = values - jnp.mean(values, axis=-1, keepdims=True)
    rate = lax.rsqrt(jnp.mean(center * center, axis=-1, keepdims=True) + 1e-05)
    return center * rate, rate


def norm_back(hat, rate, gain, grad):
    scaled = grad * gain
    inner = jnp.mean(scaled * hat, axis=-1, keepdims=True)
    result = rate * (scaled - jnp.mean(scaled, axis=-1, keepdims=True) - hat * inner)
    return result, jnp.sum(grad * hat, axis=0), jnp.sum(grad, axis=0)


def gelu_back(values, grad):
    unused, pullback = jax.vjp(lambda u: jax.nn.gelu(u, approximate=True), values)
    return pullback(grad)[0]


def split_heads(block, heads, head):
    wide = block.astype(F32)
    lane = lax.broadcasted_iota(jnp.int32, wide.shape, 1) // head
    parts = [jnp.where(lane == h, wide, 0.0).astype(BF) for h in range(heads)]
    return jnp.concatenate(parts, 0)


def spread(row, heads):
    return jnp.concatenate([row] * heads, 1)


def allowed_keys(first, chunk, low, high):
    index = first + lax.broadcasted_iota(jnp.int32, (chunk, low.shape[1]), 0)
    return (index >= low) & (index < high)


def forward_kernel(meta, q_ref, k_ref, v_ref, rows_ref, o_ref, lse_ref, top, total, mixed, *, heads, head, chunk, count, offset):
    block = pl.program_id(0) + offset
    queries = q_ref.shape[0]
    split = split_heads(q_ref[...].astype(F32) * 0.125, heads, head)
    low = spread(rows_ref[0, 0:1, :], heads)
    high = spread(rows_ref[0, 1:2, :], heads)
    top[...] = jnp.full_like(top, -1e30)
    total[...] = jnp.zeros_like(total)
    mixed[...] = jnp.zeros_like(mixed)

    def step(index, carry):
        start = pl.multiple_of((index ^ meta[0]) * chunk, chunk)
        keys = k_ref[pl.ds(start, chunk), :]
        values = jnp.transpose(v_ref[pl.ds(start, chunk), :])
        scores = dot_right(keys, split)
        scores = jnp.where(allowed_keys(index * chunk, chunk, low, high), scores, -1e30)
        before = top[...]
        now = jnp.maximum(before, jnp.max(scores, axis=0, keepdims=True))
        decay = jnp.exp(before - now)
        weight = jnp.exp(scores - now)
        top[...] = now
        total[...] = total[...] * decay + jnp.sum(weight, axis=0, keepdims=True)
        weight = weight.astype(BF)
        for h in range(heads):
            rows, cols = slice(h * head, (h + 1) * head), slice(h * queries, (h + 1) * queries)
            mixed[rows, :] = mixed[rows, :] * decay[:, cols] + dot(values[rows, :], weight[:, cols])
        return carry

    lax.fori_loop(meta[1 + block], meta[1 + count + block], step, 0)
    amount = total[...]
    for h in range(heads):
        rows, cols = slice(h * head, (h + 1) * head), slice(h * queries, (h + 1) * queries)
        mixed[rows, :] = mixed[rows, :] / amount[:, cols]
    o_ref[...] = jnp.transpose(mixed[...]).astype(BF)
    lse_ref[0] = top[...] + jnp.log(amount)


def backward_kernel(meta, q_ref, g_ref, o_ref, lse_ref, rows_ref, k_ref, v_ref, dq_ref, dk_ref, dv_ref, dq_sum, *, heads, head, chunk, count, offset):
    block = pl.program_id(0) + offset
    queries = q_ref.shape[0]

    @pl.when(pl.program_id(0) == 0)
    def _():
        dk_ref[...] = jnp.zeros_like(dk_ref)
        dv_ref[...] = jnp.zeros_like(dv_ref)

    split = split_heads(q_ref[...].astype(F32) * 0.125, heads, head)
    grads = split_heads(g_ref[...], heads, head)
    low = spread(rows_ref[0, 0:1, :], heads)
    high = spread(rows_ref[0, 1:2, :], heads)
    lse = lse_ref[0]
    product = jnp.transpose(g_ref[...].astype(F32) * o_ref[...].astype(F32))
    inner = jnp.concatenate(
        [jnp.sum(product[h * head : (h + 1) * head], axis=0, keepdims=True) for h in range(heads)], 1
    )
    dq_sum[...] = jnp.zeros_like(dq_sum)

    def step(index, carry):
        start = pl.multiple_of((index ^ meta[0]) * chunk, chunk)
        keys = k_ref[pl.ds(start, chunk), :]
        scores = dot_right(keys, split)
        scores = jnp.where(allowed_keys(index * chunk, chunk, low, high), scores, -1e30)
        weight = jnp.exp(scores - lse)
        slope = dot_right(v_ref[pl.ds(start, chunk), :], grads)
        slope = (weight * (slope - inner)).astype(BF)
        dv_ref[pl.ds(start, chunk), :] += dot(weight.astype(BF), grads)
        dk_ref[pl.ds(start, chunk), :] += dot(slope, split)
        turned = jnp.transpose(keys)
        for h in range(heads):
            rows, cols = slice(h * head, (h + 1) * head), slice(h * queries, (h + 1) * queries)
            dq_sum[rows, :] += dot(turned[rows, :], slope[:, cols])
        return carry

    lax.fori_loop(meta[1 + block], meta[1 + count + block], step, 0)
    dq_ref[...] = (jnp.transpose(dq_sum[...]) * 0.125).astype(BF)


class Attention:
    def __init__(self, low, high, tile, chunk, flip):
        self.tile, self.chunk = tile, chunk
        self.count = low.shape[0] // tile
        low, high = low.reshape(self.count, tile), high.reshape(self.count, tile)
        self.rows = jnp.stack([low, high], 1)
        first, last = jnp.min(low, 1) // chunk, (jnp.max(high, 1) - 1) // chunk + 1
        self.meta = jnp.concatenate([flip.reshape(1), first, last]).astype(jnp.int32)

    def specs(self, width, heads, offset, queries_at):
        tile = self.tile
        tall = pl.BlockSpec((tile, width), lambda i, m: (i + queries_at, 0))
        rows = pl.BlockSpec((1, 2, tile), lambda i, m: (i + offset, 0, 0))
        return tall, rows

    def forward(self, queries, keys, values, offset, steps, queries_at):
        width, heads = queries.shape[1], queries.shape[1] // HEAD
        tall, rows = self.specs(width, heads, offset, queries_at)
        whole = pl.BlockSpec(keys.shape, lambda i, m: (0, 0))
        lanes = heads * self.tile
        body = functools.partial(
            forward_kernel, heads=heads, head=HEAD, chunk=self.chunk, count=self.count, offset=offset
        )
        pairs = steps * self.tile * keys.shape[0] * heads
        return pl.pallas_call(
            body,
            grid_spec=pltpu.PrefetchScalarGridSpec(
                num_scalar_prefetch=1,
                grid=(steps,),
                in_specs=[tall, whole, whole, rows],
                out_specs=[
                    pl.BlockSpec((self.tile, width), lambda i, m: (i, 0)),
                    pl.BlockSpec((1, 1, lanes), lambda i, m: (i, 0, 0)),
                ],
                scratch_shapes=[
                    pltpu.VMEM((1, lanes), F32),
                    pltpu.VMEM((1, lanes), F32),
                    pltpu.VMEM((width, self.tile), F32),
                ],
            ),
            out_shape=[
                jax.ShapeDtypeStruct((steps * self.tile, width), BF),
                jax.ShapeDtypeStruct((steps, 1, lanes), F32),
            ],
            cost_estimate=pl.CostEstimate(flops=pairs * 256, transcendentals=pairs // 2, bytes_accessed=2 << 20),
            compiler_params=pltpu.CompilerParams(vmem_limit_bytes=24 << 20),
        )(self.meta, queries, keys, values, self.rows)

    def backward(self, queries, grads, mixed, lse, keys, values, offset, steps, queries_at):
        width, heads = queries.shape[1], queries.shape[1] // HEAD
        tall, rows = self.specs(width, heads, offset, queries_at)
        near = pl.BlockSpec((self.tile, width), lambda i, m: (i, 0))
        whole = pl.BlockSpec(keys.shape, lambda i, m: (0, 0))
        lanes = heads * self.tile
        body = functools.partial(
            backward_kernel, heads=heads, head=HEAD, chunk=self.chunk, count=self.count, offset=offset
        )
        pairs = steps * self.tile * keys.shape[0] * heads
        return pl.pallas_call(
            body,
            grid_spec=pltpu.PrefetchScalarGridSpec(
                num_scalar_prefetch=1,
                grid=(steps,),
                in_specs=[tall, near, near, pl.BlockSpec((1, 1, lanes), lambda i, m: (i, 0, 0)), rows, whole, whole],
                out_specs=[near, whole, whole],
                scratch_shapes=[pltpu.VMEM((width, self.tile), F32)],
            ),
            out_shape=[
                jax.ShapeDtypeStruct((steps * self.tile, width), BF),
                jax.ShapeDtypeStruct(keys.shape, F32),
                jax.ShapeDtypeStruct(keys.shape, F32),
            ],
            cost_estimate=pl.CostEstimate(flops=pairs * 640, transcendentals=pairs // 2, bytes_accessed=4 << 20),
            compiler_params=pltpu.CompilerParams(vmem_limit_bytes=32 << 20),
        )(self.meta, queries, grads, mixed, lse, self.rows, keys, values)


def gather_wsh(part):
    return lax.all_gather(part, "wsh", axis=0, tiled=True)


def scatter_wsh(whole):
    return lax.psum_scatter(whole.astype(BF), "wsh", scatter_dimension=0, tiled=True)


def piece_moves(groups, size):
    return [((g % size) * groups + g // size, g) for g in range(groups * size)]


def plain_body(
    inputs,
    enc_states,
    cotangent,
    slot_order,
    seq_lengths,
    enc_lengths,
    self_query,
    self_key,
    self_value,
    self_out,
    cross_query,
    cross_key,
    cross_value,
    cross_out,
    feed_in,
    feed_out,
    norm_gains,
    norm_shifts,
):
    size, groups = lax.axis_size("ctx"), lax.axis_size("wsh")
    mine, row = lax.axis_index("ctx"), lax.axis_index("wsh")
    slots = inputs.shape[1]
    total = slots * size
    enc_slots = enc_states.shape[1]
    width = inputs.shape[2]
    rows = self_query.shape[0]
    cols = width // size
    piece = rows // size
    ff_cols = feed_in.shape[1] // size
    ff_rows = feed_out.shape[0] // size

    def columns(matrix):
        return lax.dynamic_slice_in_dim(matrix, mine * cols, cols, 1)

    norms = jnp.concatenate([norm_gains, norm_shifts, jnp.zeros((rows, 120), BF)], 1)
    self_full = gather_wsh(jnp.concatenate([columns(self_query), columns(self_key), columns(self_value), norms], 1))
    q_full, k_full, v_full = (self_full[:, i * cols : (i + 1) * cols] for i in range(3))
    norm_rows = jnp.transpose(self_full[:, 3 * cols : 3 * cols + 8].astype(F32))
    gains, shifts = norm_rows[:4, None, :], norm_rows[4:, None, :]

    def out_piece(matrix):
        return lax.dynamic_slice_in_dim(matrix, mine * piece, piece, 0)

    pieces = jnp.concatenate([out_piece(self_out), out_piece(cross_out)], 0)
    pieces = lax.ppermute(pieces, ("ctx", "wsh"), piece_moves(groups, size))
    pieces = gather_wsh(pieces).reshape(groups, 2, piece, width)
    out_full, cross_o_full = pieces[:, 0].reshape(cols, width), pieces[:, 1].reshape(cols, width)
    cross_full = gather_wsh(jnp.concatenate([columns(cross_query), columns(cross_key), columns(cross_value)], 1))
    cq_full, ck_full, cv_full = (cross_full[:, i * cols : (i + 1) * cols] for i in range(3))
    first_part = lax.dynamic_slice_in_dim(feed_in.reshape(rows, groups, size, ff_rows), mine, 1, 2)
    second_part = lax.dynamic_slice_in_dim(feed_out, mine * ff_rows, ff_rows, 0)
    feed = jnp.concatenate([first_part.reshape(rows, ff_cols), second_part.reshape(rows, ff_cols)], 0)
    feed = gather_wsh(feed).reshape(groups, 2, rows, ff_cols)
    first_full = feed[:, 0].reshape(groups * rows, ff_cols)
    second_full = feed[:, 1].reshape(groups * ff_rows, width)

    relative = jnp.arange(size, dtype=jnp.int32) ^ mine
    order = jnp.take(slot_order[0].reshape(size, slots), relative, axis=0).reshape(total)
    place = (relative[:, None] * slots + jnp.arange(slots, dtype=jnp.int32)).reshape(total)
    lower = jnp.arange(seq_lengths.shape[1])
    lower = lower[None, :] <= lower[:, None]
    ends = jnp.sum(jnp.where(lower, seq_lengths[0][None, :], 0), 1)
    enc_ends = jnp.sum(jnp.where(lower, enc_lengths[0][None, :], 0), 1)
    passed = ends[None, :] <= place[:, None]
    starts = jnp.max(jnp.where(passed, ends[None, :], 0), 1)
    enc_from = jnp.max(jnp.where(passed, enc_ends[None, :], 0), 1)
    enc_to = jnp.min(jnp.where(passed, enc_slots * size, enc_ends[None, :]), 1)
    self_att = Attention(starts, place + 1, 256, 256, mine * (slots // 256))
    cross_att = Attention(enc_from, enc_to, 256, 128, mine * (enc_slots // 128))
    tiles = total // 256
    half = tiles // 2

    to_place = (order[None, :] == place[:, None]).astype(BF)
    to_slot = (order[:slots, None] == place[None, :]).astype(BF)
    tokens_all = jnp.concatenate(gather_ctx(inputs[0]), 0)
    tokens_all = dot(to_place, tokens_all)
    tokens = tokens_all[:slots]
    encoder = jnp.concatenate(gather_ctx(enc_states[0]), 0)
    outside = jnp.concatenate(gather_ctx(cotangent[0]), 0)
    outside = dot(to_place[:slots], outside)

    hat_all, unused = norm_parts(tokens_all)
    normed_one = (hat_all * gains[0] + shifts[0]).astype(BF)
    queries = dot(normed_one, q_full).astype(BF)
    keys = dot(normed_one, k_full).astype(BF)
    values = dot(normed_one, v_full).astype(BF)
    mixed_high, lse_high = self_att.forward(queries, keys, values, half, half, half)
    mixed_low, lse_low = self_att.forward(queries, keys, values, 0, half, 0)
    after_self = tokens + scatter_halves(dot(mixed_low, out_full), dot(mixed_high, out_full), slots)

    hat_two, rate_two = norm_parts(after_self)
    normed_two = halves(gather_ctx((hat_two * gains[1] + shifts[1]).astype(BF)))
    enc_keys = dot(encoder, ck_full).astype(BF)
    enc_values = dot(encoder, cv_full).astype(BF)
    queries_two = [dot(part, cq_full).astype(BF) for part in normed_two]
    mixed_two = [
        cross_att.forward(queries_two[side], enc_keys, enc_values, side * half, half, 0) for side in range(2)
    ]
    after_cross = after_self + scatter_halves(*(dot(part[0], cross_o_full) for part in mixed_two), slots)

    hat_three, rate_three = norm_parts(after_cross)
    normed_three = halves(gather_ctx((hat_three * gains[2] + shifts[2]).astype(BF)))
    pre_act = [dot(part, first_full) for part in normed_three]
    hidden = [jax.nn.gelu(part, approximate=True).astype(BF) for part in pre_act]
    after_ffn = after_cross + scatter_halves(*(dot(part, second_full) for part in hidden), slots)
    hat_four, rate_four = norm_parts(after_ffn)
    result = hat_four * gains[3] + shifts[3]
    result = jnp.concatenate(gather_ctx(result.astype(BF)), 0)
    result = dot(to_slot, result)

    grad_ffn, gain_three, shift_three = norm_back(hat_four, rate_four, gains[3], outside)
    grad_in = halves(gather_ctx(grad_ffn.astype(BF)))
    grad_pre = [
        gelu_back(part, dot_right(grad, second_full)).astype(BF)
        for part, grad in zip(pre_act, grad_in)
    ]
    arrived = scatter_halves(*(dot_right(grad, first_full) for grad in grad_pre), slots)
    norm_part, gain_two, shift_two = norm_back(hat_three, rate_three, gains[2], arrived)
    grad_cross = grad_ffn + norm_part
    grad_first = sum(dot_left(n, g) for n, g in zip(normed_three, grad_pre))
    grad_second = sum(dot_left(n, g) for n, g in zip(hidden, grad_in))
    feed_grads = jnp.concatenate(
        [
            grad_first.astype(BF).reshape(groups, rows, ff_cols),
            grad_second.astype(BF).reshape(groups, rows, ff_cols),
        ],
        1,
    )
    feed_grads = scatter_wsh(feed_grads.reshape(groups * 2 * rows, ff_cols))
    feed_grads = lax.all_gather(feed_grads, "ctx", axis=0).reshape(size, 2, rows, ff_cols)
    feed_in_grad = jnp.transpose(feed_grads[:, 0].reshape(size, rows, groups, ff_rows), (1, 2, 0, 3))
    feed_in_grad = feed_in_grad.reshape(rows, groups * size * ff_rows).astype(F32)
    feed_out_grad = feed_grads[:, 1].reshape(size * ff_rows, width).astype(F32)

    def share(query_grad, key_grad, value_grad, out_grad):
        packed = [
            query_grad.astype(BF),
            key_grad.astype(BF),
            value_grad.astype(BF),
            out_grad.astype(BF).reshape(groups * rows, cols),
        ]
        packed = scatter_wsh(jnp.concatenate(packed, 1))
        moved = packed[:, 3 * cols :].reshape(piece, width)
        moved = lax.ppermute(moved, ("ctx", "wsh"), [(b, a) for a, b in piece_moves(groups, size)])
        packed = jnp.concatenate([packed[:, : 3 * cols], moved.reshape(rows, cols)], 1)
        packed = lax.all_gather(packed, "ctx", axis=0)
        three = [
            jnp.transpose(packed[:, :, i * cols : (i + 1) * cols], (1, 0, 2)).reshape(rows, width).astype(F32)
            for i in range(3)
        ]
        return three + [packed[:, :, 3 * cols :].reshape(size, piece, width).reshape(rows, width).astype(F32)]

    grad_in = halves(gather_ctx(grad_cross.astype(BF)))
    grad_mixed = [dot_right(grad, cross_o_full).astype(BF) for grad in grad_in]
    back = [
        cross_att.backward(
            queries_two[side], grad_mixed[side], *mixed_two[side], enc_keys, enc_values, side * half, half, 0
        )
        for side in range(2)
    ]
    arrived = scatter_halves(*(dot_right(part[0], cq_full) for part in back), slots)
    norm_part, gain_one, shift_one = norm_back(hat_two, rate_two, gains[1], arrived)
    grad_self = grad_cross + norm_part
    grad_ek = (back[0][1] + back[1][1]).astype(BF)
    grad_ev = (back[0][2] + back[1][2]).astype(BF)
    enc_part = dot_right(grad_ek, ck_full) + dot_right(grad_ev, cv_full)
    enc_grad = scatter_ctx([enc_part[i * enc_slots : (i + 1) * enc_slots] for i in range(size)])
    cross_q_grad, cross_k_grad, cross_v_grad, cross_o_grad = share(
        sum(dot_left(n, part[0]) for n, part in zip(normed_two, back)),
        dot_left(encoder, grad_ek),
        dot_left(encoder, grad_ev),
        sum(dot_left(part[0], g) for part, g in zip(mixed_two, grad_in)),
    )

    grad_in = halves(gather_ctx(grad_self.astype(BF)))
    grad_mixed = [dot_right(grad, out_full).astype(BF) for grad in grad_in]
    back_low = self_att.backward(queries, grad_mixed[0], mixed_low, lse_low, keys, values, 0, half, 0)
    back_high = self_att.backward(queries, grad_mixed[1], mixed_high, lse_high, keys, values, half, half, half)
    grad_q = jnp.concatenate([back_low[0], back_high[0]], 0)
    grad_k = (back_low[1] + back_high[1]).astype(BF)
    grad_v = (back_low[2] + back_high[2]).astype(BF)
    arrived = dot_right(grad_q, q_full) + dot_right(grad_k, k_full) + dot_right(grad_v, v_full)
    arrived = scatter_ctx([arrived[i * slots : (i + 1) * slots] for i in range(size)])
    hat_one, rate_one = norm_parts(tokens)
    norm_part, gain_zero, shift_zero = norm_back(hat_one, rate_one, gains[0], arrived)
    input_grad = grad_self + norm_part
    input_grad = jnp.concatenate(gather_ctx(input_grad.astype(BF)), 0)
    input_grad = dot(to_slot, input_grad)
    query_grad, key_grad, value_grad, out_grad = share(
        dot_left(normed_one, grad_q),
        dot_left(normed_one, grad_k),
        dot_left(normed_one, grad_v),
        dot_left(mixed_low, grad_in[0]) + dot_left(mixed_high, grad_in[1]),
    )

    terms = jnp.stack(
        [gain_zero, gain_one, gain_two, gain_three, shift_zero, shift_one, shift_two, shift_three], 0
    )
    for axis, amount in (("ctx", size), ("wsh", groups)):
        bit = 1
        while bit < amount:
            terms = terms + swap(terms, axis, bit)
            bit *= 2
    terms = jnp.transpose(lax.dynamic_slice_in_dim(terms, row * rows, rows, 1))
    return (
        result[None],
        input_grad[None],
        enc_grad[None],
        query_grad,
        key_grad,
        value_grad,
        out_grad,
        cross_q_grad,
        cross_k_grad,
        cross_v_grad,
        cross_o_grad,
        feed_in_grad,
        feed_out_grad,
        terms[:, :4],
        terms[:, 4:],
    )


SMALL = pl.CostEstimate(flops=1 << 20, transcendentals=0, bytes_accessed=1 << 16)


def call(kernel, outs, scalars, *operands, scratch=(), aliases=None, vmem=12, space=pltpu.VMEM, out_space=pltpu.VMEM):
    specs = [pl.BlockSpec(memory_space=pltpu.SMEM)] * len(scalars)
    specs += [pl.BlockSpec(memory_space=space)] * len(operands)
    return pl.pallas_call(
        kernel,
        in_specs=specs,
        out_specs=[pl.BlockSpec(memory_space=out_space)] * len(outs),
        out_shape=[jax.ShapeDtypeStruct(shape, kind) for shape, kind in outs],
        scratch_shapes=list(scratch),
        input_output_aliases=aliases or {},
        cost_estimate=SMALL,
        compiler_params=pltpu.CompilerParams(vmem_limit_bytes=vmem << 20),
    )(*scalars, *operands)


def call_packing(kernel, outs, *operands):
    scratch = [pltpu.VMEM(operand.shape, operand.dtype) for operand in operands]
    count = len(operands)

    def fetching(*refs):
        sources, outs, held, done = refs[:count], refs[count : -count - 1], refs[-count - 1 : -1], refs[-1]
        copies = [pltpu.make_async_copy(sources[i], held[i], done.at[i]) for i in range(count)]
        for copy in copies:
            copy.start()
        for copy in copies:
            copy.wait()
        kernel(*held, *outs)

    operands = [pltpu.with_memory_space_constraint(operand, pltpu.HBM) for operand in operands]
    scratch.append(pltpu.SemaphoreType.DMA((count,)))
    return call(fetching, outs, (), *operands, scratch=scratch, space=pltpu.HBM)


def one_hot(hit):
    return jnp.where(hit, 1.0, 0.0).astype(BF)


def ctx_part(size):
    return pl.ds(pl.multiple_of(lax.axis_index("ctx") * size, size), size)


def my_heads(matrix, size):
    cols = matrix.shape[1] // size
    heads = cols // HEAD
    span = HEAD * size
    source = lax.broadcasted_iota(jnp.int32, (span, cols), 0) - lax.axis_index("ctx") * HEAD
    target = lax.broadcasted_iota(jnp.int32, (span, cols), 1)
    total = None
    for head in range(heads):
        part = dot(matrix[:, head * span : (head + 1) * span], one_hot((source >= 0) & (source < HEAD) & (source == target - head * HEAD)))
        total = part if total is None else total + part
    return total.astype(BF)


def give_pieces_kernel(one, two, out_ref):
    piece = out_ref.shape[0] // 2
    start = pl.multiple_of((lax.axis_index("ctx") % 2) * 2 * piece + piece, piece)
    out_ref[:piece, :] = one[pl.ds(start, piece), :]
    out_ref[piece:, :] = two[pl.ds(start, piece), :]


def my_piece(matrix, given, which):
    piece = given.shape[0] // 2
    mine = lax.axis_index("ctx")
    start = pl.multiple_of((mine % 2) * 2 * piece, piece)
    own = matrix[pl.ds(start, piece), :].astype(F32)
    other = given[which * piece : (which + 1) * piece, :].astype(F32)
    same = lax.axis_index("wsh") % 2 == mine // 2
    return jnp.where(same, own, other).astype(BF)


def pack_kernel(wq, wk, wv, wo, given, *refs, size, which):
    *norm_refs, out_ref = refs
    rows, cols = wq.shape[0], out_ref.shape[1]
    for part, full in enumerate((wq, wk, wv)):
        out_ref[part * rows : (part + 1) * rows, :] = my_heads(full, size)
    taken = my_piece(wo, given, which)
    piece = taken.shape[0]
    for chunk in range(taken.shape[1] // cols):
        at = 3 * rows + chunk * piece
        out_ref[at : at + piece, :] = taken[:, chunk * cols : (chunk + 1) * cols]
    if norm_refs:
        gains, shifts = norm_refs
        norms = jnp.concatenate([gains[...], shifts[...]], 0).astype(F32)
        norms = jnp.concatenate([norms, jnp.zeros((8, rows), F32)], 0)
        norms = jnp.concatenate([norms, jnp.zeros((16, cols - rows), F32)], 1)
        out_ref[out_ref.shape[0] - 16 :, :] = norms.astype(BF)


def pack_feed_kernel(first, second, out_ref, groups, size):
    rows, width = first.shape[0], first.shape[1] // groups
    cols = width // size
    mine = lax.axis_index("ctx")
    for group in range(groups):
        at = pl.ds(pl.multiple_of(group * width + mine * cols, cols), cols)
        out_ref[:rows, group * cols : (group + 1) * cols] = first[:, at]
    out_ref[rows:, :] = second[ctx_part(cols), :]


def sort_kernel(order_ref, *refs, size):
    sources, (hat_ref, own_ref) = refs[:size], refs[size:]
    slots = sources[0].shape[0]
    mine = lax.axis_index("ctx")

    def block(index, carry):
        base = (mine ^ index) * slots
        total = jnp.zeros(own_ref.shape, F32)
        for source in range(size):
            order = order_ref[:, source * slots : (source + 1) * slots]
            place = base + lax.broadcasted_iota(jnp.int32, (slots, slots), 0)
            total += dot(one_hot(order == place), sources[source][...])

        @pl.when(index == 0)
        def _():
            own_ref[...] = total

        hat, unused = norm_parts(total)
        hat_ref[pl.ds(pl.multiple_of(index * slots, slots), slots), :] = hat
        return carry

    lax.fori_loop(0, size, block, 0)


def pick_kernel(order_ref, *refs, size):
    sources, out_ref = refs[:size], refs[size]
    slots = sources[0].shape[0]
    base = lax.axis_index("ctx") * slots
    def columns(tile, carry):
        lanes = pl.ds(pl.multiple_of(tile * 256, 256), 256)
        total = jnp.zeros((slots, 256), F32)
        for source in range(size):
            order = order_ref[:, source * slots : (source + 1) * slots]
            place = base + lax.broadcasted_iota(jnp.int32, (slots, slots), 0)
            total += dot(one_hot(order == place), sources[source][:, lanes])
        out_ref[:, lanes] = total
        return carry

    lax.fori_loop(0, out_ref.shape[1] // 256, columns, 0)


def unsort_kernel(order_ref, *refs, size):
    count = len(refs) - 1 if len(refs) % size == 1 else len(refs) - 2
    sources, out_ref = refs[:count], refs[count]
    slots = out_ref.shape[0]
    pieces = count // size
    length = slots // pieces
    mine = lax.axis_index("ctx")

    def columns(tile, carry):
        lanes = pl.ds(pl.multiple_of(tile * 256, 256), 256)
        total = jnp.zeros((slots, 256), F32)
        for index, source in enumerate(sources):
            first = (mine ^ (index // pieces)) * slots + (index % pieces) * length
            place = first + lax.broadcasted_iota(jnp.int32, (slots, length), 1)
            total += dot(one_hot(order_ref[...] == place), source[:length, lanes])
        out_ref[:, lanes] = total
        return carry

    lax.fori_loop(0, out_ref.shape[1] // 256, columns, 0)
    if count + 1 < len(refs):
        refs[count + 1][...] = sum(source[slots:, :].astype(F32) for source in sources)


def wsh_rows(index, rows):
    target = (lax.axis_index("wsh") ^ index) * rows
    return pl.ds(pl.multiple_of(target, rows), rows)


def piece_rows(index, piece):
    target = lax.axis_index("wsh") ^ index ^ (lax.axis_index("ctx") // 2)
    return pl.ds(pl.multiple_of(target * piece, piece), piece)


def place_attention(blocks, wq, wk, wv, wo, rows, piece):
    for index, block in enumerate(blocks):
        for part, full in enumerate((wq, wk, wv)):
            full[wsh_rows(index, rows), :] = block[part * rows : (part + 1) * rows, :]
        cols = block.shape[1]
        for chunk in range(wo.shape[1] // cols):
            at = 3 * rows + chunk * piece
            wo[piece_rows(index, piece), chunk * cols : (chunk + 1) * cols] = block[at : at + piece, :]


def project_kernel(hat_ref, *refs, groups, rows, piece):
    blocks = refs[:groups]
    wq, wk, wv, wo, norms, normed_ref, q_ref, k_ref, v_ref = refs[groups:]
    place_attention(blocks, wq, wk, wv, wo, rows, piece)
    for index, block in enumerate(blocks):
        last = block.shape[0] - 16
        norms[:, wsh_rows(index, rows)] = block[last:, :rows].astype(F32)[:8]
    tile = 256

    def step(index, carry):
        at = pl.ds(pl.multiple_of(index * tile, tile), tile)
        normed = (hat_ref[at, :] * norms[0:1, :] + norms[4:5, :]).astype(BF)
        normed_ref[at, :] = normed
        for full, out in ((wq, q_ref), (wk, k_ref), (wv, v_ref)):
            out[at, :] = dot(normed, full[...]).astype(BF)
        return carry

    lax.fori_loop(0, hat_ref.shape[0] // tile, step, 0)


def cross_prepare_kernel(blocks, *refs, size, rows, piece):
    encoder = refs[:size]
    wq, wk, wv, wo, key_ref, value_ref = refs[size:]
    groups, cols = blocks.shape[0], blocks.shape[2]
    for index in range(groups):
        for part, full in enumerate((wq, wk, wv)):
            full[index * rows : (index + 1) * rows, :] = blocks[index, part * rows : (part + 1) * rows, :]
        target = (index ^ (lax.axis_index("ctx") // 2)) * piece
        there = pl.ds(pl.multiple_of(target, piece), piece)
        for chunk in range(wo.shape[1] // cols):
            at = 3 * rows + chunk * piece
            wo[there, chunk * cols : (chunk + 1) * cols] = blocks[index, at : at + piece, :]
    slots = encoder[0].shape[0]
    for index, part in enumerate(encoder):
        at = slice(index * slots, (index + 1) * slots)
        key_ref[at, :] = dot(part[...], wk[...]).astype(BF)
        value_ref[at, :] = dot(part[...], wv[...]).astype(BF)


def attend(split, low, high, first, last, flip, k_ref, v_ref, top, total, mixed, heads, chunk):
    tile = mixed.shape[1]
    top[...] = jnp.full_like(top, -1e30)
    total[...] = jnp.zeros_like(total)
    mixed[...] = jnp.zeros_like(mixed)

    def step(index, carry):
        start = pl.multiple_of((index ^ flip) * chunk, chunk)
        keys = k_ref[pl.ds(start, chunk), :]
        values = jnp.transpose(v_ref[pl.ds(start, chunk), :])
        scores = dot_right(keys, split)
        scores = jnp.where(allowed_keys(index * chunk, chunk, low, high), scores, -1e30)
        before = top[...]
        now = jnp.maximum(before, jnp.max(scores, axis=0, keepdims=True))
        decay = jnp.exp(before - now)
        weight = jnp.exp(scores - now)
        top[...] = now
        total[...] = total[...] * decay + jnp.sum(weight, axis=0, keepdims=True)
        weight = weight.astype(BF)
        for h in range(heads):
            rows, cols = slice(h * HEAD, (h + 1) * HEAD), slice(h * tile, (h + 1) * tile)
            mixed[rows, :] = mixed[rows, :] * decay[:, cols] + dot(values[rows, :], weight[:, cols])
        return carry

    lax.fori_loop(first, last, step, 0)
    amount = total[...]
    for h in range(heads):
        rows, cols = slice(h * HEAD, (h + 1) * HEAD), slice(h * tile, (h + 1) * tile)
        mixed[rows, :] = mixed[rows, :] / amount[:, cols]
    return top[...] + jnp.log(amount)


def attend_forward_kernel(meta, *refs, own_queries, parts, offset, count, chunk):
    if own_queries:
        sources, wq = refs[:parts], refs[parts]
        k_ref, v_ref, rows_ref, wo, q_ref, mixed_ref, lse_ref = refs[parts + 1 : parts + 8]
        rest = refs[parts + 8 :]
        for index, source in enumerate(sources):
            slots = source.shape[0]
            q_ref[index * slots : (index + 1) * slots, :] = dot(source[...], wq[...]).astype(BF)
        shift = 0
    else:
        q_ref, k_ref, v_ref, rows_ref, wo, mixed_ref, lse_ref = refs[:7]
        rest = refs[7:]
        shift = offset
    outs, (top, total, mixed) = rest[:parts], rest[parts:]
    tile = mixed.shape[1]
    heads = q_ref.shape[1] // HEAD

    def block(index, carry):
        at = pl.ds(pl.multiple_of((index + shift) * tile, tile), tile)
        split = split_heads(q_ref[at, :].astype(F32) * 0.125, heads, HEAD)
        low = spread(rows_ref[index + offset, 0:1, :], heads)
        high = spread(rows_ref[index + offset, 1:2, :], heads)
        first, last = meta[1 + index + offset], meta[1 + count + index + offset]
        lse_ref[index] = attend(split, low, high, first, last, meta[0], k_ref, v_ref, top, total, mixed, heads, chunk)
        here = pl.ds(pl.multiple_of(index * tile, tile), tile)
        mixed_ref[here, :] = jnp.transpose(mixed[...]).astype(BF)
        return carry

    lax.fori_loop(0, mixed_ref.shape[0] // tile, block, 0)
    for index, out in enumerate(outs):
        slots = out.shape[0]
        out[...] = dot(mixed_ref[index * slots : (index + 1) * slots, :], wo[...]).astype(BF)


def attend_backward_kernel(meta, *refs, own_queries, parts, offset, count, chunk, fresh):
    sources = refs[:parts]
    q_ref, mixed_ref, lse_ref, rows_ref, k_ref, v_ref, wo = refs[parts : parts + 7]
    rest = refs[parts + 7 :]
    if own_queries:
        wq, rest = rest[0], rest[1:]
    if not fresh:
        rest = rest[3:]
    dq_ref, dk_ref, dv_ref, dwo_ref = rest[:4]
    outs = rest[4 : 4 + parts] if own_queries else ()
    grad_ref, dq_sum = rest[-2:]
    tile = dq_sum.shape[1]
    heads = q_ref.shape[1] // HEAD
    shift = 0 if own_queries else offset
    if fresh:
        dk_ref[...] = jnp.zeros_like(dk_ref)
        dv_ref[...] = jnp.zeros_like(dv_ref)
    change = None
    for index, source in enumerate(sources):
        slots = source.shape[0]
        at = slice(index * slots, (index + 1) * slots)
        grad_ref[at, :] = dot_right(source[...], wo[...]).astype(BF)
        part = dot_left(mixed_ref[at, :], source[...])
        change = part if change is None else change + part
    dwo_ref[...] = change if fresh else dwo_ref[...] + change

    def block(index, carry):
        at = pl.ds(pl.multiple_of((index + shift) * tile, tile), tile)
        here = pl.ds(pl.multiple_of(index * tile, tile), tile)
        split = split_heads(q_ref[at, :].astype(F32) * 0.125, heads, HEAD)
        grads = split_heads(grad_ref[here, :], heads, HEAD)
        low = spread(rows_ref[index + offset, 0:1, :], heads)
        high = spread(rows_ref[index + offset, 1:2, :], heads)
        lse = lse_ref[index]
        product = jnp.transpose(grad_ref[here, :].astype(F32) * mixed_ref[here, :].astype(F32))
        inner = jnp.concatenate(
            [jnp.sum(product[h * HEAD : (h + 1) * HEAD], axis=0, keepdims=True) for h in range(heads)], 1
        )
        dq_sum[...] = jnp.zeros_like(dq_sum)

        def step(number, carry):
            start = pl.multiple_of((number ^ meta[0]) * chunk, chunk)
            keys = k_ref[pl.ds(start, chunk), :]
            scores = dot_right(keys, split)
            scores = jnp.where(allowed_keys(number * chunk, chunk, low, high), scores, -1e30)
            weight = jnp.exp(scores - lse)
            slope = dot_right(v_ref[pl.ds(start, chunk), :], grads)
            slope = (weight * (slope - inner)).astype(BF)
            dv_ref[pl.ds(start, chunk), :] += dot(weight.astype(BF), grads)
            dk_ref[pl.ds(start, chunk), :] += dot(slope, split)
            turned = jnp.transpose(keys)
            for h in range(heads):
                rows, cols = slice(h * HEAD, (h + 1) * HEAD), slice(h * tile, (h + 1) * tile)
                dq_sum[rows, :] += dot(turned[rows, :], slope[:, cols])
            return carry

        lax.fori_loop(meta[1 + index + offset], meta[1 + count + index + offset], step, 0)
        dq_ref[here, :] = (jnp.transpose(dq_sum[...]) * 0.125).astype(BF)
        return carry

    lax.fori_loop(0, dq_ref.shape[0] // tile, block, 0)
    for index, out in enumerate(outs):
        slots = out.shape[0]
        out[...] = dot_right(dq_ref[index * slots : (index + 1) * slots, :], wq[...]).astype(BF)


def total_of(base, parts):
    value = base[...]
    for part in parts:
        value = value + part[...].astype(F32)
    return value


def norm_kernel(norms, base, *refs, which):
    parts, (sum_ref, normed_ref) = refs[:-2], refs[-2:]
    value = total_of(base, parts)
    sum_ref[...] = value
    hat, unused = norm_parts(value)
    normed_ref[...] = (hat * norms[which : which + 1, :] + norms[4 + which : 5 + which, :]).astype(BF)


def norm_back_kernel(norms, value_ref, grad_ref, *refs, which):
    parts, (out_ref, sent_ref, terms_ref) = refs[:-3], refs[-3:]
    hat, rate = norm_parts(value_ref[...])
    grad = parts[0][...].astype(F32)
    for part in parts[1:]:
        grad = grad + part[...].astype(F32)
    change, gain, shift = norm_back(hat, rate, norms[which : which + 1, :], grad)
    result = grad_ref[...] + change
    out_ref[...] = result
    sent_ref[...] = result.astype(BF)
    terms_ref[0:1, :] = gain[None]
    terms_ref[1:2, :] = shift[None]


def norm_first_kernel(norms, value_ref, grad_ref, near, other, far, one, two, three, sent_ref):
    slots = value_ref.shape[0]
    hat, rate = norm_parts(value_ref[...])
    grad = near[...].astype(F32) + other[...].astype(F32) + far[...].astype(F32)
    change, gain, shift = norm_back(hat, rate, norms[0:1, :], grad)
    sent_ref[:slots, :] = (grad_ref[...] + change).astype(BF)
    sums = [gain[None], shift[None], one[...], two[...], three[...], jnp.zeros((8, gain.shape[0]), F32)]
    sent_ref[slots:, :] = jnp.concatenate(sums, 0).astype(BF)


def norm_turn_kernel(norms, base, outside, *refs):
    parts, (low_ref, high_ref, out_ref, sent_ref, terms_ref) = refs[:-5], refs[-5:]
    hat, rate = norm_parts(total_of(base, parts))
    result = (hat * norms[3:4, :] + norms[7:8, :]).astype(BF)
    low_ref[...] = result[: low_ref.shape[0]]
    high_ref[...] = result[low_ref.shape[0] :]
    change, gain, shift = norm_back(hat, rate, norms[3:4, :], outside[...])
    out_ref[...] = change
    sent_ref[...] = change.astype(BF)
    terms_ref[0:1, :] = gain[None]
    terms_ref[1:2, :] = shift[None]


def feed_tile(feed, part, tile):
    groups, rows = feed.shape[0], feed.shape[1] // 2
    block = feed[:, part * rows : (part + 1) * rows, pl.ds(pl.multiple_of(tile * 256, 256), 256)]
    return block.reshape(groups * rows, 256)


def feed_forward_kernel(*refs, parts):
    sources, (feed, hidden_ref, slope_ref), outs = refs[:parts], refs[parts : parts + 3], refs[parts + 3 :]
    rate = 0.7978845608028654
    tiles = feed.shape[2] // 256
    for index, (source, out) in enumerate(zip(sources, outs)):
        slots = source.shape[0]
        at = slice(index * slots, (index + 1) * slots)

        def first(tile, carry):
            lanes = pl.ds(pl.multiple_of(tile * 256, 256), 256)
            pre = dot(source[...], feed_tile(feed, 0, tile))
            square = pre * pre
            bend = jnp.tanh(rate * pre * (1.0 + 0.044715 * square))
            half = 0.5 * (1.0 + bend)
            slope = half + 0.5 * pre * (1.0 - bend * bend) * rate * (1.0 + 0.134145 * square)
            slope_ref[at, lanes] = slope.astype(BF)
            hidden_ref[at, lanes] = (pre * half).astype(BF)
            return carry

        def second(tile, carry):
            lanes = pl.ds(pl.multiple_of(tile * 256, 256), 256)
            out[:, lanes] = dot(hidden_ref[at, :], feed_tile(feed, 1, tile)).astype(BF)
            return carry

        lax.fori_loop(0, tiles, first, 0)
        lax.fori_loop(0, tiles, second, 0)


def feed_rows(feed, part, tile):
    rows = feed.shape[1] // 2
    count = 256 // rows
    block = feed[pl.ds(tile * count, count), part * rows : (part + 1) * rows, :]
    return block.reshape(256, feed.shape[2])


def feed_backward_kernel(*refs, parts):
    sources, (feed, slope_ref, change_ref), outs = refs[:parts], refs[parts : parts + 3], refs[parts + 3 :]
    tiles = feed.shape[0] * feed.shape[1] // 512
    for index, (source, out) in enumerate(zip(sources, outs)):
        slots = source.shape[0]
        at = slice(index * slots, (index + 1) * slots)

        def second(tile, carry):
            lanes = pl.ds(pl.multiple_of(tile * 256, 256), 256)
            change = dot_right(source[...], feed_rows(feed, 1, tile)) * slope_ref[at, lanes].astype(F32)
            change_ref[at, lanes] = change.astype(BF)
            return carry

        def first(tile, carry):
            lanes = pl.ds(pl.multiple_of(tile * 256, 256), 256)
            out[:, lanes] = dot_right(change_ref[at, :], feed_rows(feed, 0, tile)).astype(BF)
            return carry

        lax.fori_loop(0, tiles, second, 0)
        lax.fori_loop(0, tiles, first, 0)


def feed_grad_kernel(*refs, size, rows):
    normed, (change_low, change_high, hidden_low, hidden_high) = refs[:size], refs[size : size + 4]
    grads, out_ref = refs[size + 4 : 2 * size + 4], refs[-1]
    middle, slots = size // 2, normed[0].shape[0]
    wide = 2 * rows

    def step(index, carry):
        lanes = pl.ds(pl.multiple_of(index * wide, wide), wide)
        first, second = None, None
        for block in range(size):
            side, at = block // middle, (block % middle) * slots
            change = (change_low, change_high)[side][at : at + slots, :]
            hidden = (hidden_low, hidden_high)[side][at : at + slots, lanes]
            one = dot_left(normed[block][:, lanes], change)
            two = dot_left(hidden, grads[block][...])
            first, second = (one, two) if first is None else (first + one, second + two)
        for part in range(2):
            at = slice(part * rows, (part + 1) * rows)
            out_ref[2 * index + part, 0:rows, :] = first[at, :].astype(BF)
            out_ref[2 * index + part, rows : 2 * rows, :] = second[at, :].astype(BF)
        return carry

    lax.fori_loop(0, out_ref.shape[0] // 2, step, 0)


def weight_grad_kernel(*refs, terms, odd, rows, piece, count):
    operands, extra, outs, held = refs[: -count - 2], refs[-count - 2], refs[-count - 1 : -1], refs[-1]
    height, cols = outs[0].shape
    mine = lax.axis_index("wsh")

    def step(index, carry):
        target = mine ^ (2 * index + odd)
        lanes = pl.ds(pl.multiple_of(target * rows, rows), rows)
        for part in range(3):
            value = None
            for which, left, left_at, right, right_at, length in terms:
                if which == part:
                    one = dot_left(
                        operands[left][left_at : left_at + length, lanes],
                        operands[right][right_at : right_at + length, :].astype(BF),
                    )
                    value = one if value is None else value + one
            held[index, part * rows : (part + 1) * rows, :] = value.astype(held.dtype)
        taken = piece_rows(2 * index + odd, piece)
        for chunk in range(extra.shape[1] // cols):
            at = 3 * rows + chunk * piece
            held[index, at : at + piece, :] = extra[taken, chunk * cols : (chunk + 1) * cols].astype(held.dtype)
        return carry

    lax.fori_loop(0, count, step, 0)
    for index, out in enumerate(outs):
        out[...] = held[index]


def back_project_kernel(dq_ref, dk_ref, dv_ref, wq, wk, wv, *outs, first):
    for index, out in enumerate(outs):
        slots = out.shape[0]
        at = slice(index * slots, (index + 1) * slots)
        there = slice(first + index * slots, first + (index + 1) * slots)
        value = dot_right(dq_ref[at, :], wq[...])
        value += dot_right(dk_ref[there, :].astype(BF), wk[...])
        value += dot_right(dv_ref[there, :].astype(BF), wv[...])
        out[...] = value.astype(BF)


def encoder_grad_kernel(dk_ref, dv_ref, wk, wv, *outs):
    for index, out in enumerate(outs):
        slots = out.shape[0]
        at = slice(index * slots, (index + 1) * slots)
        value = dot_right(dk_ref[at, :].astype(BF), wk[...]) + dot_right(dv_ref[at, :].astype(BF), wv[...])
        out[...] = value.astype(BF)


def place_square_kernel(*refs, count, rows, piece):
    mine = lax.axis_index("ctx")
    threes, (near, other), outs = refs[:count], refs[count : count + 2], refs[count + 2 :]
    cols = threes[0].shape[1]
    span = HEAD * count
    blocks = [three[...].astype(F32) for three in threes]
    for group in range(count):
        wanted = mine ^ group
        chosen = blocks[0]
        for index in range(1, count):
            chosen = jnp.where(wanted == index, blocks[index], chosen)
        for part in range(3):
            for head in range(cols // HEAD):
                at = head * span + group * HEAD
                outs[part][:, at : at + HEAD] = chosen[
                    part * rows : (part + 1) * rows, head * HEAD : (head + 1) * HEAD
                ]
    core = mine % 2
    for source, place in ((near, core), (other, 1 - core)):
        for half in range(2):
            row = pl.ds(pl.multiple_of((2 * place + half) * piece, piece), piece)
            for chunk in range(outs[3].shape[1] // cols):
                at = (half * (outs[3].shape[1] // cols) + chunk) * piece
                outs[3][row, chunk * cols : (chunk + 1) * cols] = source[at : at + piece, :].astype(F32)


def place_feed_kernel(*refs, count, groups, rows, cols):
    mine = lax.axis_index("ctx")
    first, second = refs[count:]
    for index in range(count):
        target = mine ^ index
        for group in range(groups):
            column = pl.ds(pl.multiple_of(group * count * cols + target * cols, cols), cols)
            first[:, column] = refs[index][:rows, group * cols : (group + 1) * cols].astype(F32)
        row = pl.ds(pl.multiple_of(target * cols, cols), cols)
        second[row, :] = refs[index][rows:, :].astype(F32)


def fold(near, sent):
    arrived = swap(sent, "ctx", 1)
    return near, arrived


def after(value, *others):
    return lax.optimization_barrier((value,) + others)[0]


def far_hop(parts):
    arrived = swap(parts[1], "ctx", 1)
    sent = (parts[0].astype(F32) + arrived.astype(F32)).astype(BF)
    return sent, swap(sent, "ctx", 2)


def spread_ctx(own):
    far = swap(own, "ctx", 2)
    near = swap(own, "ctx", 1)
    return [own, near, far, swap(far, "ctx", 1)]


def start_ctx(own):
    return [own, swap(own, "ctx", 1), swap(own, "ctx", 2)]


def finish_ctx(blocks, *before):
    far = after(blocks[2], *before)
    return blocks[:2] + [far, swap(far, "ctx", 1)]


def send_z(own):
    size = lax.axis_size("wsh")
    blocks = {0: own, 1: swap(own, "wsh", 1)}
    for bit in range(2, size, 2):
        blocks[bit] = swap(own, "wsh", bit)
    return blocks


def pass_y(blocks):
    size = lax.axis_size("wsh")
    for bit in range(2, size, 2):
        blocks[bit + 1] = swap(blocks[bit], "wsh", 1)
    return [blocks[bit] for bit in range(size)]


class Ranges:
    def __init__(self, low, high, tile, chunk, flip):
        self.tile, self.chunk, self.count = tile, chunk, low.shape[0] // tile
        low, high = low.reshape(self.count, tile), high.reshape(self.count, tile)
        self.rows = jnp.stack([low, high], 1)
        first, last = jnp.min(low, 1) // chunk, (jnp.max(high, 1) - 1) // chunk + 1
        self.meta = jnp.concatenate([flip.reshape(1), first, last]).astype(jnp.int32)


def fast_body(
    inputs,
    enc_states,
    cotangent,
    slot_order,
    seq_lengths,
    enc_lengths,
    self_query,
    self_key,
    self_value,
    self_out,
    cross_query,
    cross_key,
    cross_value,
    cross_out,
    feed_in,
    feed_out,
    norm_gains,
    norm_shifts,
):
    size, groups = lax.axis_size("ctx"), lax.axis_size("wsh")
    mine, row = lax.axis_index("ctx"), lax.axis_index("wsh")
    slots = inputs.shape[1]
    total = slots * size
    enc_slots = enc_states.shape[1]
    width = inputs.shape[2]
    rows = self_query.shape[0]
    cols = width // size
    piece = rows // size
    ff_cols = feed_in.shape[1] // size
    ff_rows = feed_out.shape[0] // size
    heads = cols // HEAD
    middle = total // 2
    part = size // 2
    block_bf, block_f = ((slots, width), BF), ((slots, width), F32)
    terms_f = ((2, width), F32)

    given = call_packing(give_pieces_kernel, [((2 * piece, width), BF)], self_out, cross_out)[0]
    given = swap(given, "wsh", 1)
    height = 3 * rows + piece * (width // cols)
    self_block = call_packing(
        functools.partial(pack_kernel, size=size, which=0),
        [((height + 16, cols), BF)],
        self_query,
        self_key,
        self_value,
        self_out,
        given,
        jnp.transpose(norm_gains),
        jnp.transpose(norm_shifts),
    )[0]
    self_blocks = send_z(self_block)
    token_blocks = start_ctx(inputs[0])
    self_blocks = pass_y(self_blocks)
    token_blocks = finish_ctx(token_blocks)
    cross_block = call_packing(
        functools.partial(pack_kernel, size=size, which=1),
        [((height, cols), BF)],
        after(cross_query, self_block),
        cross_key,
        cross_value,
        cross_out,
        given,
    )[0]
    packed = cross_block
    cross_block = gather_wsh(cross_block).reshape(groups, height, cols)
    feed = call_packing(
        functools.partial(pack_feed_kernel, groups=groups, size=size),
        [((2 * rows, ff_cols), BF)],
        after(feed_in, self_block),
        feed_out,
    )[0]
    feed = gather_wsh(after(feed, packed, self_blocks[2])).reshape(groups, 2 * rows, ff_cols)

    relative = jnp.arange(size, dtype=jnp.int32) ^ mine
    order = jnp.take(slot_order[0].reshape(size, slots), relative, axis=0).reshape(1, total)
    own_order = lax.dynamic_slice_in_dim(slot_order[0], mine * slots, slots).reshape(slots, 1)
    place = (relative[:, None] * slots + jnp.arange(slots, dtype=jnp.int32)).reshape(total)
    lower = jnp.arange(seq_lengths.shape[1])
    lower = lower[None, :] <= lower[:, None]
    ends = jnp.sum(jnp.where(lower, seq_lengths[0][None, :], 0), 1)
    enc_ends = jnp.sum(jnp.where(lower, enc_lengths[0][None, :], 0), 1)
    passed = ends[None, :] <= place[:, None]
    starts = jnp.max(jnp.where(passed, ends[None, :], 0), 1)
    enc_from = jnp.max(jnp.where(passed, enc_ends[None, :], 0), 1)
    enc_to = jnp.min(jnp.where(passed, enc_slots * size, enc_ends[None, :]), 1)
    self_range = Ranges(starts, place + 1, 256, 256, mine * (slots // 256))
    cross_range = Ranges(enc_from, enc_to, 256, 128, mine * (enc_slots // 128))
    half = total // 512

    def unsort(blocks):
        outs = [block_f]
        if blocks[0].shape[0] > slots:
            outs.append(((blocks[0].shape[0] - slots, width), F32))
        return call(functools.partial(unsort_kernel, size=size), outs, (), own_order, *blocks)

    hat_all, tokens = call(
        functools.partial(sort_kernel, size=size), [((total, width), F32), block_f], (), order, *token_blocks
    )

    square, tall = ((width, cols), BF), ((total, cols), BF)
    wq, wk, wv, wo, norms, normed_one, queries, keys, values = call(
        functools.partial(project_kernel, groups=groups, rows=rows, piece=piece),
        [square] * 3 + [((cols, width), BF), ((8, width), F32), ((total, width), BF)] + [tall] * 3,
        (),
        hat_all,
        *self_blocks,
    )
    lanes = heads * 256
    half_outs = [((middle, cols), BF), ((half, 1, lanes), F32)] + [block_bf] * part
    scratch = [pltpu.VMEM((1, lanes), F32), pltpu.VMEM((1, lanes), F32), pltpu.VMEM((cols, 256), F32)]

    def self_forward(side, queries):
        body = functools.partial(
            attend_forward_kernel,
            own_queries=False,
            parts=part,
            offset=side * half,
            count=self_range.count,
            chunk=self_range.chunk,
        )
        return call(
            body, half_outs, (self_range.meta,), queries, keys, values, self_range.rows, wo, scratch=scratch
        )

    encoder = spread_ctx(after(enc_states[0], normed_one))
    mixed_high, lse_high, *far = self_forward(1, queries)
    sent, arrived = far_hop(far)
    mixed_low, lse_low, *near = self_forward(0, after(queries, sent))

    def normalize(base, near, arrived, which):
        return call(
            functools.partial(norm_kernel, which=which),
            [block_f, block_bf],
            (),
            norms,
            base,
            near[0],
            swap(near[1], "ctx", 1),
            arrived,
        )

    after_self, normed = normalize(tokens, near, arrived, 1)
    outside = spread_ctx(after(cotangent[0], arrived))
    outside = call(functools.partial(pick_kernel, size=size), [block_f], (), order, *outside)[0]

    normed_two = start_ctx(normed)
    cq, ck, cv, co, enc_keys, enc_values = call(
        functools.partial(cross_prepare_kernel, size=size, rows=rows, piece=piece),
        [square] * 3 + [((cols, width), BF)] + [((enc_slots * size, cols), BF)] * 2,
        (),
        cross_block,
        *encoder,
    )

    def cross_forward(side):
        body = functools.partial(
            attend_forward_kernel,
            own_queries=True,
            parts=part,
            offset=side * half,
            count=cross_range.count,
            chunk=cross_range.chunk,
        )
        return call(
            body,
            [((middle, cols), BF)] + half_outs,
            (cross_range.meta,),
            *normed_two[side * part : (side + 1) * part],
            cq,
            enc_keys,
            enc_values,
            cross_range.rows,
            co,
            scratch=scratch,
        )

    cross_low = cross_forward(0)
    normed_two = finish_ctx(normed_two, cross_low[3])
    cross_high = cross_forward(1)
    sent, arrived = far_hop(cross_high[3:])
    after_cross, normed = normalize(after_self, cross_low[3:], arrived, 2)

    normed_three = start_ctx(normed)
    def feed_forward(side):
        return call(
            functools.partial(feed_forward_kernel, parts=part),
            [((middle, ff_cols), BF)] * 2 + [block_bf] * part,
            (),
            *normed_three[side * part : (side + 1) * part],
            feed,
        )

    hidden_low, slope_low, *near = feed_forward(0)
    normed_three = finish_ctx(normed_three, near[0])
    hidden_high, slope_high, *far = feed_forward(1)
    sent, arrived = far_hop(far)
    result_low, result_high, grad_ffn, grad, terms_three = call(
        norm_turn_kernel,
        [((slots // 2, width), BF)] * 2 + [block_f, block_bf, terms_f],
        (),
        norms,
        after_cross,
        outside,
        near[0],
        swap(near[1], "ctx", 1),
        arrived,
    )

    def denormalize(value, grad, near, arrived, which):
        return call(
            functools.partial(norm_back_kernel, which=which),
            [block_f, block_bf, terms_f],
            (),
            norms,
            value,
            grad,
            near[0],
            swap(near[1], "ctx", 1),
            arrived,
        )

    grad_in = start_ctx(grad)

    def feed_backward(side, slope):
        return call(
            functools.partial(feed_backward_kernel, parts=part),
            [((middle, ff_cols), BF)] + [block_bf] * part,
            (),
            *grad_in[side * part : (side + 1) * part],
            feed,
            slope,
        )

    change_low, *near = feed_backward(0, slope_low)
    grad_in = finish_ctx(grad_in, near[0])
    change_high, *far = feed_backward(1, slope_high)
    sent, arrived = far_hop(far)
    feed_grads = call(
        functools.partial(feed_grad_kernel, size=size, rows=rows),
        [((groups, 2 * rows, width), BF)],
        (),
        *normed_three,
        change_low,
        after(change_high, sent),
        hidden_low,
        hidden_high,
        *grad_in,
    )[0]
    grad_cross, grad, terms_two = denormalize(after_cross, grad_ffn, near, after(arrived, feed_grads), 2)
    feed_grads = scatter_wsh(after(feed_grads, arrived).reshape(groups * 2 * rows, width))

    def weight_grads(terms, operands, out_grad, odd):
        count = groups // 2
        kind = BF if odd else F32
        body = functools.partial(weight_grad_kernel, terms=terms, odd=odd, rows=rows, piece=piece, count=count)
        outs = [((height, cols), kind)] * count
        return call(body, outs, (), *operands, out_grad, scratch=[pltpu.VMEM((count, height, cols), kind)])

    def pass_z(even, odd, index):
        value = (even[index] + odd[index].astype(F32)).astype(BF)
        return swap(value, "wsh", 2 * index)

    def backward(span, side, own_queries, sources, queries, mixed, lse, keys, values, wo, wq, before):
        body = functools.partial(
            attend_backward_kernel,
            own_queries=own_queries,
            parts=part,
            offset=side * half,
            count=span.count,
            chunk=span.chunk,
            fresh=before is None,
        )
        operands = [*sources, queries, mixed, lse, span.rows, keys, values, wo]
        if own_queries:
            operands.append(wq)
        aliases = {}
        if before is not None:
            aliases = {1 + len(operands) + i: 1 + i for i in range(3)}
            operands += before
        outs = [((middle, cols), BF), (keys.shape, F32), (keys.shape, F32), ((cols, width), F32)]
        if own_queries:
            outs += [block_bf] * part
        return call(
            body,
            outs,
            (span.meta,),
            *operands,
            scratch=[pltpu.VMEM((middle, cols), BF), pltpu.VMEM((cols, 256), F32)],
            aliases=aliases,
        )

    grad_in = start_ctx(grad)
    low = backward(
        cross_range, 0, True, grad_in[:part], *cross_low[:3], enc_keys, enc_values, co, cq, None
    )
    grad_in = finish_ctx(grad_in, low[4])
    result_low = start_ctx(after(result_low, grad_in[2]))
    high = backward(
        cross_range, 1, True, grad_in[part:], *cross_high[:3], enc_keys, enc_values, co, cq, list(low[1:4])
    )
    sent, arrived = far_hop([high[4], after(high[5], result_low[2])])
    dk, dv, dwo = high[1:4]
    operands = [*normed_two, low[0], high[0], *encoder, dk, dv]
    terms = []
    for index in range(size):
        side = index // part
        terms.append((0, index, 0, size + side, (index % part) * slots, slots))
    for index in range(size):
        for which in (1, 2):
            terms.append((which, size + 2 + index, 0, 2 * size + 1 + which, index * enc_slots, enc_slots))
    dk = after(dk, sent)
    operands[-2] = dk
    odd = weight_grads(tuple(terms), operands, dwo, 1)
    cross_even = weight_grads(tuple(terms), operands, dwo, 0)
    enc_parts = call(encoder_grad_kernel, [((enc_slots, width), BF)] * size, (), dk, dv, ck, cv)
    cross_odd = [swap(block, "wsh", 1) for block in odd]
    cross_far = pass_z(cross_even, cross_odd, 3)
    arrived = after(arrived, cross_even[0], cross_odd[3], *enc_parts)
    grad_self, grad, terms_one = denormalize(after_self, grad_cross, low[4:], arrived, 1)

    grad_in = start_ctx(grad)
    low = backward(
        self_range, 0, False, grad_in[:part], queries, mixed_low, lse_low, keys, values, wo, None, None
    )
    grad_in = finish_ctx(grad_in, low[0], cross_odd[2])
    cross_middle = pass_z(cross_even, cross_odd, 2)
    result_high = start_ctx(after(result_high, grad_in[2]))
    enc_sent, enc_far = far_hop([after(enc_parts[2], grad_in[2]), enc_parts[3]])
    enc_near = swap(enc_parts[1], "ctx", 1)
    enc_grad = enc_parts[0].astype(F32) + enc_near.astype(F32) + enc_far.astype(F32)
    high = backward(
        self_range, 1, False, grad_in[part:], queries, mixed_high, lse_high, keys, values, wo, None, list(low[1:4])
    )
    dk, dv, dwo = high[1:4]

    def back_project(side, dq):
        body = functools.partial(back_project_kernel, first=side * middle)
        return call(body, [block_bf] * part, (), dq, dk, dv, wq, wk, wv)

    far = back_project(1, after(high[0], cross_odd[1], cross_far))
    cross_near = pass_z(cross_even, cross_odd, 1)
    operands = [normed_one, low[0], high[0], after(dk, result_high[2]), dv]
    terms = ((0, 0, 0, 1, 0, middle), (0, 0, middle, 2, 0, middle), (1, 0, 0, 3, 0, total), (2, 0, 0, 4, 0, total))
    odd = weight_grads(terms, operands, dwo, 1)
    sent, arrived = far_hop(far)
    self_odd = [swap(block, "wsh", 1) for block in odd]
    near = back_project(0, after(low[0], sent, odd[0]))
    self_even = weight_grads(terms, operands, after(dwo, *near), 0)
    self_far = pass_z(self_even, self_odd, 3)

    feed_blocks = start_ctx(after(feed_grads, sent))
    grad = call(
        norm_first_kernel,
        [((slots + 16, width), BF)],
        (),
        norms,
        tokens,
        grad_self,
        near[0],
        swap(near[1], "ctx", 1),
        after(arrived, self_even[0]),
        terms_one,
        terms_two,
        terms_three,
    )[0]
    input_grad = start_ctx(grad)

    def finish(even, odd, *parts):
        share = even[0] + odd[0].astype(F32)
        for value in parts:
            share = share + value.astype(F32)
        share = share.astype(BF)
        three, fourth = share[: 3 * rows], share[3 * rows :]
        pair = jnp.concatenate([fourth, swap(fourth, "wsh", 1)], 0)
        pair = jnp.where(row % 2 == mine // 2, pair, swap(pair, "ctx", 2))
        return call(
            functools.partial(place_square_kernel, count=size, rows=rows, piece=piece),
            [((rows, width), F32)] * 4,
            (),
            *spread_ctx(three),
            pair,
            swap(pair, "ctx", 1),
        )

    result_low = finish_ctx(result_low, self_odd[3], grad)
    result_high = finish_ctx(result_high)
    result = unsort([half for pair in zip(result_low, result_high) for half in pair])[0]
    self_middle = pass_z(self_even, self_odd, 2)
    self_near = pass_z(self_even, self_odd, 1)
    feed_in_grad, feed_out_grad = call(
        functools.partial(place_feed_kernel, count=size, groups=groups, rows=rows, cols=ff_rows),
        [((rows, groups * size * ff_rows), F32), ((size * ff_rows, width), F32)],
        (),
        *finish_ctx(feed_blocks, self_odd[2], result, cross_near),
    )
    input_grad, terms = unsort(finish_ctx(input_grad, self_odd[1], self_far, feed_in_grad))
    terms = terms[:8]
    terms = terms + swap(terms, "wsh", 1)
    pieces = [lax.dynamic_slice_in_dim(terms, (row ^ bit) * rows, rows, 1) for bit in range(0, groups, 2)]
    terms = pieces[0]
    for index in range(1, groups // 2):
        terms = terms + swap(pieces[index], "wsh", 2 * index)
    terms = jnp.transpose(terms)
    cross_odd[0] = after(cross_odd[0], input_grad, self_near)
    cross_grads = finish(cross_even, cross_odd, cross_near, cross_middle, cross_far)
    self_grads = finish(self_even, self_odd, self_near, self_middle, self_far)
    return (
        result[None],
        input_grad[None],
        enc_grad[None],
        *self_grads,
        *cross_grads,
        feed_in_grad,
        feed_out_grad,
        terms[:, 0::2],
        terms[:, 1::2],
    )


def solution(mesh):
    token, weight = P("wsh", "ctx", None), P("wsh", None)
    in_specs = (token,) * 3 + (weight,) * 15
    out_specs = (token,) * 3 + (weight,) * 12
    body = fast_body if mesh.shape["ctx"] == 4 else plain_body
    return jax.shard_map(body, mesh=mesh, in_specs=in_specs, out_specs=out_specs, check_vma=False)
```
